128 devices in a mesh: dp: 16 (over x_lo, y, core), tensor: 8 (over x_hi, z).
Axes of the slice: x: 4 (x_hi: 2, x_lo: 2; x = x_hi * 2 + x_lo), y: 4, z: 4, core: 2. Of those that a mesh axis runs over, the one named last changes fastest.
Arguments:
- block_input: bfloat16 [32768, 768], P(('dp', 'tensor')), may hold values from -6 to 6
- w_value: bfloat16 [768, 768], replicated, may hold values from -0.21875 to 0.21875
- b_value: bfloat16 [768], replicated, may hold values from -2 to 2
- conv_kernel: bfloat16 [65, 768], replicated, may hold values from -0.75 to 0.75
- w_out: bfloat16 [768, 768], replicated, may hold values from -0.21875 to 0.21875
- b_out: bfloat16 [768], replicated, may hold values from -2 to 2
- gain_attn: bfloat16 [768], replicated, may hold values from 0.5 to 1.5
- shift_attn: bfloat16 [768], replicated, may hold values from -2 to 2
- w_up: bfloat16 [768, 3072], P(None, 'tensor'), may hold values from -0.21875 to 0.21875
- b_up: bfloat16 [3072], P('tensor'), may hold values from -2 to 2
- w_down: bfloat16 [3072, 768], P('tensor'), may hold values from -0.109375 to 0.109375
- b_down: bfloat16 [768], replicated, may hold values from -2 to 2
- gain_ffn: bfloat16 [768], replicated, may hold values from 0.5 to 1.5
- shift_ffn: bfloat16 [768], replicated, may hold values from -2 to 2
- query_codes: int32 [32768, 384], P(('dp', 'tensor')), may hold values from 0 to 255
- key_codes: int32 [32768, 384], P(('dp', 'tensor')), may hold values from 0 to 255
- key_live: int32 [32768], P(('dp', 'tensor')), may hold values 0 or 1
- seq_lengths: int32 [128, 4], P(('dp', 'tensor')), may hold values from 1 to 128, 256 in all within a row
- out_grad: bfloat16 [32768, 768], P(('dp', 'tensor')), may hold values from -6 to 6
Outputs:
- block_output: bfloat16 [32768, 768], P(('dp', 'tensor'))
- input_grad: float32 [32768, 768], P(('dp', 'tensor'))
- grad_w_value: float32 [768, 768], replicated
- grad_b_value: float32 [768], replicated
- grad_conv_kernel: float32 [65, 768], replicated
- grad_w_out: float32 [768, 768], replicated
- grad_b_out: float32 [768], replicated
- grad_gain_attn: float32 [768], replicated
- grad_shift_attn: float32 [768], replicated
- grad_w_up: float32 [768, 3072], P(None, 'tensor')
- grad_b_up: float32 [3072], P('tensor')
- grad_w_down: float32 [3072, 768], P('tensor')
- grad_b_down: float32 [768], replicated
- grad_gain_ffn: float32 [768], replicated
- grad_shift_ffn: float32 [768], replicated
The draws below stay inside these ranges and needn't reach their ends.
Inputs may be any that keep to these rules, and one draw needn't show every extreme that they name: `seq_lengths`: each item's lengths sum to 256; the longest is 128. `key_live`: 1 marks a live key, 0 a padded one. `query_codes`: column h * 32 + s holds head h's code in hash set s. `key_codes`: column h * 32 + s holds head h's code in hash set s.
All inputs are finite; a program needn't handle non-finite values. No bound on the sum of `key_live` on one device may be relied on, other than what follows from the above.
Results may differ from the reference program's by a relative error of at most 0.02.
Values may be sent and summed in bfloat16 or wider, within the bound.
No kernel may reach another device: no remote copies, remote signals or barrier semaphores. Data moves between devices by JAX's collectives and lax.ppermute only.
A program may use at most 128 MiB of HBM per device.

```python
import math
import jax
import jax.numpy as jnp
import numpy as np
from jax import lax

D = 768
HEADS = 12
HEAD_DIM = 64
FF = 3072
SETS = 32
BUCKETS = 256
KW = 65
TOK_DEV = 256
SEQ_DEV = 4
ITEMS = 128
TOKENS = 32768


def with_ends(values, own_key, smallest, largest):
    extent = values.shape
    index_at = [jax.random.randint(jax.random.fold_in(own_key, axis), (), 0, extent[axis]) for axis in range(len(extent))]
    values = values.at[tuple(index_at)].set(smallest)
    longest = extent.index(max(extent))
    index_at[longest] = (index_at[longest] + 1) % extent[longest]
    return values.at[tuple(index_at)].set(largest)


def shard_levels(stream_key, shape, cuts, low, largest):
    level, own = 1.0, jax.random.fold_in(stream_key, 6)
    for dim, shards_of in cuts:
        heights = jnp.exp(jax.random.uniform(jax.random.fold_in(own, dim), (shards_of,), jnp.float32, low / len(cuts), largest / len(cuts)))
        level = level * jnp.repeat(heights, shape[dim] // shards_of).reshape([-1 if axis == dim else 1 for axis in range(len(shape))])
    return level


def profile(amount, total, reach, slope):
    loads = [(1 << 20) // math.isqrt(standing ** slope) + 1 for standing in range(2, amount + 1)]
    spare, given = total - reach - (amount - 1), [1] * (amount - 1)
    while spare > 0:
        candidates = [i for i in range(amount - 1) if given[i] < reach]
        mass, budget = sum([loads[i] for i in candidates]), spare
        for i in candidates:
            more = min(reach - given[i], max(1, budget * loads[i] // mass), spare)
            given[i] = given[i] + more
            spare = spare - more
    return np.array([reach] + given)


def ragged_sizes(stream_key, number_of, total, reach, lean):
    if number_of == 2:
        one = jax.random.randint(stream_key, (), max(1, total - reach), min(reach, total - 1) + 1)
        return jnp.stack([one, total - one])
    lengths = jnp.asarray(profile(number_of, total, reach, lean), jnp.int32)
    couples = (number_of - 1) // 2
    donor, taker = lengths[1:1 + 2 * couples:2], lengths[2:2 + 2 * couples:2]
    room = jnp.minimum(donor - 1, reach - taker)
    moved = jax.random.randint(jax.random.fold_in(stream_key, 1), (couples,), 0, 1 << 20) % (room + 1)
    lengths = lengths.at[1:1 + 2 * couples:2].set(donor - moved).at[2:2 + 2 * couples:2].set(taker + moved)
    return lengths[jax.random.permutation(jax.random.fold_in(stream_key, 2), number_of)]


def normal_values(key, extent, scale, limit, shards=(), kind=jnp.bfloat16):
    values = jax.random.normal(key, extent, jnp.float32) * scale
    if len(shards) > 0:
        values = shard_levels(key, extent, shards, -0.22, 0.18) * values
    return jnp.clip(values, min=-limit, max=limit).astype(kind)


def setup_inputs(seed: int = 0) -> dict:
    seeds = jax.random.split(jax.random.key(seed), 20)
    block_input = normal_values(seeds[0], (TOKENS, D), 1.0, 6.0, ((0, 128),))
    w_value = normal_values(seeds[1], (D, D), D ** -0.5, 0.21875)
    b_value = normal_values(seeds[2], (D,), 0.3, 2.0)
    conv_kernel = normal_values(seeds[3], (KW, D), KW ** -0.5, 0.75)
    w_out = normal_values(seeds[4], (D, D), D ** -0.5, 0.21875)
    b_out = normal_values(seeds[5], (D,), 0.3, 2.0)
    gain_attn = jnp.clip(1.0 + 0.1 * jax.random.normal(seeds[6], (D,), jnp.float32), 0.5, 1.5).astype(jnp.bfloat16)
    shift_attn = normal_values(seeds[7], (D,), 0.3, 2.0)
    w_up = normal_values(seeds[8], (D, FF), D ** -0.5, 0.21875, ((1, 8),))
    b_up = normal_values(seeds[9], (FF,), 0.3, 2.0, ((0, 8),))
    w_down = normal_values(seeds[10], (FF, D), FF ** -0.5, 0.109375, ((0, 8),))
    b_down = normal_values(seeds[11], (D,), 0.3, 2.0)
    gain_ffn = jnp.clip(1.0 + 0.1 * jax.random.normal(seeds[12], (D,), jnp.float32), 0.5, 1.5).astype(jnp.bfloat16)
    shift_ffn = normal_values(seeds[13], (D,), 0.3, 2.0)
    query_codes = with_ends(jax.random.randint(seeds[14], (TOKENS, HEADS * SETS), 0, BUCKETS), jax.random.fold_in(seeds[14], 1), 0, BUCKETS - 1).astype(jnp.int32)
    key_codes = with_ends(jax.random.randint(seeds[15], (TOKENS, HEADS * SETS), 0, BUCKETS), jax.random.fold_in(seeds[15], 1), 0, BUCKETS - 1).astype(jnp.int32)
    key_live = with_ends((jax.random.randint(seeds[16], (TOKENS,), 0, 8) < 7).astype(jnp.int32), jax.random.fold_in(seeds[16], 1), 0, 1)
    seq_lengths = jax.vmap(lambda own: ragged_sizes(own, SEQ_DEV, TOK_DEV, TOK_DEV // 2, 2))(jax.random.split(seeds[17], ITEMS)).reshape((ITEMS, SEQ_DEV)).astype(jnp.int32)
    out_grad = normal_values(seeds[18], (TOKENS, D), 1.0, 6.0, ((0, 128),))
    return dict(block_input=block_input, w_value=w_value, b_value=b_value, conv_kernel=conv_kernel, w_out=w_out, b_out=b_out, gain_attn=gain_attn, shift_attn=shift_attn, w_up=w_up, b_up=b_up, w_down=w_down, b_down=b_down, gain_ffn=gain_ffn, shift_ffn=shift_ffn, query_codes=query_codes, key_codes=key_codes, key_live=key_live, seq_lengths=seq_lengths, out_grad=out_grad)


highest = lax.Precision.HIGHEST

@jax.custom_vjp
def low(v):
    return lax.optimization_barrier(v.astype(jnp.bfloat16)).astype(jnp.float32)

@jax.custom_vjp
def low_back(v):
    return v

def low_keep(v):
    return (low(v), None)

def low_pass(kept, grad):
    return (grad,)

def back_keep(v):
    return (v, None)

def back_low(kept, grad):
    return (low(grad),)
low.defvjp(low_keep, low_pass)
low_back.defvjp(back_keep, back_low)

def matmul(former, latter):
    return jnp.einsum('gld,de->gle', former, latter, precision=highest)

def layer_norm(residual, gain_vec, shift_vec):
    average = lax.optimization_barrier(jnp.mean(residual, axis=-1, keepdims=True))
    centred = residual - average
    variance = lax.optimization_barrier(jnp.mean(centred * centred, axis=-1, keepdims=True))
    return centred * lax.rsqrt(variance + 1e-05) * gain_vec + shift_vec

def depth_conv(values, kernel, segment):
    margin = kernel.shape[0] // 2
    length = values.shape[1]
    padded = jnp.pad(values, ((0, 0), (margin, margin), (0, 0)))
    seg_padded = jnp.pad(segment, ((0, 0), (margin, margin)), constant_values=-1)

    def add_tap(offset, running):
        window = lax.dynamic_slice_in_dim(padded, offset, length, 1)
        seg_window = lax.dynamic_slice_in_dim(seg_padded, offset, length, 1)
        joined = (seg_window == segment).astype(jnp.float32)[:, :, None]
        weight = lax.dynamic_slice_in_dim(kernel, offset, 1, 0)
        return running + window * joined * weight
    return lax.fori_loop(0, kernel.shape[0], add_tap, jnp.zeros_like(values))

def collisions(query_part, key_part, segment):
    groups = segment.shape[0]
    query_heads = jnp.moveaxis(query_part.reshape(groups, TOK_DEV, HEADS, SETS), 2, 1)
    key_heads = jnp.moveaxis(key_part.reshape(groups, TOK_DEV, HEADS, SETS), 2, 1)

    def add_set(offset, running):
        query_set = lax.dynamic_index_in_dim(query_heads, offset, 3, keepdims=False)
        key_set = lax.dynamic_index_in_dim(key_heads, offset, 3, keepdims=False)
        return running + (query_set[:, :, :, None] == key_set[:, :, None, :]).astype(jnp.float32)
    counts = lax.fori_loop(0, SETS, add_set, jnp.zeros((groups, HEADS, TOK_DEV, TOK_DEV), jnp.float32))
    joined = (segment[:, :, None] == segment[:, None, :]).astype(jnp.float32)
    return counts * joined[:, None] / SETS

def forward(row_block, params, collide, live_keys, segment):
    w_value, b_value, kernel, w_out, b_out, gain_attn, shift_attn, w_up, b_up, w_down, b_down, gain_ffn, shift_ffn = params
    groups = row_block.shape[0]
    values = low_back(low(matmul(row_block, w_value) + b_value))
    masked = values * live_keys
    heads_in = masked.reshape(groups, TOK_DEV, HEADS, HEAD_DIM)
    mixed = low_back(jnp.einsum('ghij,gjhd->gihd', collide, heads_in, precision=highest))
    scaling = lax.rsqrt(lax.optimization_barrier(jnp.mean(mixed * mixed, axis=-1, keepdims=True)) + 1e-06)
    normed = (mixed * scaling).reshape(groups, TOK_DEV, D)
    context = low(normed + depth_conv(masked, kernel, segment))
    attended = low_back(matmul(context, w_out) + b_out)
    first = layer_norm(row_block + attended, gain_attn, shift_attn)
    upper = low_back(matmul(low(first), w_up) + b_up)
    active = low(jax.nn.gelu(upper, approximate=False))
    branch = low_back(matmul(active, w_down) + b_down)
    return layer_norm(first + branch, gain_ffn, shift_ffn)

def reference(block_input, w_value, b_value, conv_kernel, w_out, b_out, gain_attn, shift_attn, w_up, b_up, w_down, b_down, gain_ffn, shift_ffn, query_codes, key_codes, key_live, seq_lengths, out_grad):
    params = tuple((weight.astype(jnp.float32) for weight in (w_value, b_value, conv_kernel, w_out, b_out, gain_attn, shift_attn, w_up, b_up, w_down, b_down, gain_ffn, shift_ffn)))
    positions = jnp.arange(TOK_DEV, dtype=jnp.int32)
    seq_ends = jnp.cumsum(seq_lengths, axis=1, dtype=jnp.int32)
    segment_all = lax.optimization_barrier(jnp.sum((seq_ends[:, None, :] <= positions[None, :, None]).astype(jnp.int32), axis=2, dtype=jnp.int32))
    per_round = math.gcd(ITEMS, max(1, 4096 // TOK_DEV))
    rounds = ITEMS // per_round
    rows_all = block_input.astype(jnp.float32).reshape(rounds, per_round, TOK_DEV, D)
    cot_all = out_grad.astype(jnp.float32).reshape(rounds, per_round, TOK_DEV, D)
    query_all = query_codes.reshape(rounds, per_round, TOK_DEV, HEADS * SETS)
    key_all = key_codes.reshape(rounds, per_round, TOK_DEV, HEADS * SETS)
    live_all = key_live.astype(jnp.float32).reshape(rounds, per_round, TOK_DEV, 1)
    seg_all = segment_all.reshape(rounds, per_round, TOK_DEV)

    def one_round(running, pieces):
        row_block, cot_rows, query_part, key_part, live_part, seg_part = pieces
        collide = collisions(query_part, key_part, seg_part)

        def run_block(rows_in, weights_in):
            return forward(rows_in, weights_in, collide, live_part, seg_part)
        outputs, pullback = jax.vjp(run_block, row_block, params)
        grad_rows, grad_params = pullback(cot_rows)
        running = tuple((summed + added for summed, added in zip(running, grad_params)))
        return (running, (outputs, grad_rows))
    zeroed = tuple((jnp.zeros_like(weight) for weight in params))
    totals, (outputs, grad_rows) = lax.scan(one_round, zeroed, (rows_all, cot_all, query_all, key_all, live_all, seg_all))
    return (outputs.reshape(TOKENS, D).astype(jnp.bfloat16), grad_rows.reshape(TOKENS, D), totals[0], totals[1], totals[2], totals[3], totals[4], totals[5], totals[6], totals[7], totals[8], totals[9], totals[10], totals[11], totals[12])
```

```python
import math

import jax
import jax.numpy as jnp
from jax import lax
from jax.experimental import pallas as pl
from jax.experimental.pallas import tpu as pltpu
from jax.sharding import PartitionSpec as P

HEADS = 12
SETS = 32
ROWS = 256
WIDTH = 768
HEAD_DIM = 64
COLS = WIDTH // 128
TAPS = 65
MARGIN = 32
DFT_LEN = 384
FREQ = 256
LIVE_FREQ = DFT_LEN // 2 + 1
PIECE = 24
UNITS = 3 * COLS + 1
TALL = 848
TALL_TILES = TALL // 8
PACK = 640
ALL = ("dp", "tensor")

bf16 = jnp.bfloat16
f32 = jnp.float32
i32 = jnp.int32

VMEM = pl.BlockSpec(memory_space=pltpu.VMEM)
SMEM = pl.BlockSpec(memory_space=pltpu.SMEM)


def shape(dims, dtype):
    return jax.ShapeDtypeStruct(dims, dtype)


def params(mib):
    return pltpu.CompilerParams(vmem_limit_bytes=mib << 20)


def dot(a, b):
    return lax.dot_general(a, b, (((1,), (0,)), ((), ())), preferred_element_type=f32)


def dot_last(a, b):
    return lax.dot_general(a, b, (((1,), (1,)), ((), ())), preferred_element_type=f32)


def dot_first(a, b):
    return lax.dot_general(a, b, (((0,), (0,)), ((), ())), preferred_element_type=f32)


def lanes(dims):
    return lax.broadcasted_iota(i32, dims, len(dims) - 1)


def norm_rows(r):
    mean = jnp.mean(r, axis=-1, keepdims=True)
    centred = r - mean
    inv = lax.rsqrt(jnp.mean(centred * centred, axis=-1, keepdims=True) + 1e-05)
    return centred * inv, inv


def norm_back(g, n, inv, gain):
    e = g * gain
    return (
        e - jnp.mean(e, axis=-1, keepdims=True) - n * jnp.mean(e * n, axis=-1, keepdims=True)
    ) * inv


def prep_kernel(place, up_ref, down_ref, bias_ref, out_ref, tall, cols, piece):
    rep = place[0] % 8

    @pl.when(pl.program_id(0) == 0)
    def _():
        @pl.when(place[0] < 8)
        def _():
            tall[...] = up_ref[...].astype(f32).T
            cols[...] = jnp.broadcast_to(bias_ref[...].astype(f32), (8, 384)).T

        @pl.when(place[0] >= 8)
        def _():
            tall[...] = down_ref[...].astype(f32)
            cols[...] = jnp.zeros(cols.shape, f32)

        for c in range(2):
            start = pl.multiple_of(192 * c + PIECE * rep, 8)
            rows = tall[pl.ds(start, PIECE), :]
            for ct in range(COLS):
                part = rows[:, ct * 128 : ct * 128 + 128].reshape(3, 8, 128)
                piece[c, 3 * ct : 3 * ct + 3] = part.astype(bf16)
            bias = jnp.zeros((8, 128), f32)
            for rt in range(3):
                col = cols[pl.ds(pl.multiple_of(start + 8 * rt, 8), 8), :][:, 0:1]
                bias = jnp.where(lanes((8, 128)) == rt, jnp.broadcast_to(col, (8, 128)), bias)
            piece[c, UNITS - 1] = bias.astype(bf16)

    for s in range(16):
        out_ref[s] = piece[s // 8]


def prep(place, w_up, w_down, b_up):
    whole = lambda *dims: pl.BlockSpec(dims, lambda i: (0,) * len(dims))
    return pl.pallas_call(
        prep_kernel,
        grid=(8,),
        out_shape=shape((128, UNITS, 8, 128), bf16),
        in_specs=[SMEM, whole(768, 384), whole(384, 768), whole(1, 384)],
        out_specs=pl.BlockSpec((16, UNITS, 8, 128), lambda i: (i, 0, 0, 0)),
        scratch_shapes=[
            pltpu.VMEM((384, 768), f32),
            pltpu.VMEM((384, 8), f32),
            pltpu.VMEM((2, UNITS, 8, 128), bf16),
        ],
        compiler_params=params(32),
        name="prep",
    )(place, w_up, w_down, b_up)


def segment_ends(len_ref):
    e0 = len_ref[0, 0]
    e1 = e0 + len_ref[0, 1]
    return e0, e1, e1 + len_ref[0, 2]


def segment_of(p, ends):
    return sum((p >= e).astype(i32) for e in ends)


def turn(product):
    r = product.astype(f32) * (1.0 / DFT_LEN)
    m = product - DFT_LEN * jnp.round(r).astype(i32)
    x = m.astype(f32) * (2.0 * math.pi / DFT_LEN)
    z = x * x
    c = 1.0
    s = 1.0
    for k in range(8, 0, -1):
        c = 1.0 - z * c * (1.0 / ((2 * k - 1) * (2 * k)))
        s = 1.0 - z * s * (1.0 / ((2 * k) * (2 * k + 1)))
    return c, x * s


def attend_kernel(
    len_ref, x_ref, wv_ref, bv_ref, taps_ref, wo_ref, bo_ref, ga_ref, sa_ref, q_ref, k_ref, live_ref,
    n_ref, inv_ref, low_ref, ctx_ref, col_ref, nrm_ref, scl_ref, wave_ref, wavet_ref, ks_ref, vs_ref,
    tapt_ref, live_out, qw, kb, jn, tapbuf, mix, mskd,
):
    ends = segment_ends(len_ref)
    square = (ROWS, ROWS)
    rows_i = lax.broadcasted_iota(i32, square, 0)
    lanes_i = lax.broadcasted_iota(i32, square, 1)
    jn[...] = jnp.where(segment_of(rows_i, ends) == segment_of(lanes_i, ends), 1.0 / SETS, 0.0)
    d = lax.broadcasted_iota(i32, (384, 128), 0) - 4 * lax.broadcasted_iota(i32, (384, 128), 1)
    w_lo = jnp.where(d == 0, 1.0, jnp.where(d == 1, 256.0, 0.0)).astype(bf16)
    w_hi = jnp.where(d == 2, 1.0, jnp.where(d == 3, 256.0, 0.0)).astype(bf16)
    q_codes = q_ref[...].astype(f32).astype(bf16)
    k_codes = k_ref[...].astype(f32).astype(bf16)
    qw[...] = dot(q_codes, w_lo).astype(i32) | (dot(q_codes, w_hi).astype(i32) << 16)
    kw = dot(k_codes, w_lo).T.astype(i32) | (dot(k_codes, w_hi).T.astype(i32) << 16)
    for r in range(96):
        for j in range(2):
            kb[r, j] = jnp.broadcast_to(kw[r : r + 1, j * 128 : j * 128 + 128], (8, 128))
    low7 = jnp.int32(0x7F7F7F7F)
    ones = jnp.int32(0x01010101)
    byte2 = jnp.int32(0x00FF00FF)
    tile_rows = 32
    groups = tile_rows // 8

    def tile(rt, carry):
        rs = pl.ds(pl.multiple_of(rt * tile_rows, tile_rows), tile_rows)
        qt = qw[rs, :]
        for h in range(HEADS):
            acc = [[jnp.zeros((8, 128), i32) for _ in range(2)] for _ in range(groups)]
            for g in range(8):
                c = h * 8 + g
                qc = [
                    jnp.broadcast_to(qt[t * 8 : t * 8 + 8, c : c + 1], (8, 128))
                    for t in range(groups)
                ]
                for j in range(2):
                    kk = kb[c, j]
                    for t in range(groups):
                        x = qc[t] ^ kk
                        y = ((x & low7) + low7) | x
                        acc[t][j] = acc[t][j] + (lax.shift_right_logical(y, 7) & ones)
            for j in range(2):
                parts = []
                for t in range(groups):
                    z = acc[t][j]
                    z = (z & byte2) + (lax.shift_right_logical(z, 8) & byte2)
                    z = (z & jnp.int32(0xFFFF)) + lax.shift_right_logical(z, 16)
                    parts.append((SETS - z).astype(f32))
                m = jnp.concatenate(parts, axis=0) * jn[rs, j * 128 : j * 128 + 128]
                col_ref[h, rs, j * 128 : j * 128 + 128] = m.astype(bf16)
        return carry

    lax.fori_loop(0, ROWS // tile_rows, tile, 0)

    dims = (FREQ, ROWS)
    f = lax.broadcasted_iota(i32, dims, 0)
    p = lax.broadcasted_iota(i32, dims, 1)
    c, s = turn(f * (p + MARGIN * segment_of(p, ends)))
    ok = f < LIVE_FREQ
    wave_ref[0:FREQ] = jnp.where(ok, c, 0.0).astype(bf16)
    wave_ref[FREQ:] = jnp.where(ok, s, 0.0).astype(bf16)
    p = lax.broadcasted_iota(i32, dims, 0)
    f = lax.broadcasted_iota(i32, dims, 1)
    c, s = turn(f * (p + MARGIN * segment_of(p, ends)))
    ok = f < LIVE_FREQ
    wavet_ref[:, 0:FREQ] = jnp.where(ok, c, 0.0).astype(bf16)
    wavet_ref[:, FREQ:] = jnp.where(ok, s, 0.0).astype(bf16)
    dims = (FREQ, 128)
    f = lax.broadcasted_iota(i32, dims, 0)
    c, s = turn(f * (lax.broadcasted_iota(i32, dims, 1) - MARGIN))
    tap_c = c.astype(bf16)
    tap_s = s.astype(bf16)
    dims = (128, FREQ)
    f = lax.broadcasted_iota(i32, dims, 1)
    c, s = turn(f * (lax.broadcasted_iota(i32, dims, 0) - MARGIN))
    tapt_ref[:, 0:FREQ] = c.astype(bf16)
    tapt_ref[:, FREQ:] = s.astype(bf16)
    tapbuf[...] = jnp.zeros(tapbuf.shape, f32)
    tapbuf[0:TAPS] = taps_ref[...].astype(f32)
    kernel = tapbuf[...].astype(bf16)
    f = lax.broadcasted_iota(i32, (FREQ, 1), 0)
    weight = jnp.where((f == 0) | (f == DFT_LEN // 2), 1.0 / DFT_LEN, 2.0 / DFT_LEN)
    weight = jnp.where(f < LIVE_FREQ, weight, 0.0)
    k_cos = dot(tap_c, kernel) * weight
    k_sin = dot(tap_s, kernel) * weight
    ks_ref[0:FREQ] = k_cos
    ks_ref[FREQ:] = k_sin

    live = jnp.broadcast_to(live_ref[...].astype(f32), (8, ROWS)).T[:, 0:1]
    live_out[...] = jnp.broadcast_to(live, (ROWS, 128))
    values = (dot(x_ref[...], wv_ref[...]) + bv_ref[...].astype(f32)).astype(bf16).astype(f32)
    mskd[...] = (values * live).astype(bf16)
    masked = mskd[...]
    spec = dot(wave_ref[...], masked)
    vs_ref[...] = spec.astype(bf16)
    v_cos = spec[0:FREQ]
    v_sin = spec[FREQ:]
    first_head = lanes((ROWS, 128)) < HEAD_DIM
    y_cos = (k_cos * v_cos + k_sin * v_sin).astype(bf16)
    y_sin = (k_cos * v_sin - k_sin * v_cos).astype(bf16)
    conv = dot(wavet_ref[:, 0:FREQ], y_cos) + dot(wavet_ref[:, FREQ:], y_sin)
    for b in range(COLS):
        cs = slice(b * 128, b * 128 + 128)
        block = masked[:, cs]
        m = jnp.where(first_head, dot(col_ref[2 * b], block), dot(col_ref[2 * b + 1], block))
        sq = m * m
        one = jnp.sum(jnp.where(first_head, sq, 0.0), axis=1, keepdims=True)
        two = jnp.sum(jnp.where(first_head, 0.0, sq), axis=1, keepdims=True)
        scale = lax.rsqrt(jnp.where(first_head, one, two) * (1.0 / HEAD_DIM) + 1e-06)
        scl_ref[:, cs] = scale
        nrm = m * scale
        nrm_ref[:, cs] = nrm.astype(bf16)
        mix[:, cs] = nrm
    context = (mix[...] + conv).astype(bf16)
    ctx_ref[...] = context
    attended = dot(context, wo_ref[...]) + bo_ref[...].astype(f32)
    n, inv = norm_rows(x_ref[...].astype(f32) + attended)
    n_ref[...] = n
    inv_ref[...] = jnp.broadcast_to(inv, (ROWS, 128))
    low_ref[...] = (n * ga_ref[...].astype(f32) + sa_ref[...].astype(f32)).astype(bf16)


def attend(seq_lengths, x, wv, bv, taps, wo, bo, ga, sa, q, k, live):
    wide = (ROWS, WIDTH)
    return pl.pallas_call(
        attend_kernel,
        out_shape=(
            shape(wide, f32), shape((ROWS, 128), f32), shape(wide, bf16), shape(wide, bf16),
            shape((HEADS, ROWS, ROWS), bf16), shape(wide, bf16), shape(wide, f32),
            shape((2 * FREQ, ROWS), bf16), shape((ROWS, 2 * FREQ), bf16),
            shape((2 * FREQ, WIDTH), f32), shape((2 * FREQ, WIDTH), bf16),
            shape((128, 2 * FREQ), bf16), shape((ROWS, 128), f32),
        ),
        in_specs=[SMEM] + [VMEM] * 11,
        out_specs=(VMEM,) * 13,
        scratch_shapes=[
            pltpu.VMEM((ROWS, 128), i32),
            pltpu.VMEM((96, 2, 8, 128), i32),
            pltpu.VMEM((ROWS, ROWS), f32),
            pltpu.VMEM((128, WIDTH), f32),
            pltpu.VMEM(wide, f32),
            pltpu.VMEM(wide, bf16),
        ],
        compiler_params=params(48),
        name="attend",
    )(seq_lengths, x, wv, bv, taps, wo, bo, ga, sa, q, k, live)


def untile(ref, first):
    part = ref[:, first : first + 3].astype(f32)
    return part.reshape(-1, 128).astype(bf16)


def load_up(ref, out):
    for ct in range(COLS):
        out[:, ct * 128 : ct * 128 + 128] = untile(ref, 3 * ct)
    tile = ref[:, UNITS - 1].astype(f32)
    lane = lanes(tile.shape)
    parts = [jnp.where(lane == rt, tile, 0.0)[:, None] for rt in range(3)]
    out[:, WIDTH:] = jnp.concatenate(parts, axis=1).reshape(-1, 128).astype(bf16)


def load_down(ref, out):
    for ct in range(COLS):
        out[:, ct * 128 : ct * 128 + 128] = untile(ref, 3 * ct)


def ffn_kernel(own, sib, up, down, act, slope, part_own, part_sib, rows, wu, wd, acc):
    step = pl.program_id(0)

    @pl.when(step == 0)
    def _():
        rows[0:ROWS, 0:WIDTH] = own[...]
        rows[ROWS:, 0:WIDTH] = sib[...]
        rows[:, WIDTH:] = jnp.where(lanes((2 * ROWS, 128)) < 3, 1.0, 0.0).astype(bf16)
        acc[...] = jnp.zeros(acc.shape, f32)

    load_up(up, wu)
    load_down(down, wd)

    def block(i, carry):
        hs = pl.ds(pl.multiple_of(i * 256, 256), 256)
        upper = dot_last(rows[...], wu[hs, :])
        cdf = 0.5 * (1.0 + lax.erf(upper * math.sqrt(0.5)))
        a = (upper * cdf).astype(bf16)
        act[i] = a
        density = jnp.exp(-0.5 * upper * upper) * (1.0 / math.sqrt(2.0 * math.pi))
        slope[i] = (cdf + upper * density).astype(bf16)
        acc[...] += dot(a, wd[hs, :])
        return carry

    lax.fori_loop(0, 3, block, 0)

    @pl.when(step == 1)
    def _():
        part_own[...] = acc[0:ROWS]
        part_sib[...] = acc[ROWS:].astype(bf16)


def ffn(own, sib, weights):
    wide = (ROWS, WIDTH)
    whole = lambda *dims: pl.BlockSpec(dims, lambda b: (0,) * len(dims))
    piece = (32, UNITS, 8, 128)
    hidden = (3, 2 * ROWS, 256)
    return pl.pallas_call(
        ffn_kernel,
        grid=(2,),
        out_shape=(
            shape((6, 2 * ROWS, 256), bf16), shape((6, 2 * ROWS, 256), bf16),
            shape(wide, f32), shape(wide, bf16),
        ),
        in_specs=[
            whole(*wide), whole(*wide),
            pl.BlockSpec(piece, lambda b: (b, 0, 0, 0)),
            pl.BlockSpec(piece, lambda b: (2 + b, 0, 0, 0)),
        ],
        out_specs=(
            pl.BlockSpec(hidden, lambda b: (b, 0, 0)), pl.BlockSpec(hidden, lambda b: (b, 0, 0)),
            whole(*wide), whole(*wide),
        ),
        scratch_shapes=[
            pltpu.VMEM((2 * ROWS, WIDTH + 128), bf16),
            pltpu.VMEM((768, WIDTH + 128), bf16),
            pltpu.VMEM((768, WIDTH), bf16),
            pltpu.VMEM((2 * ROWS, WIDTH), f32),
        ],
        compiler_params=params(48),
        name="ffn",
    )(own, sib, weights, weights)


def middle_kernel(n1, own, got, bd, ga, sa, gf, sf, og, out, second, low, sums):
    first = n1[...] * ga[...].astype(f32) + sa[...].astype(f32)
    n, inv = norm_rows(first + own[...] + got[...].astype(f32) + bd[...].astype(f32))
    gain = gf[...].astype(f32)
    out[...] = (n * gain + sf[...].astype(f32)).astype(bf16)
    g = og[...].astype(f32)
    grad = norm_back(g, n, inv, gain)
    second[...] = grad
    grad_low = grad.astype(bf16)
    low[...] = grad_low
    sums[0:1] = jnp.sum(grad_low.astype(f32), axis=0, keepdims=True)
    sums[1:2] = jnp.sum(g * n, axis=0, keepdims=True)
    sums[2:3] = jnp.sum(g, axis=0, keepdims=True)
    sums[3:8] = jnp.zeros((5, WIDTH), f32)


def middle(*args):
    wide = (ROWS, WIDTH)
    return pl.pallas_call(
        middle_kernel,
        out_shape=(shape(wide, bf16), shape(wide, f32), shape(wide, bf16), shape((8, WIDTH), f32)),
        in_specs=[VMEM] * 9,
        out_specs=(VMEM,) * 4,
        compiler_params=params(32),
        name="middle",
    )(*args)


def ffn_back_kernel(
    own, sib, r_own, r_sib, up, down, act, slope, grads, first_own, first_sib, rows, g, wu, wd, acc,
    gu, gd,
):
    step = pl.program_id(0)

    @pl.when(step == 0)
    def _():
        g[0:ROWS] = own[...]
        g[ROWS:] = sib[...]
        rows[0:ROWS, 0:WIDTH] = r_own[...]
        rows[ROWS:, 0:WIDTH] = r_sib[...]
        rows[:, WIDTH:] = jnp.ones((2 * ROWS, 128), bf16)
        acc[...] = jnp.zeros(acc.shape, f32)

    load_up(up, wu)
    load_down(down, wd)

    def block(i, carry):
        hs = pl.ds(pl.multiple_of(i * 256, 256), 256)
        u = (dot_last(g[...], wd[hs, :]) * slope[i].astype(f32)).astype(bf16)
        gd[hs, :] = dot_first(act[i], g[...])
        gu[hs, :] = dot_first(u, rows[...])
        acc[...] += dot(u, wu[hs, 0:WIDTH])
        return carry

    lax.fori_loop(0, 3, block, 0)
    for ct in range(COLS):
        cs = slice(ct * 128, ct * 128 + 128)
        grads[0, :, 3 * ct : 3 * ct + 3] = gu[:, cs].reshape(32, 3, 8, 128).astype(bf16)
        grads[1, :, 3 * ct : 3 * ct + 3] = gd[:, cs].reshape(32, 3, 8, 128).astype(bf16)
    bias = gu[:, WIDTH:].reshape(32, 3, 8, 128)
    lane = lanes((32, 8, 128))
    tile = jnp.where(lane == 0, bias[:, 0], jnp.where(lane == 1, bias[:, 1], bias[:, 2]))
    grads[0, :, UNITS - 1] = tile.astype(bf16)
    grads[1, :, UNITS - 1] = jnp.zeros((32, 8, 128), bf16)

    @pl.when(step == 1)
    def _():
        first_own[...] = acc[0:ROWS]
        first_sib[...] = acc[ROWS:].astype(bf16)


def ffn_back(own, sib, r_own, r_sib, weights, act, slope):
    wide = (ROWS, WIDTH)
    whole = lambda *dims: pl.BlockSpec(dims, lambda b: (0,) * len(dims))
    piece = (32, UNITS, 8, 128)
    hidden = pl.BlockSpec((3, 2 * ROWS, 256), lambda b: (b, 0, 0))
    return pl.pallas_call(
        ffn_back_kernel,
        grid=(2,),
        out_shape=(shape((2, 64, UNITS, 8, 128), bf16), shape(wide, f32), shape(wide, bf16)),
        in_specs=[
            whole(*wide), whole(*wide), whole(*wide), whole(*wide),
            pl.BlockSpec(piece, lambda b: (b, 0, 0, 0)),
            pl.BlockSpec(piece, lambda b: (2 + b, 0, 0, 0)),
            hidden, hidden,
        ],
        out_specs=(
            pl.BlockSpec((2, 32, UNITS, 8, 128), lambda b: (0, b, 0, 0, 0)),
            whole(*wide), whole(*wide),
        ),
        scratch_shapes=[
            pltpu.VMEM((2 * ROWS, WIDTH + 128), bf16),
            pltpu.VMEM((2 * ROWS, WIDTH), bf16),
            pltpu.VMEM((768, WIDTH + 128), bf16),
            pltpu.VMEM((768, WIDTH), bf16),
            pltpu.VMEM((2 * ROWS, WIDTH), f32),
            pltpu.VMEM((768, WIDTH + 128), f32),
            pltpu.VMEM((768, WIDTH), f32),
        ],
        compiler_params=params(56),
        name="ffn_back",
    )(own, sib, r_own, r_sib, weights, weights, act, slope)


def back_kernel(
    place, own, got, second, n1, inv1, ga, ctx, wo, nrm, scl, wave, wavet, ks, vs, tapt, col, live, x,
    wv, sums, in_grad, keep, give, buf_a, buf_b, mg, mb,
):
    first_grad = second[...] + own[...] + got[...].astype(f32)
    n = n1[...]
    buf_a[768 + 2 : 768 + 3] = jnp.sum(first_grad * n, axis=0, keepdims=True)
    buf_a[768 + 3 : 768 + 4] = jnp.sum(first_grad, axis=0, keepdims=True)
    resid = norm_back(first_grad, n, inv1[...][:, 0:1], ga[...].astype(f32))
    ag = resid.astype(bf16)
    buf_a[768 + 1 : 768 + 2] = jnp.sum(ag.astype(f32), axis=0, keepdims=True)
    buf_a[768 + 4 : 768 + 7] = sums[0:3]
    buf_a[768 + 7 :] = jnp.zeros((TALL - 775, WIDTH), f32)
    buf_b[0:768] = dot_first(ctx[...], ag)
    cg = dot_last(ag, wo[...])
    first_head = lanes((ROWS, 128)) < HEAD_DIM
    for b in range(COLS):
        cs = slice(b * 128, b * 128 + 128)
        c = cg[:, cs]
        m = nrm[:, cs].astype(f32)
        prod = c * m
        one = jnp.sum(jnp.where(first_head, prod, 0.0), axis=1, keepdims=True)
        two = jnp.sum(jnp.where(first_head, 0.0, prod), axis=1, keepdims=True)
        mean = jnp.where(first_head, one, two) * (1.0 / HEAD_DIM)
        mg[:, cs] = (scl[:, cs] * (c - m * mean)).astype(bf16)
    for b in range(COLS):
        cs = slice(b * 128, b * 128 + 128)
        block = mg[:, cs]
        mb[:, cs] = jnp.where(
            first_head, dot_first(col[2 * b], block), dot_first(col[2 * b + 1], block)
        )
    spec = dot(wave[...], cg.astype(bf16))
    g_cos = spec[0:FREQ]
    g_sin = spec[FREQ:]
    k_cos = ks[0:FREQ]
    k_sin = ks[FREQ:]
    z_cos = (k_cos * g_cos - k_sin * g_sin).astype(bf16)
    z_sin = (k_cos * g_sin + k_sin * g_cos).astype(bf16)
    conv = dot(wavet[:, 0:FREQ], z_cos) + dot(wavet[:, FREQ:], z_sin)
    v_cos = vs[0:FREQ].astype(f32)
    v_sin = vs[FREQ:].astype(f32)
    f = lax.broadcasted_iota(i32, (FREQ, 1), 0)
    weight = jnp.where((f == 0) | (f == DFT_LEN // 2), 1.0 / DFT_LEN, 2.0 / DFT_LEN)
    weight = jnp.where(f < LIVE_FREQ, weight, 0.0)
    re = ((g_cos * v_cos + g_sin * v_sin) * weight).astype(bf16)
    im = ((g_cos * v_sin - g_sin * v_cos) * weight).astype(bf16)
    gk = dot(tapt[:, 0:FREQ], re) + dot(tapt[:, FREQ:], im)
    buf_b[768:] = jnp.zeros((TALL - 768, WIDTH), f32)
    buf_b[768 : 768 + TAPS] = gk[0:TAPS]
    vg = ((mb[...] + conv) * live[...][:, 0:1]).astype(bf16)
    buf_a[768:769] = jnp.sum(vg.astype(f32), axis=0, keepdims=True)
    buf_a[0:768] = dot_first(x[...], vg)
    in_grad[...] = resid + dot_last(vg, wv[...])

    def write(kept, given):
        for ct in range(COLS):
            cs = slice(ct * 128, ct * 128 + 128)
            ts = slice(ct * TALL_TILES, ct * TALL_TILES + TALL_TILES)
            keep[ts] = kept[:, cs].reshape(TALL_TILES, 8, 128)
            give[ts] = given[:, cs].reshape(TALL_TILES, 8, 128).astype(bf16)

    rest = PACK - COLS * TALL_TILES
    keep[PACK - rest :] = jnp.zeros((rest, 8, 128), f32)
    give[PACK - rest :] = jnp.zeros((rest, 8, 128), bf16)

    @pl.when(place[0] % 2 == 0)
    def _():
        write(buf_a, buf_b)

    @pl.when(place[0] % 2 == 1)
    def _():
        write(buf_b, buf_a)


def attend_back(*args):
    wide = (ROWS, WIDTH)
    return pl.pallas_call(
        back_kernel,
        out_shape=(shape(wide, f32), shape((PACK, 8, 128), f32), shape((PACK, 8, 128), bf16)),
        in_specs=[SMEM] + [VMEM] * 20,
        out_specs=(VMEM,) * 3,
        scratch_shapes=[
            pltpu.VMEM((TALL, WIDTH), f32),
            pltpu.VMEM((TALL, WIDTH), f32),
            pltpu.VMEM(wide, bf16),
            pltpu.VMEM(wide, f32),
        ],
        compiler_params=params(56),
        name="attend_back",
    )(*args)


def sum_ffn_kernel(got, out, acc):
    step = pl.program_id(0)

    @pl.when(step == 0)
    def _():
        acc[...] = jnp.zeros(acc.shape, f32)

    for c in range(2):
        total = acc[c]
        for t in range(8):
            total = total + got[c * 8 + t].astype(f32)
        acc[c] = total

    @pl.when(step == 7)
    def _():
        out[...] = acc[...].astype(bf16)


def sum_ffn(got):
    return pl.pallas_call(
        sum_ffn_kernel,
        grid=(8,),
        out_shape=shape((2, UNITS, 8, 128), bf16),
        in_specs=[pl.BlockSpec((16, UNITS, 8, 128), lambda i: (i, 0, 0, 0))],
        out_specs=pl.BlockSpec((2, UNITS, 8, 128), lambda i: (0, 0, 0, 0)),
        scratch_shapes=[pltpu.VMEM((2, UNITS, 8, 128), f32)],
        compiler_params=params(32),
        name="sum_ffn",
    )(got)


def sum_rest_kernel(got, out):
    per = PACK // 128
    total = [jnp.zeros((per, 8, 128), f32) for _ in range(2)]
    for i in range(8):
        for c in range(2):
            for t in range(8):
                total[c] = total[c] + got[i * 16 + c * 8 + t].astype(f32)
    low = [t.astype(bf16) for t in total]
    for i in range(8):
        for c in range(2):
            for t in range(8):
                out[i * 16 + c * 8 + t] = low[c]


def sum_rest(got):
    return pl.pallas_call(
        sum_rest_kernel,
        out_shape=shape(got.shape, bf16),
        in_specs=[VMEM],
        out_specs=VMEM,
        compiler_params=params(32),
        name="sum_rest",
    )(got)


def final_kernel(
    place, own, other, ffn_ref, bias_ref, g_wv, g_bv, g_conv, g_wo, g_bo, g_ga, g_sa, g_up, g_bup,
    g_down, g_bd, g_gf, g_sf, vecs,
):
    ct = pl.program_id(0)

    def write(a, b):
        g_wv[...] = a[0:96].astype(f32).reshape(768, 128)
        vecs[ct] = a[96].astype(f32)
        g_wo[...] = b[0:96].astype(f32).reshape(768, 128)
        g_conv[...] = b[96:105].astype(f32).reshape(72, 128)[0:TAPS]

    @pl.when(place[0] % 2 == 0)
    def _():
        write(own, other)

    @pl.when(place[0] % 2 == 1)
    def _():
        write(other, own)

    for c in range(2):
        rs = slice(192 * c, 192 * c + 192)
        g_down[rs, :] = ffn_ref[8:16, c].astype(f32).reshape(192, 128)
        g_up[:, rs] = ffn_ref[0:8, c].astype(f32).reshape(192, 128).T

    @pl.when(ct == COLS - 1)
    def _():
        for j, ref in enumerate((g_bv, g_bo, g_ga, g_sa, g_bd, g_gf, g_sf)):
            for i in range(COLS):
                ref[i * 128 : i * 128 + 128] = vecs[i, j]
        parts = []
        for c in range(2):
            tile = bias_ref[0:8, c, 0].astype(f32)
            lane = lanes(tile.shape)
            rows = [jnp.where(lane == rt, tile, 0.0)[:, None] for rt in range(3)]
            parts.append(jnp.concatenate(rows, axis=1).reshape(192, 128))
        tall = jnp.concatenate(parts, axis=0).astype(bf16)
        g_bup[...] = dot_last(jnp.ones((8, 128), bf16), tall)[0]


def final(place, own, other, gathered):
    tile = pl.BlockSpec((TALL_TILES, 8, 128), lambda i: (i, 0, 0))
    tall = pl.BlockSpec((768, 128), lambda i: (0, i))
    vec = pl.BlockSpec((WIDTH,), lambda i: (0,))
    v = shape((WIDTH,), f32)
    return pl.pallas_call(
        final_kernel,
        grid=(COLS,),
        out_shape=(
            shape((768, 768), f32), v, shape((TAPS, 768), f32), shape((768, 768), f32), v, v, v,
            shape((768, 384), f32), shape((384,), f32), shape((384, 768), f32), v, v, v,
        ),
        in_specs=[
            SMEM, tile, tile,
            pl.BlockSpec((16, 2, 3, 8, 128), lambda i: (0, 0, i, 0, 0)),
            pl.BlockSpec((16, 2, 1, 8, 128), lambda i: (0, 0, UNITS - 1, 0, 0)),
        ],
        out_specs=(
            tall, vec, pl.BlockSpec((TAPS, 128), lambda i: (0, i)), tall, vec, vec, vec,
            pl.BlockSpec((128, 384), lambda i: (i, 0)), pl.BlockSpec((384,), lambda i: (0,)),
            pl.BlockSpec((384, 128), lambda i: (0, i)), vec, vec, vec,
        ),
        scratch_shapes=[pltpu.VMEM((COLS, 8, 128), f32)],
        compiler_params=params(32),
        name="final",
    )(place, own, other, gathered, gathered)


def body(
    block_input,
    w_value,
    b_value,
    conv_kernel,
    w_out,
    b_out,
    gain_attn,
    shift_attn,
    w_up,
    b_up,
    w_down,
    b_down,
    gain_ffn,
    shift_ffn,
    query_codes,
    key_codes,
    key_live,
    seq_lengths,
    out_grad,
):
    dp = lax.axis_index("dp")
    place = jnp.stack([dp, lax.axis_index("tensor")]).astype(i32)
    pairs = [(i, i ^ 1) for i in range(lax.axis_size("dp"))]

    def swap(x):
        return lax.ppermute(x, "dp", pairs)

    def exchange(x):
        return lax.all_to_all(x, ALL, 0, 0, tiled=True)

    def row(v):
        return v.reshape(1, -1)

    weights = exchange(prep(place, w_up, w_down, row(b_up)))
    (n1, inv1, low, ctx, collide, nrm, scl, wave, wavet, ks, vs, tapt, live) = attend(
        seq_lengths, block_input, w_value, row(b_value), conv_kernel, w_out, row(b_out),
        row(gain_attn), row(shift_attn), query_codes, key_codes, row(key_live),
    )
    low_sib = swap(low)
    act, slope, part_own, part_sib = ffn(low, low_sib, weights)
    block_output, second, grad_low, sums = middle(
        n1, part_own, swap(part_sib), row(b_down), row(gain_attn), row(shift_attn), row(gain_ffn),
        row(shift_ffn), out_grad,
    )
    grads, first_own, first_sib = ffn_back(
        grad_low, swap(grad_low), low, low_sib, weights, act, slope
    )
    owned = exchange(grads.reshape(128, UNITS, 8, 128))
    input_grad, keep, give = attend_back(
        place, first_own, swap(first_sib), second, n1, inv1, row(gain_attn), ctx, w_out, nrm, scl,
        wave, wavet, ks, vs, tapt, collide, live, block_input, w_value, sums,
    )
    pair = (keep + swap(give).astype(f32)).astype(bf16).reshape(128, PACK // 128, 8, 128)
    owned = sum_ffn(owned)
    pair, owned = lax.optimization_barrier((pair, owned))
    gathered = lax.all_gather(owned, "dp", axis=0)
    back = exchange(sum_rest(exchange(pair))).reshape(PACK, 8, 128)
    (g_wv, g_bv, g_conv, g_wo, g_bo, g_ga, g_sa, g_up, g_bup, g_down, g_bd, g_gf, g_sf) = final(
        place, back, swap(back), gathered
    )
    return (
        block_output, input_grad, g_wv, g_bv, g_conv, g_wo, g_bo, g_ga, g_sa, g_up, g_bup, g_down,
        g_bd, g_gf, g_sf,
    )


def solution(mesh):
    rows = P(ALL, None)
    return jax.shard_map(
        body,
        mesh=mesh,
        in_specs=(
            rows, P(), P(), P(), P(), P(), P(), P(),
            P(None, "tensor"), P("tensor"), P("tensor", None), P(), P(), P(),
            rows, rows, P(ALL), rows, rows,
        ),
        out_specs=(
            rows, rows, P(), P(), P(), P(), P(), P(), P(),
            P(None, "tensor"), P("tensor"), P("tensor", None), P(), P(), P(),
        ),
        check_vma=False,
    )
```

```python
import math

import jax
import jax.numpy as jnp
from jax import lax
from jax.experimental import pallas as pl
from jax.experimental.pallas import tpu as pltpu
from jax.sharding import PartitionSpec as P

HEADS = 12
SETS = 32
ROWS = 256
WIDTH = 768
HEAD_DIM = 64
COLS = WIDTH // 128
TAPS = 65
MARGIN = 32
DFT_LEN = 384
FREQ = 256
LIVE_FREQ = DFT_LEN // 2 + 1
CLASSES = 4
SUB = 96
PIECE = 24
PIECES = SUB // PIECE
UNITS = 10
HIDDEN = 768
HALF = ROWS // 2
TALL = 848
TALL_TILES = TALL // 8
PACK = 640
ALL = ("dp", "tensor")

bf16 = jnp.bfloat16
f32 = jnp.float32
i32 = jnp.int32

VMEM = pl.BlockSpec(memory_space=pltpu.VMEM)
SMEM = pl.BlockSpec(memory_space=pltpu.SMEM)


def shape(dims, dtype):
    return jax.ShapeDtypeStruct(dims, dtype)


def params(mib):
    return pltpu.CompilerParams(vmem_limit_bytes=mib << 20)


def dot(a, b):
    return lax.dot_general(a, b, (((1,), (0,)), ((), ())), preferred_element_type=f32)


def dot_last(a, b):
    return lax.dot_general(a, b, (((1,), (1,)), ((), ())), preferred_element_type=f32)


def dot_first(a, b):
    return lax.dot_general(a, b, (((0,), (0,)), ((), ())), preferred_element_type=f32)


def lanes(dims):
    return lax.broadcasted_iota(i32, dims, len(dims) - 1)


def norm_rows(r):
    mean = jnp.mean(r, axis=-1, keepdims=True)
    centred = r - mean
    inv = lax.rsqrt(jnp.mean(centred * centred, axis=-1, keepdims=True) + 1e-05)
    return centred * inv, inv


def norm_back(g, n, inv, gain):
    e = g * gain
    return (
        e - jnp.mean(e, axis=-1, keepdims=True) - n * jnp.mean(e * n, axis=-1, keepdims=True)
    ) * inv


def prep_kernel(place, up_ref, down_ref, bias_ref, out_ref, tall, cols, piece):
    rep = place[0] % 8
    side = rep % 2

    @pl.when(pl.program_id(0) == 0)
    def _():
        @pl.when(place[0] < 8)
        def _():
            tall[...] = up_ref[...].astype(f32).T
            cols[...] = jnp.broadcast_to(bias_ref[...].astype(f32), (8, 384)).T

        @pl.when(place[0] >= 8)
        def _():
            tall[...] = down_ref[...].astype(f32)
            cols[...] = jnp.zeros(cols.shape, f32)

        for q in range(CLASSES):
            start = pl.multiple_of(SUB * q + PIECE * (rep // 2), 8)
            rows = tall[pl.ds(start, PIECE), :]
            for j in range(3):
                left = rows[:, j * 128 : j * 128 + 128]
                right = rows[:, 384 + j * 128 : 512 + j * 128]
                part = jnp.where(side == 0, left, right).reshape(3, 8, 128)
                piece[q, 3 * j : 3 * j + 3] = part.astype(bf16)
            bias = jnp.zeros((8, 128), f32)
            for rt in range(3):
                col = cols[pl.ds(pl.multiple_of(start + 8 * rt, 8), 8), :][:, 0:1]
                bias = jnp.where(lanes((8, 128)) == rt, jnp.broadcast_to(col, (8, 128)), bias)
            piece[q, UNITS - 1] = jnp.where(side == 0, bias, 0.0).astype(bf16)

    for n in range(32):
        out_ref[n] = piece[n // 8]


def prep(place, w_up, w_down, b_up):
    whole = lambda *dims: pl.BlockSpec(dims, lambda i: (0,) * len(dims))
    return pl.pallas_call(
        prep_kernel,
        grid=(4,),
        out_shape=shape((128, UNITS, 8, 128), bf16),
        in_specs=[SMEM, whole(768, 384), whole(384, 768), whole(1, 384)],
        out_specs=pl.BlockSpec((32, UNITS, 8, 128), lambda i: (i, 0, 0, 0)),
        scratch_shapes=[
            pltpu.VMEM((384, 768), f32),
            pltpu.VMEM((384, 8), f32),
            pltpu.VMEM((CLASSES, UNITS, 8, 128), bf16),
        ],
        compiler_params=params(32),
        name="prep",
    )(place, w_up, w_down, b_up)


def segment_ends(len_ref):
    e0 = len_ref[0, 0]
    e1 = e0 + len_ref[0, 1]
    return e0, e1, e1 + len_ref[0, 2]


def segment_of(p, ends):
    return sum((p >= e).astype(i32) for e in ends)


def turn(product):
    r = product.astype(f32) * (1.0 / DFT_LEN)
    m = product - DFT_LEN * jnp.round(r).astype(i32)
    x = m.astype(f32) * (2.0 * math.pi / DFT_LEN)
    z = x * x
    c = 1.0
    s = 1.0
    for k in range(8, 0, -1):
        c = 1.0 - z * c * (1.0 / ((2 * k - 1) * (2 * k)))
        s = 1.0 - z * s * (1.0 / ((2 * k) * (2 * k + 1)))
    return c, x * s


def attend_kernel(
    len_ref, x_ref, wv_ref, bv_ref, taps_ref, wo_ref, bo_ref, ga_ref, sa_ref, q_ref, k_ref, live_ref,
    n_ref, inv_ref, low_ref, low_a, low_b, ctx_ref, col_ref, nrm_ref, scl_ref, wave_ref, wavet_ref, ks_ref, vs_ref,
    tapt_ref, live_out, qw, kb, jn, tapbuf, mix, mskd,
):
    ends = segment_ends(len_ref)
    square = (ROWS, ROWS)
    rows_i = lax.broadcasted_iota(i32, square, 0)
    lanes_i = lax.broadcasted_iota(i32, square, 1)
    jn[...] = jnp.where(segment_of(rows_i, ends) == segment_of(lanes_i, ends), 1.0 / SETS, 0.0)
    d = lax.broadcasted_iota(i32, (384, 128), 0) - 4 * lax.broadcasted_iota(i32, (384, 128), 1)
    w_lo = jnp.where(d == 0, 1.0, jnp.where(d == 1, 256.0, 0.0)).astype(bf16)
    w_hi = jnp.where(d == 2, 1.0, jnp.where(d == 3, 256.0, 0.0)).astype(bf16)
    q_codes = q_ref[...].astype(f32).astype(bf16)
    k_codes = k_ref[...].astype(f32).astype(bf16)
    qw[...] = dot(q_codes, w_lo).astype(i32) | (dot(q_codes, w_hi).astype(i32) << 16)
    kw = dot(k_codes, w_lo).T.astype(i32) | (dot(k_codes, w_hi).T.astype(i32) << 16)
    for r in range(96):
        for j in range(2):
            kb[r, j] = jnp.broadcast_to(kw[r : r + 1, j * 128 : j * 128 + 128], (8, 128))
    low7 = jnp.int32(0x7F7F7F7F)
    ones = jnp.int32(0x01010101)
    byte2 = jnp.int32(0x00FF00FF)
    tile_rows = 32
    groups = tile_rows // 8

    def tile(rt, carry):
        rs = pl.ds(pl.multiple_of(rt * tile_rows, tile_rows), tile_rows)
        qt = qw[rs, :]
        for h in range(HEADS):
            acc = [[jnp.zeros((8, 128), i32) for _ in range(2)] for _ in range(groups)]
            for g in range(8):
                c = h * 8 + g
                qc = [
                    jnp.broadcast_to(qt[t * 8 : t * 8 + 8, c : c + 1], (8, 128))
                    for t in range(groups)
                ]
                for j in range(2):
                    kk = kb[c, j]
                    for t in range(groups):
                        x = qc[t] ^ kk
                        y = ((x & low7) + low7) | x
                        acc[t][j] = acc[t][j] + (lax.shift_right_logical(y, 7) & ones)
            for j in range(2):
                parts = []
                for t in range(groups):
                    z = acc[t][j]
                    z = (z & byte2) + (lax.shift_right_logical(z, 8) & byte2)
                    z = (z & jnp.int32(0xFFFF)) + lax.shift_right_logical(z, 16)
                    parts.append((SETS - z).astype(f32))
                m = jnp.concatenate(parts, axis=0) * jn[rs, j * 128 : j * 128 + 128]
                col_ref[h, rs, j * 128 : j * 128 + 128] = m.astype(bf16)
        return carry

    lax.fori_loop(0, ROWS // tile_rows, tile, 0)

    dims = (FREQ, ROWS)
    f = lax.broadcasted_iota(i32, dims, 0)
    p = lax.broadcasted_iota(i32, dims, 1)
    c, s = turn(f * (p + MARGIN * segment_of(p, ends)))
    ok = f < LIVE_FREQ
    wave_ref[0:FREQ] = jnp.where(ok, c, 0.0).astype(bf16)
    wave_ref[FREQ:] = jnp.where(ok, s, 0.0).astype(bf16)
    p = lax.broadcasted_iota(i32, dims, 0)
    f = lax.broadcasted_iota(i32, dims, 1)
    c, s = turn(f * (p + MARGIN * segment_of(p, ends)))
    ok = f < LIVE_FREQ
    wavet_ref[:, 0:FREQ] = jnp.where(ok, c, 0.0).astype(bf16)
    wavet_ref[:, FREQ:] = jnp.where(ok, s, 0.0).astype(bf16)
    dims = (FREQ, 128)
    f = lax.broadcasted_iota(i32, dims, 0)
    c, s = turn(f * (lax.broadcasted_iota(i32, dims, 1) - MARGIN))
    tap_c = c.astype(bf16)
    tap_s = s.astype(bf16)
    dims = (128, FREQ)
    f = lax.broadcasted_iota(i32, dims, 1)
    c, s = turn(f * (lax.broadcasted_iota(i32, dims, 0) - MARGIN))
    tapt_ref[:, 0:FREQ] = c.astype(bf16)
    tapt_ref[:, FREQ:] = s.astype(bf16)
    tapbuf[...] = jnp.zeros(tapbuf.shape, f32)
    tapbuf[0:TAPS] = taps_ref[...].astype(f32)
    kernel = tapbuf[...].astype(bf16)
    f = lax.broadcasted_iota(i32, (FREQ, 1), 0)
    weight = jnp.where((f == 0) | (f == DFT_LEN // 2), 1.0 / DFT_LEN, 2.0 / DFT_LEN)
    weight = jnp.where(f < LIVE_FREQ, weight, 0.0)
    k_cos = dot(tap_c, kernel) * weight
    k_sin = dot(tap_s, kernel) * weight
    ks_ref[0:FREQ] = k_cos
    ks_ref[FREQ:] = k_sin

    live = jnp.broadcast_to(live_ref[...].astype(f32), (8, ROWS)).T[:, 0:1]
    live_out[...] = jnp.broadcast_to(live, (ROWS, 128))
    values = (dot(x_ref[...], wv_ref[...]) + bv_ref[...].astype(f32)).astype(bf16).astype(f32)
    mskd[...] = (values * live).astype(bf16)
    masked = mskd[...]
    spec = dot(wave_ref[...], masked)
    vs_ref[...] = spec.astype(bf16)
    v_cos = spec[0:FREQ]
    v_sin = spec[FREQ:]
    first_head = lanes((ROWS, 128)) < HEAD_DIM
    y_cos = (k_cos * v_cos + k_sin * v_sin).astype(bf16)
    y_sin = (k_cos * v_sin - k_sin * v_cos).astype(bf16)
    conv = dot(wavet_ref[:, 0:FREQ], y_cos) + dot(wavet_ref[:, FREQ:], y_sin)
    for b in range(COLS):
        cs = slice(b * 128, b * 128 + 128)
        block = masked[:, cs]
        m = jnp.where(first_head, dot(col_ref[2 * b], block), dot(col_ref[2 * b + 1], block))
        sq = m * m
        one = jnp.sum(jnp.where(first_head, sq, 0.0), axis=1, keepdims=True)
        two = jnp.sum(jnp.where(first_head, 0.0, sq), axis=1, keepdims=True)
        scale = lax.rsqrt(jnp.where(first_head, one, two) * (1.0 / HEAD_DIM) + 1e-06)
        scl_ref[:, cs] = scale
        nrm = m * scale
        nrm_ref[:, cs] = nrm.astype(bf16)
        mix[:, cs] = nrm
    context = (mix[...] + conv).astype(bf16)
    ctx_ref[...] = context
    attended = dot(context, wo_ref[...]) + bo_ref[...].astype(f32)
    n, inv = norm_rows(x_ref[...].astype(f32) + attended)
    n_ref[...] = n
    inv_ref[...] = jnp.broadcast_to(inv, (ROWS, 128))
    low = (n * ga_ref[...].astype(f32) + sa_ref[...].astype(f32)).astype(bf16)
    low_ref[...] = low
    low_a[...] = low[0:HALF]
    low_b[...] = low[HALF:]


def attend(seq_lengths, x, wv, bv, taps, wo, bo, ga, sa, q, k, live):
    wide = (ROWS, WIDTH)
    half = (HALF, WIDTH)
    return pl.pallas_call(
        attend_kernel,
        out_shape=(
            shape(wide, f32), shape((ROWS, 128), f32), shape(wide, bf16), shape(half, bf16),
            shape(half, bf16), shape(wide, bf16), shape((HEADS, ROWS, ROWS), bf16), shape(wide, bf16), shape(wide, f32),
            shape((2 * FREQ, ROWS), bf16), shape((ROWS, 2 * FREQ), bf16),
            shape((2 * FREQ, WIDTH), f32), shape((2 * FREQ, WIDTH), bf16),
            shape((128, 2 * FREQ), bf16), shape((ROWS, 128), f32),
        ),
        in_specs=[SMEM] + [VMEM] * 11,
        out_specs=(VMEM,) * 15,
        scratch_shapes=[
            pltpu.VMEM((ROWS, 128), i32),
            pltpu.VMEM((96, 2, 8, 128), i32),
            pltpu.VMEM((ROWS, ROWS), f32),
            pltpu.VMEM((128, WIDTH), f32),
            pltpu.VMEM(wide, f32),
            pltpu.VMEM(wide, bf16),
        ],
        compiler_params=params(32),
        name="attend",
    )(seq_lengths, x, wv, bv, taps, wo, bo, ga, sa, q, k, live)


def unpack(ref, m, out):
    for a in range(PIECES):
        rs = slice(a * 192, a * 192 + 192)
        for ct in range(COLS):
            first = 3 * (ct % 3)
            part = ref[m, a, ct // 3, :, first : first + 3].astype(f32)
            out[rs, ct * 128 : ct * 128 + 128] = part.reshape(192, 128).astype(bf16)


def unpack_bias(ref, out):
    for a in range(PIECES):
        tile = ref[0, a, 0, :, UNITS - 1].astype(f32)
        lane = lanes(tile.shape)
        parts = [jnp.where(lane == rt, tile, 0.0)[:, None] for rt in range(3)]
        column = jnp.concatenate(parts, axis=1).reshape(192, 128)
        out[a * 192 : a * 192 + 192, WIDTH:] = column.astype(bf16)


def ffn_rows(own, sib, rows, ones):
    rows[0:ROWS, 0:WIDTH] = own
    rows[ROWS:, 0:WIDTH] = sib
    rows[:, WIDTH:] = jnp.where(lanes((2 * ROWS, 128)) < ones, 1.0, 0.0).astype(bf16)


def ffn_blocks(rows, wu, wd, act, slope, acc):
    acc[...] = jnp.zeros(acc.shape, f32)

    def block(i, carry):
        hs = pl.ds(pl.multiple_of(i * 256, 256), 256)
        upper = dot_last(rows[...], wu[hs, :])
        cdf = 0.5 * (1.0 + lax.erf(upper * math.sqrt(0.5)))
        a = (upper * cdf).astype(bf16)
        act[:, hs] = a
        density = jnp.exp(-0.5 * upper * upper) * (1.0 / math.sqrt(2.0 * math.pi))
        slope[:, hs] = (cdf + upper * density).astype(bf16)
        acc[...] += dot(a, wd[hs, :])
        return carry

    lax.fori_loop(0, HIDDEN // 256, block, 0)


def ffn_far_kernel(
    got_a, got_b, sib, w, act, slope, part_own, part_sib, rows_out, wu, wd, rows, acc,
):
    ffn_rows(jnp.concatenate([got_a[...], got_b[...]], axis=0), sib[...], rows, 3)
    unpack(w, 0, wu)
    unpack_bias(w, wu)
    unpack(w, 1, wd)
    rows_out[...] = rows[:, 0:WIDTH]
    ffn_blocks(rows, wu, wd, act, slope, acc)
    part_own[...] = acc[0:ROWS]
    part_sib[...] = acc[ROWS:].astype(bf16)


def ffn_near_kernel(own, sib, wu, wd, act, slope, part_own, part_sib, rows_out, rows, acc):
    ffn_rows(own[...], sib[...], rows, 3)
    rows_out[...] = rows[:, 0:WIDTH]
    ffn_blocks(rows, wu, wd, act, slope, acc)
    part_own[...] = acc[0:ROWS]
    part_sib[...] = acc[ROWS:].astype(bf16)


def ffn_call(kernel, weights_out, *args):
    wide = (ROWS, WIDTH)
    tall = shape((2 * ROWS, WIDTH), bf16)
    outs = (tall, tall, shape(wide, f32), shape(wide, bf16), tall)
    if weights_out:
        outs += (shape((HIDDEN, WIDTH + 128), bf16), shape((HIDDEN, WIDTH), bf16))
    return pl.pallas_call(
        kernel,
        out_shape=outs,
        in_specs=[VMEM] * len(args),
        out_specs=(VMEM,) * len(outs),
        scratch_shapes=[
            pltpu.VMEM((2 * ROWS, WIDTH + 128), bf16),
            pltpu.VMEM((2 * ROWS, WIDTH), f32),
        ],
        compiler_params=params(24),
        name="ffn_far" if weights_out else "ffn_near",
    )(*args)


def combine_kernel(own, got, out_a, out_b):
    total = (own[...] + got[...].astype(f32)).astype(bf16)
    out_a[...] = total[0:HALF]
    out_b[...] = total[HALF:]


def combine(own, got):
    half = shape((HALF, WIDTH), bf16)
    return pl.pallas_call(
        combine_kernel,
        out_shape=(half, half),
        in_specs=[VMEM] * 2,
        out_specs=(VMEM,) * 2,
        compiler_params=params(32),
        name="combine",
    )(own, got)


def gather_rows(own, near, far_a, far_b):
    far = jnp.concatenate([far_a[...], far_b[...]], axis=0)
    return own[...] + near[...].astype(f32) + far.astype(f32)


def middle_kernel(
    n1, own, near, far_a, far_b, bd, ga, sa, gf, sf, og, out, second, low, low_a, low_b, sums,
):
    first = n1[...] * ga[...].astype(f32) + sa[...].astype(f32)
    n, inv = norm_rows(first + gather_rows(own, near, far_a, far_b) + bd[...].astype(f32))
    gain = gf[...].astype(f32)
    out[...] = (n * gain + sf[...].astype(f32)).astype(bf16)
    g = og[...].astype(f32)
    grad = norm_back(g, n, inv, gain)
    second[...] = grad
    grad_low = grad.astype(bf16)
    low[...] = grad_low
    low_a[...] = grad_low[0:HALF]
    low_b[...] = grad_low[HALF:]
    sums[0:1] = jnp.sum(grad_low.astype(f32), axis=0, keepdims=True)
    sums[1:2] = jnp.sum(g * n, axis=0, keepdims=True)
    sums[2:3] = jnp.sum(g, axis=0, keepdims=True)
    sums[3:8] = jnp.zeros((5, WIDTH), f32)


def middle(*args):
    wide = (ROWS, WIDTH)
    half = (HALF, WIDTH)
    return pl.pallas_call(
        middle_kernel,
        out_shape=(
            shape(wide, bf16), shape(wide, f32), shape(wide, bf16), shape(half, bf16),
            shape(half, bf16), shape((8, WIDTH), f32),
        ),
        in_specs=[VMEM] * 11,
        out_specs=(VMEM,) * 6,
        compiler_params=params(32),
        name="middle",
    )(*args)


def back_blocks(g, wu, wd, slope, u_out, bias, acc):
    acc[...] = jnp.zeros(acc.shape, f32)
    bias[...] = jnp.zeros(bias.shape, f32)

    def block(i, carry):
        hs = pl.ds(pl.multiple_of(i * 256, 256), 256)
        u = (dot_last(g[...], wd[hs, :]) * slope[:, hs].astype(f32)).astype(bf16)
        u_out[:, hs] = u
        bias[0:1, hs] = jnp.sum(u.astype(f32), axis=0, keepdims=True)
        acc[...] += dot(u, wu[hs, 0:WIDTH])
        return carry

    lax.fori_loop(0, HIDDEN // 256, block, 0)


def back_near_kernel(own, sib, wu, wd, slope, first_own, first_sib, g, u, bias, acc):
    g[0:ROWS] = own[...]
    g[ROWS:] = sib[...]
    back_blocks(g, wu, wd, slope, u, bias, acc)
    first_own[...] = acc[0:ROWS]
    first_sib[...] = acc[ROWS:].astype(bf16)


def back_far_kernel(got_a, got_b, sib, wu, wd, slope, first_own, first_sib, g, u, bias, acc):
    g[0:HALF] = got_a[...]
    g[HALF:ROWS] = got_b[...]
    g[ROWS:] = sib[...]
    back_blocks(g, wu, wd, slope, u, bias, acc)
    first_own[...] = acc[0:ROWS]
    first_sib[...] = acc[ROWS:].astype(bf16)


def back_call(kernel, name, *args):
    wide = (ROWS, WIDTH)
    tall = shape((2 * ROWS, WIDTH), bf16)
    outs = (shape(wide, f32), shape(wide, bf16), tall, tall, shape((8, HIDDEN), f32))
    return pl.pallas_call(
        kernel,
        out_shape=outs,
        in_specs=[VMEM] * len(args),
        out_specs=(VMEM,) * len(outs),
        scratch_shapes=[pltpu.VMEM((2 * ROWS, WIDTH), f32)],
        compiler_params=params(24),
        name=name,
    )(*args)


def pack_kernel(gu, gd, bias_n, bias_f, grads):
    column = (bias_n[...] + bias_f[...]).T[:, 0:1]
    for a in range(PIECES):
        rs = slice(a * 192, a * 192 + 192)
        for ct in range(COLS):
            cs = slice(ct * 128, ct * 128 + 128)
            us = slice(3 * (ct % 3), 3 * (ct % 3) + 3)
            up = gu[rs, cs].astype(f32).reshape(8, 3, 8, 128)
            down = gd[rs, cs].astype(f32).reshape(8, 3, 8, 128)
            grads[0, a, ct // 3, :, us] = up.astype(bf16)
            grads[1, a, ct // 3, :, us] = down.astype(bf16)
        bias = jnp.broadcast_to(column[rs], (192, 128)).reshape(8, 3, 8, 128)
        lane = lanes((8, 8, 128))
        tile = jnp.where(lane == 0, bias[:, 0], jnp.where(lane == 1, bias[:, 1], bias[:, 2]))
        empty = jnp.zeros((8, 8, 128), bf16)
        grads[0, a, 0, :, UNITS - 1] = tile.astype(bf16)
        grads[0, a, 1, :, UNITS - 1] = empty
        grads[1, a, 0, :, UNITS - 1] = empty
        grads[1, a, 1, :, UNITS - 1] = empty


def pack(*args):
    return pl.pallas_call(
        pack_kernel,
        out_shape=shape((2, PIECES, 2, 8, UNITS, 8, 128), bf16),
        in_specs=[VMEM] * 4,
        out_specs=VMEM,
        compiler_params=params(16),
        name="pack",
    )(*args)


def back_kernel(
    place, own, near, far_a, far_b, second, n1, inv1, ga, ctx, wo, nrm, scl, wave, wavet, ks, vs, tapt, col, live, x,
    wv, sums, in_grad, keep, give, buf_a, buf_b, mg, mb,
):
    first_grad = second[...] + gather_rows(own, near, far_a, far_b)
    n = n1[...]
    buf_a[768 + 2 : 768 + 3] = jnp.sum(first_grad * n, axis=0, keepdims=True)
    buf_a[768 + 3 : 768 + 4] = jnp.sum(first_grad, axis=0, keepdims=True)
    resid = norm_back(first_grad, n, inv1[...][:, 0:1], ga[...].astype(f32))
    ag = resid.astype(bf16)
    buf_a[768 + 1 : 768 + 2] = jnp.sum(ag.astype(f32), axis=0, keepdims=True)
    buf_a[768 + 4 : 768 + 7] = sums[0:3]
    buf_a[768 + 7 :] = jnp.zeros((TALL - 775, WIDTH), f32)
    buf_b[0:768] = dot_first(ctx[...], ag)
    cg = dot_last(ag, wo[...])
    first_head = lanes((ROWS, 128)) < HEAD_DIM
    for b in range(COLS):
        cs = slice(b * 128, b * 128 + 128)
        c = cg[:, cs]
        m = nrm[:, cs].astype(f32)
        prod = c * m
        one = jnp.sum(jnp.where(first_head, prod, 0.0), axis=1, keepdims=True)
        two = jnp.sum(jnp.where(first_head, 0.0, prod), axis=1, keepdims=True)
        mean = jnp.where(first_head, one, two) * (1.0 / HEAD_DIM)
        mg[:, cs] = (scl[:, cs] * (c - m * mean)).astype(bf16)
    for b in range(COLS):
        cs = slice(b * 128, b * 128 + 128)
        block = mg[:, cs]
        mb[:, cs] = jnp.where(
            first_head, dot_first(col[2 * b], block), dot_first(col[2 * b + 1], block)
        )
    spec = dot(wave[...], cg.astype(bf16))
    g_cos = spec[0:FREQ]
    g_sin = spec[FREQ:]
    k_cos = ks[0:FREQ]
    k_sin = ks[FREQ:]
    z_cos = (k_cos * g_cos - k_sin * g_sin).astype(bf16)
    z_sin = (k_cos * g_sin + k_sin * g_cos).astype(bf16)
    conv = dot(wavet[:, 0:FREQ], z_cos) + dot(wavet[:, FREQ:], z_sin)
    v_cos = vs[0:FREQ].astype(f32)
    v_sin = vs[FREQ:].astype(f32)
    f = lax.broadcasted_iota(i32, (FREQ, 1), 0)
    weight = jnp.where((f == 0) | (f == DFT_LEN // 2), 1.0 / DFT_LEN, 2.0 / DFT_LEN)
    weight = jnp.where(f < LIVE_FREQ, weight, 0.0)
    re = ((g_cos * v_cos + g_sin * v_sin) * weight).astype(bf16)
    im = ((g_cos * v_sin - g_sin * v_cos) * weight).astype(bf16)
    gk = dot(tapt[:, 0:FREQ], re) + dot(tapt[:, FREQ:], im)
    buf_b[768:] = jnp.zeros((TALL - 768, WIDTH), f32)
    buf_b[768 : 768 + TAPS] = gk[0:TAPS]
    vg = ((mb[...] + conv) * live[...][:, 0:1]).astype(bf16)
    buf_a[768:769] = jnp.sum(vg.astype(f32), axis=0, keepdims=True)
    buf_a[0:768] = dot_first(x[...], vg)
    in_grad[...] = resid + dot_last(vg, wv[...])

    def write(kept, given):
        for ct in range(COLS):
            cs = slice(ct * 128, ct * 128 + 128)
            ts = slice(ct * TALL_TILES, ct * TALL_TILES + TALL_TILES)
            keep[ts] = kept[:, cs].reshape(TALL_TILES, 8, 128).astype(bf16)
            give[ts] = given[:, cs].reshape(TALL_TILES, 8, 128).astype(bf16)

    rest = PACK - COLS * TALL_TILES
    keep[PACK - rest :] = jnp.zeros((rest, 8, 128), bf16)
    give[PACK - rest :] = jnp.zeros((rest, 8, 128), bf16)

    @pl.when(place[0] % 2 == 0)
    def _():
        write(buf_a, buf_b)

    @pl.when(place[0] % 2 == 1)
    def _():
        write(buf_b, buf_a)


def attend_back(*args):
    wide = (ROWS, WIDTH)
    return pl.pallas_call(
        back_kernel,
        out_shape=(shape(wide, f32), shape((PACK, 8, 128), bf16), shape((PACK, 8, 128), bf16)),
        in_specs=[SMEM] + [VMEM] * 22,
        out_specs=(VMEM,) * 3,
        scratch_shapes=[
            pltpu.VMEM((TALL, WIDTH), f32),
            pltpu.VMEM((TALL, WIDTH), f32),
            pltpu.VMEM(wide, bf16),
            pltpu.VMEM(wide, f32),
        ],
        compiler_params=params(40),
        name="attend_back",
    )(*args)


def sum_ffn_kernel(got, out, acc):
    step = pl.program_id(0)

    @pl.when(step == 0)
    def _():
        acc[...] = jnp.zeros(acc.shape, f32)

    for q in range(CLASSES):
        total = acc[q]
        for t in range(8):
            total = total + got[q * 8 + t].astype(f32)
        acc[q] = total

    @pl.when(step == 3)
    def _():
        out[...] = acc[...].astype(bf16)


def sum_ffn(got):
    return pl.pallas_call(
        sum_ffn_kernel,
        grid=(4,),
        out_shape=shape((CLASSES, UNITS, 8, 128), bf16),
        in_specs=[pl.BlockSpec((32, UNITS, 8, 128), lambda i: (i, 0, 0, 0))],
        out_specs=pl.BlockSpec((CLASSES, UNITS, 8, 128), lambda i: (0, 0, 0, 0)),
        scratch_shapes=[pltpu.VMEM((CLASSES, UNITS, 8, 128), f32)],
        compiler_params=params(32),
        name="sum_ffn",
    )(got)


def sum_rest_kernel(got, out):
    per = PACK // 128
    total = [jnp.zeros((per, 8, 128), f32) for _ in range(2)]
    for i in range(8):
        for c in range(2):
            for t in range(8):
                total[c] = total[c] + got[i * 16 + c * 8 + t].astype(f32)
    low = [t.astype(bf16) for t in total]
    for i in range(8):
        for c in range(2):
            for t in range(8):
                out[i * 16 + c * 8 + t] = low[c]


def sum_rest(got):
    return pl.pallas_call(
        sum_rest_kernel,
        out_shape=shape(got.shape, bf16),
        in_specs=[VMEM],
        out_specs=VMEM,
        compiler_params=params(32),
        name="sum_rest",
    )(got)


def final_kernel(
    place, own, other, ffn_own, ffn_oth, bias_own, bias_oth, g_wv, g_bv, g_conv, g_wo, g_bo, g_ga, g_sa, g_up, g_bup,
    g_down, g_bd, g_gf, g_sf, vecs, tall,
):
    ct = pl.program_id(0)

    def write(a, b):
        g_wv[...] = a[0:96].astype(f32).reshape(768, 128)
        vecs[ct] = a[96].astype(f32)
        g_wo[...] = b[0:96].astype(f32).reshape(768, 128)
        g_conv[...] = b[96:105].astype(f32).reshape(72, 128)[0:TAPS]

    @pl.when(place[0] % 2 == 0)
    def _():
        write(own, other)

    @pl.when(place[0] % 2 == 1)
    def _():
        write(other, own)

    core = place[0] % 2

    def index(m, a):
        return (m + place[0] // 8) % 2 * 4 + (place[0] // 2 % 4 + 4 - a) % 4

    def spread(ref):
        for a in range(PIECES):
            up = ref[index(0, a)].astype(f32)
            down = ref[index(1, a)].astype(f32)
            for q in range(CLASSES):
                rs = slice(SUB * q + PIECE * a, SUB * q + PIECE * a + PIECE)
                tall[rs, :] = up[q].reshape(PIECE, 128)
                g_down[rs, :] = down[q].reshape(PIECE, 128)

    @pl.when(ct // 3 == core)
    def _():
        spread(ffn_own)

    @pl.when(ct // 3 != core)
    def _():
        spread(ffn_oth)

    g_up[...] = tall[...].T

    @pl.when(ct == COLS - 1)
    def _():
        for j, ref in enumerate((g_bv, g_bo, g_ga, g_sa, g_bd, g_gf, g_sf)):
            for i in range(COLS):
                ref[i * 128 : i * 128 + 128] = vecs[i, j]

        def bias(ref):
            lane = lanes((CLASSES, 8, 128))
            for a in range(PIECES):
                tile = ref[index(0, a)][:, 0].astype(f32)
                rows = [jnp.where(lane == rt, tile, 0.0)[:, None] for rt in range(3)]
                column = jnp.concatenate(rows, axis=1)
                for q in range(CLASSES):
                    rs = slice(SUB * q + PIECE * a, SUB * q + PIECE * a + PIECE)
                    tall[rs, :] = column[q].reshape(PIECE, 128)
            g_bup[...] = dot_last(jnp.ones((8, 128), bf16), tall[...].astype(bf16))[0]

        @pl.when(core == 0)
        def _():
            bias(bias_own)

        @pl.when(core == 1)
        def _():
            bias(bias_oth)


def final(place, own, other, ffn_own, ffn_oth):
    tile = pl.BlockSpec((TALL_TILES, 8, 128), lambda i: (i, 0, 0))
    tall = pl.BlockSpec((768, 128), lambda i: (0, i))
    vec = pl.BlockSpec((WIDTH,), lambda i: (0,))
    units = pl.BlockSpec((8, CLASSES, 3, 8, 128), lambda i: (0, 0, i % 3, 0, 0))
    last = pl.BlockSpec((8, CLASSES, 1, 8, 128), lambda i: (0, 0, UNITS - 1, 0, 0))
    v = shape((WIDTH,), f32)
    return pl.pallas_call(
        final_kernel,
        grid=(COLS,),
        out_shape=(
            shape((768, 768), f32), v, shape((TAPS, 768), f32), shape((768, 768), f32), v, v, v,
            shape((768, 384), f32), shape((384,), f32), shape((384, 768), f32), v, v, v,
        ),
        in_specs=[
            SMEM, tile, tile,
            units, units, last, last,
        ],
        out_specs=(
            tall, vec, pl.BlockSpec((TAPS, 128), lambda i: (0, i)), tall, vec, vec, vec,
            pl.BlockSpec((128, 384), lambda i: (i, 0)), pl.BlockSpec((384,), lambda i: (0,)),
            pl.BlockSpec((384, 128), lambda i: (0, i)), vec, vec, vec,
        ),
        scratch_shapes=[pltpu.VMEM((COLS, 8, 128), f32), pltpu.VMEM((384, 128), f32)],
        compiler_params=params(32),
        name="final",
    )(place, own, other, ffn_own, ffn_oth, ffn_own, ffn_oth)


def body(
    block_input,
    w_value,
    b_value,
    conv_kernel,
    w_out,
    b_out,
    gain_attn,
    shift_attn,
    w_up,
    b_up,
    w_down,
    b_down,
    gain_ffn,
    shift_ffn,
    query_codes,
    key_codes,
    key_live,
    seq_lengths,
    out_grad,
):
    dp = lax.axis_index("dp")
    place = jnp.stack([dp, lax.axis_index("tensor")]).astype(i32)
    n_dp = lax.axis_size("dp")

    def shift(i, by):
        return i // 8 * 8 + (i // 2 + by) % 4 * 2 + i % 2

    def swap(x):
        return lax.ppermute(x, "dp", [(i, i ^ 1) for i in range(n_dp)])

    def ahead(x):
        return lax.ppermute(x, "dp", [(i, shift(i, 1)) for i in range(n_dp)])

    def behind(x):
        return lax.ppermute(x, "dp", [(i, shift(i, -1)) for i in range(n_dp)])

    def exchange(x):
        return lax.all_to_all(x, ALL, 0, 0, tiled=True)

    def row(v):
        return v.reshape(1, -1)

    def fetch(a, b):
        far_a, far_b = ahead(a), behind(b)
        return far_a, far_b, swap(jnp.concatenate([far_a, far_b], axis=0))

    def send_back(own, sib):
        a, b = combine(own, swap(sib))
        return behind(a), ahead(b)

    weights = exchange(prep(place, w_up, w_down, row(b_up)))
    weights = weights.reshape(2, PIECES, 2, 8, UNITS, 8, 128)
    (n1, inv1, low, low_a, low_b, ctx, collide, nrm, scl, wave, wavet, ks, vs, tapt, live) = attend(
        seq_lengths, block_input, w_value, row(b_value), conv_kernel, w_out, row(b_out),
        row(gain_attn), row(shift_attn), query_codes, key_codes, row(key_live),
    )
    low_sib = swap(low)
    row_a, row_b, row_sib = fetch(low_a, low_b)
    act_f, slope_f, far_own, far_sib, rows_f, wu, wd = ffn_call(
        ffn_far_kernel, True, row_a, row_b, row_sib, weights
    )
    act_n, slope_n, near_own, near_sib, rows_n = ffn_call(
        ffn_near_kernel, False, low, low_sib, wu, wd
    )
    back_a, back_b = send_back(far_own, far_sib)
    block_output, second, grad, grad_a, grad_b, sums = middle(
        n1, near_own, swap(near_sib), back_a, back_b, row(b_down), row(gain_attn), row(shift_attn),
        row(gain_ffn), row(shift_ffn), out_grad,
    )
    got_a, got_b, got_sib = fetch(grad_a, grad_b)
    near_own, near_sib, g_n, u_n, bias_n = back_call(
        back_near_kernel, "back_near", grad, swap(grad), wu, wd, slope_n
    )
    far_own, far_sib, g_f, u_f, bias_f = back_call(
        back_far_kernel, "back_far", got_a, got_b, got_sib, wu, wd, slope_f
    )
    grad_down = (dot_first(act_n, g_n) + dot_first(act_f, g_f)).astype(bf16)
    grad_up = (dot_first(u_n, rows_n) + dot_first(u_f, rows_f)).astype(bf16)
    grads = pack(grad_up, grad_down, bias_n, bias_f)
    back_a, back_b = send_back(far_own, far_sib)
    grads, back_a, back_b = lax.optimization_barrier((grads, back_a, back_b))
    owned = exchange(grads.reshape(128, UNITS, 8, 128))
    input_grad, keep, give = attend_back(
        place, near_own, swap(near_sib), back_a, back_b, second, n1, inv1, row(gain_attn), ctx,
        w_out, nrm, scl, wave, wavet, ks, vs, tapt, collide, live, block_input, w_value, sums,
    )
    pair = (keep + swap(give).astype(f32)).astype(bf16).reshape(128, PACK // 128, 8, 128)
    owned = sum_ffn(owned)
    pair, owned = lax.optimization_barrier((pair, owned))
    around = [owned]
    for side in range(2):
        for by in range(4):
            if side or by:
                pairs = [(i, (i // 8 + side) % 2 * 8 + shift(i % 8, by)) for i in range(n_dp)]
                around.append(lax.ppermute(owned, "dp", pairs))
    ffn_own = jnp.stack(around)
    back = exchange(sum_rest(exchange(pair))).reshape(PACK, 8, 128)
    (g_wv, g_bv, g_conv, g_wo, g_bo, g_ga, g_sa, g_up, g_bup, g_down, g_bd, g_gf, g_sf) = final(
        place, back, swap(back), ffn_own, swap(ffn_own)
    )
    return (
        block_output, input_grad, g_wv, g_bv, g_conv, g_wo, g_bo, g_ga, g_sa, g_up, g_bup, g_down,
        g_bd, g_gf, g_sf,
    )


def solution(mesh):
    rows = P(ALL, None)
    return jax.shard_map(
        body,
        mesh=mesh,
        in_specs=(
            rows, P(), P(), P(), P(), P(), P(), P(),
            P(None, "tensor"), P("tensor"), P("tensor", None), P(), P(), P(),
            rows, rows, P(ALL), rows, rows,
        ),
        out_specs=(
            rows, rows, P(), P(), P(), P(), P(), P(), P(),
            P(None, "tensor"), P("tensor"), P("tensor", None), P(), P(), P(),
        ),
        check_vma=False,
    )
```

```python
import math

import jax
import jax.numpy as jnp
from jax import lax
from jax.experimental import pallas as pl
from jax.experimental.pallas import tpu as pltpu
from jax.sharding import PartitionSpec as P

HEADS = 12
SETS = 32
ROWS = 256
WIDTH = 768
HEAD_DIM = 64
COLS = WIDTH // 128
TAPS = 65
MARGIN = 32
DFT_LEN = 384
FREQ = 256
LIVE_FREQ = DFT_LEN // 2 + 1
CLASSES = 4
SUB = 96
PIECE = 24
PIECES = SUB // PIECE
UNITS = 10
GRAD_UNITS = 9
HIDDEN = 768
HALF = ROWS // 2
TALL = 848
TALL_TILES = TALL // 8
PACK = 640
ALL = ("dp", "tensor")

bf16 = jnp.bfloat16
f32 = jnp.float32
i32 = jnp.int32

VMEM = pl.BlockSpec(memory_space=pltpu.VMEM)
SMEM = pl.BlockSpec(memory_space=pltpu.SMEM)
HBM = pl.BlockSpec(memory_space=pltpu.HBM)


def shape(dims, dtype):
    return jax.ShapeDtypeStruct(dims, dtype)


def params(mib):
    return pltpu.CompilerParams(vmem_limit_bytes=mib << 20)


def dot(a, b):
    return lax.dot_general(a, b, (((1,), (0,)), ((), ())), preferred_element_type=f32)


def dot_last(a, b):
    return lax.dot_general(a, b, (((1,), (1,)), ((), ())), preferred_element_type=f32)


def dot_first(a, b):
    return lax.dot_general(a, b, (((0,), (0,)), ((), ())), preferred_element_type=f32)


def lanes(dims):
    return lax.broadcasted_iota(i32, dims, len(dims) - 1)


def norm_rows(r):
    mean = jnp.mean(r, axis=-1, keepdims=True)
    centred = r - mean
    inv = lax.rsqrt(jnp.mean(centred * centred, axis=-1, keepdims=True) + 1e-05)
    return centred * inv, inv


def norm_back(g, n, inv, gain):
    e = g * gain
    return (
        e - jnp.mean(e, axis=-1, keepdims=True) - n * jnp.mean(e * n, axis=-1, keepdims=True)
    ) * inv


class Staged:
    def __init__(self, ref, buf, sem, incoming):
        pair = (ref, buf) if incoming else (buf, ref)
        self.buf = buf
        self.copy = pltpu.make_async_copy(*pair, sem)
        self.incoming = incoming
        self.pending = True
        if incoming:
            self.copy.start()

    def ready(self):
        if self.pending:
            self.copy.wait()
            self.pending = False

    def leave(self):
        if self.pending:
            self.copy.start()
            self.pending = False

    def __getitem__(self, index):
        if self.incoming:
            self.ready()
        return self.buf[index]

    def __setitem__(self, index, value):
        self.buf[index] = value


def staged_call(kernel, name, mib, ins, outs, scratch=()):
    spec = {"smem": SMEM, "vmem": VMEM, "hbm": HBM}
    arrays = [a for _, a in ins]
    kinds = [k for k, _ in ins] + [k for k, _ in outs]
    avals = arrays + [o for _, o in outs]
    staged = [i for i, k in enumerate(kinds) if k == "hbm"]
    n_in = len(ins)

    if not staged:
        return pl.pallas_call(
            kernel,
            out_shape=tuple(o for _, o in outs),
            in_specs=[spec[k] for k, _ in ins],
            out_specs=tuple(spec[k] for k, _ in outs),
            scratch_shapes=list(scratch),
            compiler_params=params(mib),
            name=name,
        )(*arrays)

    def run(*refs):
        refs = list(refs)
        sems = refs.pop()
        split = len(refs) - len(staged)
        bufs = refs[split:]
        refs = refs[:split]
        for n, i in enumerate(staged):
            refs[i] = Staged(refs[i], bufs[n], sems.at[n], i < n_in)
        kernel(*refs)
        for i in staged:
            if i < n_in:
                refs[i].ready()
            else:
                refs[i].leave()
        for i in staged:
            if i >= n_in:
                refs[i].copy.wait()

    buffers = [pltpu.VMEM(avals[i].shape, avals[i].dtype) for i in staged]
    arrays = [
        pltpu.with_memory_space_constraint(a, pltpu.HBM) if k == "hbm" else a for k, a in ins
    ]
    return pl.pallas_call(
        run,
        out_shape=tuple(pltpu.HBM(o.shape, o.dtype) if k == "hbm" else o for k, o in outs),
        in_specs=[spec[k] for k, _ in ins],
        out_specs=tuple(spec[k] for k, _ in outs),
        scratch_shapes=[*scratch, *buffers, pltpu.SemaphoreType.DMA((len(staged),))],
        compiler_params=params(mib),
        name=name,
    )(*arrays)


def prep_kernel(place, up_ref, down_ref, bias_ref, out_ref, up, down, tall, cols, block, sems):
    rep = place[0] % 8
    side = rep % 2

    @pl.when(place[0] < 8)
    def _():
        copy = pltpu.make_async_copy(up_ref, up, sems.at[0])
        copy.start()
        cols[...] = jnp.broadcast_to(bias_ref[...].astype(f32), (8, 384)).T
        copy.wait()
        tall[...] = up[...].astype(f32).T

    @pl.when(place[0] >= 8)
    def _():
        copy = pltpu.make_async_copy(down_ref, down, sems.at[0])
        copy.start()
        cols[...] = jnp.zeros(cols.shape, f32)
        copy.wait()
        tall[...] = down[...].astype(f32)

    for q in range(CLASSES):
        start = pl.multiple_of(SUB * q + PIECE * (rep // 2), 8)
        rows = tall[pl.ds(start, PIECE), :]
        piece = []
        for j in range(3):
            left = rows[:, j * 128 : j * 128 + 128]
            right = rows[:, 384 + j * 128 : 512 + j * 128]
            piece.append(jnp.where(side == 0, left, right).reshape(3, 8, 128).astype(bf16))
        bias = jnp.zeros((8, 128), f32)
        for rt in range(3):
            col = cols[pl.ds(pl.multiple_of(start + 8 * rt, 8), 8), :][:, 0:1]
            bias = jnp.where(lanes((8, 128)) == rt, jnp.broadcast_to(col, (8, 128)), bias)
        bias = jnp.where(side == 0, bias, 0.0).astype(bf16)
        for n in range(8):
            for j in range(3):
                block[q * 8 + n, 3 * j : 3 * j + 3] = piece[j]
            block[q * 8 + n, UNITS - 1] = bias
    copies = [
        pltpu.make_async_copy(block, out_ref.at[32 * i : 32 * i + 32], sems.at[1 + i])
        for i in range(4)
    ]
    for copy in copies:
        copy.start()
    for copy in copies:
        copy.wait()


def prep(place, w_up, w_down, b_up):
    return pl.pallas_call(
        prep_kernel,
        out_shape=pltpu.HBM((128, UNITS, 8, 128), bf16),
        in_specs=[SMEM, HBM, HBM, VMEM],
        out_specs=HBM,
        scratch_shapes=[
            pltpu.VMEM((768, 384), bf16),
            pltpu.VMEM((384, 768), bf16),
            pltpu.VMEM((384, 768), f32),
            pltpu.VMEM((384, 8), f32),
            pltpu.VMEM((32, UNITS, 8, 128), bf16),
            pltpu.SemaphoreType.DMA((5,)),
        ],
        compiler_params=params(16),
        name="prep",
    )(
        place,
        pltpu.with_memory_space_constraint(w_up, pltpu.HBM),
        pltpu.with_memory_space_constraint(w_down, pltpu.HBM),
        b_up,
    )


def segment_ends(len_ref):
    e0 = len_ref[0, 0]
    e1 = e0 + len_ref[0, 1]
    return e0, e1, e1 + len_ref[0, 2]


def segment_of(p, ends):
    return sum((p >= e).astype(i32) for e in ends)


def turn(product):
    r = product.astype(f32) * (1.0 / DFT_LEN)
    m = product - DFT_LEN * jnp.round(r).astype(i32)
    x = m.astype(f32) * (2.0 * math.pi / DFT_LEN)
    z = x * x
    c = 1.0
    s = 1.0
    for k in range(8, 0, -1):
        c = 1.0 - z * c * (1.0 / ((2 * k - 1) * (2 * k)))
        s = 1.0 - z * s * (1.0 / ((2 * k) * (2 * k + 1)))
    return c, x * s


def attend_kernel(
    len_ref, x_ref, wv_ref, bv_ref, taps_ref, wo_ref, bo_ref, ga_ref, sa_ref, q_ref, k_ref, live_ref,
    n_ref, inv_ref, low_ref, low_a, low_b, ctx_ref, col_ref, nrm_ref, scl_ref, wave_ref, wavet_ref, ks_ref, vs_ref,
    tapt_ref, live_out, qw, kb, jn, tapbuf, mix, mskd,
):
    ends = segment_ends(len_ref)
    square = (ROWS, ROWS)
    rows_i = lax.broadcasted_iota(i32, square, 0)
    lanes_i = lax.broadcasted_iota(i32, square, 1)
    jn[...] = jnp.where(segment_of(rows_i, ends) == segment_of(lanes_i, ends), 1.0 / SETS, 0.0)
    d = lax.broadcasted_iota(i32, (384, 128), 0) - 4 * lax.broadcasted_iota(i32, (384, 128), 1)
    w_lo = jnp.where(d == 0, 1.0, jnp.where(d == 1, 256.0, 0.0)).astype(bf16)
    w_hi = jnp.where(d == 2, 1.0, jnp.where(d == 3, 256.0, 0.0)).astype(bf16)
    q_codes = q_ref[...].astype(f32).astype(bf16)
    k_codes = k_ref[...].astype(f32).astype(bf16)
    qw[...] = dot(q_codes, w_lo).astype(i32) | (dot(q_codes, w_hi).astype(i32) << 16)
    kw = dot(k_codes, w_lo).T.astype(i32) | (dot(k_codes, w_hi).T.astype(i32) << 16)
    for r in range(96):
        for j in range(2):
            kb[r, j] = jnp.broadcast_to(kw[r : r + 1, j * 128 : j * 128 + 128], (8, 128))
    low7 = jnp.int32(0x7F7F7F7F)
    ones = jnp.int32(0x01010101)
    byte2 = jnp.int32(0x00FF00FF)
    tile_rows = 16
    groups = tile_rows // 8

    def tile(rt, carry):
        rs = pl.ds(pl.multiple_of(rt * tile_rows, tile_rows), tile_rows)
        qt = qw[rs, :]
        for h in range(HEADS):
            acc = [[jnp.zeros((8, 128), i32) for _ in range(2)] for _ in range(groups)]
            for g in range(8):
                c = h * 8 + g
                qc = [
                    jnp.broadcast_to(qt[t * 8 : t * 8 + 8, c : c + 1], (8, 128))
                    for t in range(groups)
                ]
                for j in range(2):
                    kk = kb[c, j]
                    for t in range(groups):
                        x = qc[t] ^ kk
                        y = ((x & low7) + low7) | x
                        acc[t][j] = acc[t][j] + (lax.shift_right_logical(y, 7) & ones)
            for j in range(2):
                parts = []
                for t in range(groups):
                    z = acc[t][j]
                    z = (z & byte2) + (lax.shift_right_logical(z, 8) & byte2)
                    z = (z & jnp.int32(0xFFFF)) + lax.shift_right_logical(z, 16)
                    parts.append((SETS - z).astype(f32))
                m = jnp.concatenate(parts, axis=0) * jn[rs, j * 128 : j * 128 + 128]
                col_ref[h, rs, j * 128 : j * 128 + 128] = m.astype(bf16)
        return carry

    lax.fori_loop(0, ROWS // tile_rows, tile, 0)

    col_ref.leave()

    dims = (FREQ, ROWS)
    f = lax.broadcasted_iota(i32, dims, 0)
    p = lax.broadcasted_iota(i32, dims, 1)
    c, s = turn(f * (p + MARGIN * segment_of(p, ends)))
    ok = f < LIVE_FREQ
    wave_ref[0:FREQ] = jnp.where(ok, c, 0.0).astype(bf16)
    wave_ref[FREQ:] = jnp.where(ok, s, 0.0).astype(bf16)
    p = lax.broadcasted_iota(i32, dims, 0)
    f = lax.broadcasted_iota(i32, dims, 1)
    c, s = turn(f * (p + MARGIN * segment_of(p, ends)))
    ok = f < LIVE_FREQ
    wavet_ref[:, 0:FREQ] = jnp.where(ok, c, 0.0).astype(bf16)
    wavet_ref[:, FREQ:] = jnp.where(ok, s, 0.0).astype(bf16)
    dims = (FREQ, 128)
    f = lax.broadcasted_iota(i32, dims, 0)
    c, s = turn(f * (lax.broadcasted_iota(i32, dims, 1) - MARGIN))
    tap_c = c.astype(bf16)
    tap_s = s.astype(bf16)
    dims = (128, FREQ)
    f = lax.broadcasted_iota(i32, dims, 1)
    c, s = turn(f * (lax.broadcasted_iota(i32, dims, 0) - MARGIN))
    tapt_ref[:, 0:FREQ] = c.astype(bf16)
    tapt_ref[:, FREQ:] = s.astype(bf16)
    tapbuf[...] = jnp.zeros(tapbuf.shape, f32)
    tapbuf[0:TAPS] = taps_ref[...].astype(f32)
    kernel = tapbuf[...].astype(bf16)
    f = lax.broadcasted_iota(i32, (FREQ, 1), 0)
    weight = jnp.where((f == 0) | (f == DFT_LEN // 2), 1.0 / DFT_LEN, 2.0 / DFT_LEN)
    weight = jnp.where(f < LIVE_FREQ, weight, 0.0)
    k_cos = dot(tap_c, kernel) * weight
    k_sin = dot(tap_s, kernel) * weight
    ks_ref[0:FREQ] = k_cos
    ks_ref[FREQ:] = k_sin

    live = jnp.broadcast_to(live_ref[...].astype(f32), (8, ROWS)).T[:, 0:1]
    live_out[...] = jnp.broadcast_to(live, (ROWS, 128))
    values = (dot(x_ref[...], wv_ref[...]) + bv_ref[...].astype(f32)).astype(bf16).astype(f32)
    mskd[...] = (values * live).astype(bf16)
    masked = mskd[...]
    spec = dot(wave_ref[...], masked)
    vs_ref[...] = spec.astype(bf16)
    v_cos = spec[0:FREQ]
    v_sin = spec[FREQ:]
    first_head = lanes((ROWS, 128)) < HEAD_DIM
    y_cos = (k_cos * v_cos + k_sin * v_sin).astype(bf16)
    y_sin = (k_cos * v_sin - k_sin * v_cos).astype(bf16)
    conv = dot(wavet_ref[:, 0:FREQ], y_cos) + dot(wavet_ref[:, FREQ:], y_sin)
    for done in (wave_ref, wavet_ref, tapt_ref, ks_ref, live_out, vs_ref):
        done.leave()

    def heads(b, carry):
        cs = pl.ds(pl.multiple_of(b * 128, 128), 128)
        block = mskd[:, cs]
        m = jnp.where(first_head, dot(col_ref[2 * b], block), dot(col_ref[2 * b + 1], block))
        sq = m * m
        one = jnp.sum(jnp.where(first_head, sq, 0.0), axis=1, keepdims=True)
        two = jnp.sum(jnp.where(first_head, 0.0, sq), axis=1, keepdims=True)
        scale = lax.rsqrt(jnp.where(first_head, one, two) * (1.0 / HEAD_DIM) + 1e-06)
        scl_ref[:, cs] = scale
        nrm = m * scale
        nrm_ref[:, cs] = nrm.astype(bf16)
        mix[:, cs] = nrm
        return carry

    lax.fori_loop(0, COLS, heads, 0)
    context = (mix[...] + conv).astype(bf16)
    ctx_ref[...] = context
    for done in (scl_ref, nrm_ref, ctx_ref):
        done.leave()
    attended = dot(context, wo_ref[...]) + bo_ref[...].astype(f32)
    n, inv = norm_rows(x_ref[...].astype(f32) + attended)
    n_ref[...] = n
    inv_ref[...] = jnp.broadcast_to(inv, (ROWS, 128))
    low = (n * ga_ref[...].astype(f32) + sa_ref[...].astype(f32)).astype(bf16)
    low_ref[...] = low
    low_a[...] = low[0:HALF]
    low_b[...] = low[HALF:]


def attend(seq_lengths, x, wv, bv, taps, wo, bo, ga, sa, q, k, live):
    wide = (ROWS, WIDTH)
    half = (HALF, WIDTH)
    h = "hbm"
    v = "vmem"
    return staged_call(
        attend_kernel, "attend", 36,
        [
            ("smem", seq_lengths), (h, x), (h, wv), (v, bv), (v, taps), (h, wo), (v, bo), (v, ga),
            (v, sa), (h, q), (h, k), (v, live),
        ],
        [
            (h, shape(wide, f32)), (h, shape((ROWS, 128), f32)), (v, shape(wide, bf16)),
            (v, shape(half, bf16)), (v, shape(half, bf16)), (h, shape(wide, bf16)),
            (h, shape((HEADS, ROWS, ROWS), bf16)), (h, shape(wide, bf16)), (h, shape(wide, f32)),
            (h, shape((2 * FREQ, ROWS), bf16)), (h, shape((ROWS, 2 * FREQ), bf16)),
            (h, shape((2 * FREQ, WIDTH), f32)), (h, shape((2 * FREQ, WIDTH), bf16)),
            (h, shape((128, 2 * FREQ), bf16)), (h, shape((ROWS, 128), f32)),
        ],
        [
            pltpu.VMEM((ROWS, 128), i32),
            pltpu.VMEM((96, 2, 8, 128), i32),
            pltpu.VMEM((ROWS, ROWS), f32),
            pltpu.VMEM((128, WIDTH), f32),
            pltpu.VMEM(wide, f32),
            pltpu.VMEM(wide, bf16),
        ],
    )


def unpack(ref, m, out):
    for a in range(PIECES):
        rs = slice(a * 192, a * 192 + 192)
        for ct in range(COLS):
            first = 3 * (ct % 3)
            part = ref[m, a, ct // 3, :, first : first + 3].astype(f32)
            out[rs, ct * 128 : ct * 128 + 128] = part.reshape(192, 128).astype(bf16)


def unpack_bias(ref, out):
    for a in range(PIECES):
        tile = ref[0, a, 0, :, UNITS - 1].astype(f32)
        lane = lanes(tile.shape)
        parts = [jnp.where(lane == rt, tile, 0.0)[:, None] for rt in range(3)]
        column = jnp.concatenate(parts, axis=1).reshape(192, 128)
        out[a * 192 : a * 192 + 192, WIDTH:] = column.astype(bf16)


def ffn_blocks(rows, wu, wd, act, slope, acc):
    acc[...] = jnp.zeros(acc.shape, f32)

    def block(i, carry):
        hs = pl.ds(pl.multiple_of(i * 256, 256), 256)
        upper = dot_last(rows[...], wu[hs, :])
        cdf = 0.5 * (1.0 + lax.erf(upper * math.sqrt(0.5)))
        a = (upper * cdf).astype(bf16)
        act[:, hs] = a
        density = jnp.exp(-0.5 * upper * upper) * (1.0 / math.sqrt(2.0 * math.pi))
        slope[:, hs] = (cdf + upper * density).astype(bf16)
        acc[...] += dot(a, wd[hs, :])
        return carry

    lax.fori_loop(0, HIDDEN // 256, block, 0)


def ffn_near_kernel(
    own, sib, w, act, slope, part_own, part_sib, rows_out, wu, wd, rows, acc,
):
    rows[0:ROWS, 0:WIDTH] = own[...]
    rows[ROWS:, 0:WIDTH] = sib[...]
    rows[:, WIDTH:] = jnp.where(lanes((2 * ROWS, 128)) < 3, 1.0, 0.0).astype(bf16)
    unpack(w, 0, wu)
    unpack_bias(w, wu)
    unpack(w, 1, wd)
    rows_out[...] = rows[:, 0:WIDTH]
    ffn_blocks(rows, wu, wd, act, slope, acc)
    part_own[...] = acc[0:ROWS]
    part_sib[...] = acc[ROWS:].astype(bf16)


def ffn_far_kernel(
    got_a, got_b, sib_a, sib_b, wu, wd, act, slope, part_own, part_sib, rows_out, rows, acc,
):
    for i, ref in enumerate((got_a, got_b, sib_a, sib_b)):
        rows[i * HALF : i * HALF + HALF, 0:WIDTH] = ref[...]
    rows[:, WIDTH:] = jnp.where(lanes((2 * ROWS, 128)) < 3, 1.0, 0.0).astype(bf16)
    rows_out[...] = rows[:, 0:WIDTH]
    ffn_blocks(rows, wu, wd, act, slope, acc)
    part_own[...] = acc[0:ROWS]
    part_sib[...] = acc[ROWS:].astype(bf16)


def ffn_call(kernel, name, ins, outs):
    wide = (ROWS, WIDTH)
    tall = shape((2 * ROWS, WIDTH), bf16)
    return staged_call(
        kernel, name, 24, ins,
        [("vmem", o) for o in (tall, tall, shape(wide, f32), shape(wide, bf16), tall, *outs)],
        [pltpu.VMEM((2 * ROWS, WIDTH + 128), bf16), pltpu.VMEM((2 * ROWS, WIDTH), f32)],
    )


def ffn_near(own, sib, weights):
    return ffn_call(
        ffn_near_kernel, "ffn_near", [("vmem", own), ("vmem", sib), ("hbm", weights)],
        [shape((HIDDEN, WIDTH + 128), bf16), shape((HIDDEN, WIDTH), bf16)],
    )


def ffn_far(*args):
    return ffn_call(ffn_far_kernel, "ffn_far", [("vmem", a) for a in args], [])


def combine_kernel(own, got, out_a, out_b):
    total = (own[...] + got[...].astype(f32)).astype(bf16)
    out_a[...] = total[0:HALF]
    out_b[...] = total[HALF:]


def combine(own, got):
    half = shape((HALF, WIDTH), bf16)
    return pl.pallas_call(
        combine_kernel,
        out_shape=(half, half),
        in_specs=[VMEM] * 2,
        out_specs=(VMEM,) * 2,
        compiler_params=params(32),
        name="combine",
    )(own, got)


def gather_rows(own, near, far_a, far_b):
    far = jnp.concatenate([far_a[...], far_b[...]], axis=0)
    return own[...] + near[...].astype(f32) + far.astype(f32)


def middle_kernel(
    n1, own, near, far_a, far_b, bd, ga, sa, gf, sf, og, out, second, low, low_a, low_b, sums,
):
    first = n1[...] * ga[...].astype(f32) + sa[...].astype(f32)
    n, inv = norm_rows(first + gather_rows(own, near, far_a, far_b) + bd[...].astype(f32))
    gain = gf[...].astype(f32)
    out[...] = (n * gain + sf[...].astype(f32)).astype(bf16)
    g = og[...].astype(f32)
    grad = norm_back(g, n, inv, gain)
    second[...] = grad
    grad_low = grad.astype(bf16)
    low[...] = grad_low
    low_a[...] = grad_low[0:HALF]
    low_b[...] = grad_low[HALF:]
    sums[0:1] = jnp.sum(grad_low.astype(f32), axis=0, keepdims=True)
    sums[1:2] = jnp.sum(g * n, axis=0, keepdims=True)
    sums[2:3] = jnp.sum(g, axis=0, keepdims=True)
    sums[3:8] = jnp.zeros((5, WIDTH), f32)


def middle(*args):
    wide = (ROWS, WIDTH)
    half = (HALF, WIDTH)
    return staged_call(
        middle_kernel, "middle", 16, [("vmem", a) for a in args],
        [
            ("hbm", shape(wide, bf16)), ("hbm", shape(wide, f32)), ("vmem", shape(wide, bf16)),
            ("vmem", shape(half, bf16)), ("vmem", shape(half, bf16)), ("hbm", shape((8, WIDTH), f32)),
        ],
    )


def back_blocks(g, wu, wd, slope, u_out, bias, acc):
    acc[...] = jnp.zeros(acc.shape, f32)
    bias[...] = jnp.zeros((8, HIDDEN), f32)

    def block(i, carry):
        hs = pl.ds(pl.multiple_of(i * 256, 256), 256)
        u = (dot_last(g[...], wd[hs, :]) * slope[:, hs].astype(f32)).astype(bf16)
        u_out[:, hs] = u
        bias[0:1, hs] = jnp.sum(u.astype(f32), axis=0, keepdims=True)
        acc[...] += dot(u, wu[hs, 0:WIDTH])
        return carry

    lax.fori_loop(0, HIDDEN // 256, block, 0)


def back_near_kernel(own, sib, wu, wd, slope, first_own, first_sib, g, u, bias, acc):
    g[0:ROWS] = own[...]
    g[ROWS:] = sib[...]
    back_blocks(g, wu, wd, slope, u, bias, acc)
    first_own[...] = acc[0:ROWS]
    first_sib[...] = acc[ROWS:].astype(bf16)


def back_far_kernel(
    got_a, got_b, sib_a, sib_b, wu, wd, slope, first_own, first_sib, g, u, bias, acc,
):
    for i, ref in enumerate((got_a, got_b, sib_a, sib_b)):
        g[i * HALF : i * HALF + HALF] = ref[...]
    back_blocks(g, wu, wd, slope, u, bias, acc)
    first_own[...] = acc[0:ROWS]
    first_sib[...] = acc[ROWS:].astype(bf16)


def back_call(kernel, name, *args):
    wide = (ROWS, WIDTH)
    tall = shape((2 * ROWS, WIDTH), bf16)
    return staged_call(
        kernel, name, 20, [("vmem", a) for a in args],
        [
            ("hbm" if name == "back_near" else "vmem", shape(wide, f32)), ("vmem", shape(wide, bf16)),
            ("vmem", tall), ("vmem", tall), ("hbm", shape((8, HIDDEN), f32)),
        ],
        [pltpu.VMEM((2 * ROWS, WIDTH), f32)],
    )


def pack_kernel(gu, gd, grads):
    for a in range(PIECES):
        rs = slice(a * 192, a * 192 + 192)
        for ct in range(COLS):
            cs = slice(ct * 128, ct * 128 + 128)
            us = slice(3 * (ct % 3), 3 * (ct % 3) + 3)
            up = gu[rs, cs].astype(f32).reshape(8, 3, 8, 128)
            down = gd[rs, cs].astype(f32).reshape(8, 3, 8, 128)
            grads[0, a, ct // 3, :, us] = up.astype(bf16)
            grads[1, a, ct // 3, :, us] = down.astype(bf16)


def pack(*args):
    return staged_call(
        pack_kernel, "pack", 12, [("vmem", a) for a in args],
        [("hbm", shape((2, PIECES, 2, 8, GRAD_UNITS, 8, 128), bf16))],
    )[0]


def back_kernel(
    place, own, near, far_a, far_b, second, n1, inv1, ga, ctx, wo, nrm, scl, wave, wavet, ks, vs, tapt, col, live, x,
    wv, sums, bias_n, bias_f, in_grad, keep, give, buf_a, buf_b, mb,
):
    first_grad = second[...] + gather_rows(own, near, far_a, far_b)
    n = n1[...]
    buf_a[768 + 2 : 768 + 3] = jnp.sum(first_grad * n, axis=0, keepdims=True)
    buf_a[768 + 3 : 768 + 4] = jnp.sum(first_grad, axis=0, keepdims=True)
    resid = norm_back(first_grad, n, inv1[...][:, 0:1], ga[...].astype(f32))
    ag = resid.astype(bf16)
    buf_a[768 + 1 : 768 + 2] = jnp.sum(ag.astype(f32), axis=0, keepdims=True)
    buf_a[768 + 4 : 768 + 7] = sums[0:3]
    buf_a[768 + 7 :] = jnp.zeros((TALL - 775, WIDTH), f32)
    mine = lax.broadcasted_iota(i32, (8, WIDTH), 0) == place[0] % CLASSES
    bias = jnp.broadcast_to(bias_n[0:1] + bias_f[0:1], (8, WIDTH))
    buf_a[776:784] = jnp.where(mine, bias, 0.0)
    buf_b[0:768] = dot_first(ctx[...], ag)
    cg = dot_last(ag, wo[...])
    mb[...] = cg
    first_head = lanes((ROWS, 128)) < HEAD_DIM
    nrm.ready()
    scl.ready()
    col.ready()

    def heads(b, carry):
        cs = pl.ds(pl.multiple_of(b * 128, 128), 128)
        c = mb[:, cs]
        m = nrm[:, cs].astype(f32)
        prod = c * m
        one = jnp.sum(jnp.where(first_head, prod, 0.0), axis=1, keepdims=True)
        two = jnp.sum(jnp.where(first_head, 0.0, prod), axis=1, keepdims=True)
        mean = jnp.where(first_head, one, two) * (1.0 / HEAD_DIM)
        block = (scl[:, cs] * (c - m * mean)).astype(bf16)
        mb[:, cs] = jnp.where(
            first_head, dot_first(col[2 * b], block), dot_first(col[2 * b + 1], block)
        )
        return carry

    lax.fori_loop(0, COLS, heads, 0)
    spec = dot(wave[...], cg.astype(bf16))
    g_cos = spec[0:FREQ]
    g_sin = spec[FREQ:]
    k_cos = ks[0:FREQ]
    k_sin = ks[FREQ:]
    z_cos = (k_cos * g_cos - k_sin * g_sin).astype(bf16)
    z_sin = (k_cos * g_sin + k_sin * g_cos).astype(bf16)
    conv = dot(wavet[:, 0:FREQ], z_cos) + dot(wavet[:, FREQ:], z_sin)
    v_cos = vs[0:FREQ].astype(f32)
    v_sin = vs[FREQ:].astype(f32)
    f = lax.broadcasted_iota(i32, (FREQ, 1), 0)
    weight = jnp.where((f == 0) | (f == DFT_LEN // 2), 1.0 / DFT_LEN, 2.0 / DFT_LEN)
    weight = jnp.where(f < LIVE_FREQ, weight, 0.0)
    re = ((g_cos * v_cos + g_sin * v_sin) * weight).astype(bf16)
    im = ((g_cos * v_sin - g_sin * v_cos) * weight).astype(bf16)
    gk = dot(tapt[:, 0:FREQ], re) + dot(tapt[:, FREQ:], im)
    buf_b[768:] = jnp.zeros((TALL - 768, WIDTH), f32)
    buf_b[768 : 768 + TAPS] = gk[0:TAPS]
    vg = ((mb[...] + conv) * live[...][:, 0:1]).astype(bf16)
    buf_a[768:769] = jnp.sum(vg.astype(f32), axis=0, keepdims=True)
    buf_a[0:768] = dot_first(x[...], vg)
    in_grad[...] = resid + dot_last(vg, wv[...])

    def write(kept, given):
        for ct in range(COLS):
            cs = slice(ct * 128, ct * 128 + 128)
            ts = slice(ct * TALL_TILES, ct * TALL_TILES + TALL_TILES)
            keep[ts] = kept[:, cs].reshape(TALL_TILES, 8, 128).astype(bf16)
            give[ts] = given[:, cs].reshape(TALL_TILES, 8, 128).astype(bf16)

    rest = PACK - COLS * TALL_TILES
    keep[PACK - rest :] = jnp.zeros((rest, 8, 128), bf16)
    give[PACK - rest :] = jnp.zeros((rest, 8, 128), bf16)

    @pl.when(place[0] % 2 == 0)
    def _():
        write(buf_a, buf_b)

    @pl.when(place[0] % 2 == 1)
    def _():
        write(buf_b, buf_a)


def attend_back(*args):
    wide = (ROWS, WIDTH)
    packed = shape((PACK, 8, 128), bf16)
    kinds = ["smem"] + ["hbm"] * (len(args) - 1)
    for i in (2, 3, 4, 8):
        kinds[i] = "vmem"
    return staged_call(
        back_kernel, "attend_back", 40, list(zip(kinds, args, strict=True)),
        [("hbm", shape(wide, f32)), ("vmem", packed), ("vmem", packed)],
        [
            pltpu.VMEM((TALL, WIDTH), f32),
            pltpu.VMEM((TALL, WIDTH), f32),
            pltpu.VMEM(wide, f32),
        ],
    )


def sum_ffn_kernel(got, out, acc):
    step = pl.program_id(0)

    @pl.when(step == 0)
    def _():
        acc[...] = jnp.zeros(acc.shape, f32)

    for q in range(CLASSES):
        total = acc[q]
        for t in range(8):
            total = total + got[q * 8 + t].astype(f32)
        acc[q] = total

    @pl.when(step == 3)
    def _():
        out[...] = acc[...].astype(bf16)


def sum_ffn(got):
    return pl.pallas_call(
        sum_ffn_kernel,
        grid=(4,),
        out_shape=shape((CLASSES, GRAD_UNITS, 8, 128), bf16),
        in_specs=[pl.BlockSpec((32, GRAD_UNITS, 8, 128), lambda i: (i, 0, 0, 0))],
        out_specs=pl.BlockSpec((CLASSES, GRAD_UNITS, 8, 128), lambda i: (0, 0, 0, 0)),
        scratch_shapes=[pltpu.VMEM((CLASSES, GRAD_UNITS, 8, 128), f32)],
        compiler_params=params(32),
        name="sum_ffn",
    )(got)


def sum_rest_kernel(got, out):
    per = PACK // 128
    total = [jnp.zeros((per, 8, 128), f32) for _ in range(2)]
    for i in range(8):
        for c in range(2):
            for t in range(8):
                total[c] = total[c] + got[i * 16 + c * 8 + t].astype(f32)
    low = [t.astype(bf16) for t in total]
    for i in range(8):
        for c in range(2):
            for t in range(8):
                out[i * 16 + c * 8 + t] = low[c]


def sum_rest(got):
    return pl.pallas_call(
        sum_rest_kernel,
        out_shape=shape(got.shape, bf16),
        in_specs=[VMEM],
        out_specs=VMEM,
        compiler_params=params(32),
        name="sum_rest",
    )(got)


def final_ffn_kernel(place, ffn_own, ffn_oth, g_up, g_down, tall):
    ct = pl.program_id(0)
    core = place[0] % 2

    def index(m, a):
        return (place[0] // 2 % 4 + 4 - a) % 4 * 2 + (m + place[0] // 8) % 2

    def spread(ref):
        for a in range(PIECES):
            up = ref[index(0, a)].astype(f32)
            down = ref[index(1, a)].astype(f32)
            for q in range(CLASSES):
                rs = slice(SUB * q + PIECE * a, SUB * q + PIECE * a + PIECE)
                tall[rs, :] = up[q].reshape(PIECE, 128)
                g_down[rs, :] = down[q].reshape(PIECE, 128)

    @pl.when(ct // 3 == core)
    def _():
        spread(ffn_own)

    @pl.when(ct // 3 != core)
    def _():
        spread(ffn_oth)

    g_up[...] = tall[...].T


def final_ffn(place, ffn_own, ffn_oth):
    units = pl.BlockSpec((8, CLASSES, 3, 8, 128), lambda i: (0, 0, i % 3, 0, 0))
    return pl.pallas_call(
        final_ffn_kernel,
        grid=(COLS,),
        out_shape=(shape((768, 384), f32), shape((384, 768), f32)),
        in_specs=[SMEM, units, units],
        out_specs=(
            pl.BlockSpec((128, 384), lambda i: (i, 0)),
            pl.BlockSpec((384, 128), lambda i: (0, i)),
        ),
        scratch_shapes=[pltpu.VMEM((384, 128), f32)],
        compiler_params=params(16),
        name="final_ffn",
    )(place, ffn_own, ffn_oth)


def final_kernel(
    place, own, other, g_wv, g_bv, g_conv, g_wo, g_bo, g_ga, g_sa, g_bup, g_bd, g_gf, g_sf, vecs,
    bias, line,
):
    ct = pl.program_id(0)

    def write(a, b):
        g_wv[...] = a[0:96].astype(f32).reshape(768, 128)
        vecs[ct] = a[96].astype(f32)
        bias[ct] = a[97].astype(f32)
        g_wo[...] = b[0:96].astype(f32).reshape(768, 128)
        g_conv[...] = b[96:105].astype(f32).reshape(72, 128)[0:TAPS]

    @pl.when(place[0] % 2 == 0)
    def _():
        write(own, other)

    @pl.when(place[0] % 2 == 1)
    def _():
        write(other, own)

    @pl.when(ct == COLS - 1)
    def _():
        for j, ref in enumerate((g_bv, g_bo, g_ga, g_sa, g_bd, g_gf, g_sf)):
            for i in range(COLS):
                ref[i * 128 : i * 128 + 128] = vecs[i, j]
        n = lanes((128, 128))
        a = (n >= PIECE).astype(i32) + (n >= 2 * PIECE).astype(i32) + (n >= 3 * PIECE).astype(i32)
        at = (8 * a + place[1]) * PIECE + n - PIECE * a
        total = jnp.zeros((8, 128), f32)
        for i in range(COLS):
            pick = lax.broadcasted_iota(i32, (128, 128), 0) + 128 * i == at
            total = total + dot(bias[i].astype(bf16), jnp.where(pick, 1.0, 0.0).astype(bf16))
        for q in range(CLASSES):
            line[0:1, SUB * q : SUB * q + SUB] = total[q : q + 1, 0:SUB]
        g_bup[...] = line[...][0]


def final(place, own, other):
    tile = pl.BlockSpec((TALL_TILES, 8, 128), lambda i: (i, 0, 0))
    tall = pl.BlockSpec((768, 128), lambda i: (0, i))
    vec = pl.BlockSpec((WIDTH,), lambda i: (0,))
    v = shape((WIDTH,), f32)
    return pl.pallas_call(
        final_kernel,
        grid=(COLS,),
        out_shape=(
            shape((768, 768), f32), v, shape((TAPS, 768), f32), shape((768, 768), f32), v, v, v,
            shape((384,), f32), v, v, v,
        ),
        in_specs=[SMEM, tile, tile],
        out_specs=(
            tall, vec, pl.BlockSpec((TAPS, 128), lambda i: (0, i)), tall, vec, vec, vec,
            pl.BlockSpec((384,), lambda i: (0,)), vec, vec, vec,
        ),
        scratch_shapes=[
            pltpu.VMEM((COLS, 8, 128), f32),
            pltpu.VMEM((COLS, 8, 128), f32),
            pltpu.VMEM((1, 384), f32),
        ],
        compiler_params=params(16),
        name="final",
    )(place, own, other)


def body(
    block_input,
    w_value,
    b_value,
    conv_kernel,
    w_out,
    b_out,
    gain_attn,
    shift_attn,
    w_up,
    b_up,
    w_down,
    b_down,
    gain_ffn,
    shift_ffn,
    query_codes,
    key_codes,
    key_live,
    seq_lengths,
    out_grad,
):
    dp = lax.axis_index("dp")
    place = jnp.stack([dp, lax.axis_index("tensor")]).astype(i32)
    n_dp = lax.axis_size("dp")

    def shift(i, by):
        return i // 8 * 8 + (i // 2 + by) % 4 * 2 + i % 2

    def swap(x):
        return lax.ppermute(x, "dp", [(i, i ^ 1) for i in range(n_dp)])

    def ahead(x):
        return lax.ppermute(x, "dp", [(i, shift(i, 1)) for i in range(n_dp)])

    def behind(x):
        return lax.ppermute(x, "dp", [(i, shift(i, -1)) for i in range(n_dp)])

    def exchange(x):
        return lax.all_to_all(x, ALL, 0, 0, tiled=True)

    def row(v):
        return v.reshape(1, -1)

    weights = exchange(prep(place, w_up, w_down, row(b_up)))
    weights = weights.reshape(2, PIECES, 2, 8, UNITS, 8, 128)
    (n1, inv1, low, low_a, low_b, ctx, collide, nrm, scl, wave, wavet, ks, vs, tapt, live) = attend(
        seq_lengths, block_input, w_value, row(b_value), conv_kernel, w_out, row(b_out),
        row(gain_attn), row(shift_attn), query_codes, key_codes, row(key_live),
    )
    low_sib = swap(low)
    row_a, row_b = ahead(low_a), behind(low_b)
    act_n, slope_n, near_own, near_sib, rows_n, wu, wd = ffn_near(low, low_sib, weights)
    act_f, slope_f, far_own, far_sib, rows_f = ffn_far(
        row_a, row_b, swap(row_a), swap(row_b), wu, wd
    )
    sent_a, sent_b = combine(far_own, swap(far_sib))
    block_output, second, grad, grad_a, grad_b, sums = middle(
        n1, near_own, swap(near_sib), behind(sent_a), ahead(sent_b), row(b_down), row(gain_attn),
        row(shift_attn), row(gain_ffn), row(shift_ffn), out_grad,
    )
    got_a, got_b = ahead(grad_a), behind(grad_b)
    near_own, near_sib, g_n, u_n, bias_n = back_call(
        back_near_kernel, "back_near", grad, swap(grad), wu, wd, slope_n
    )
    got_a, got_b, near_sib = lax.optimization_barrier((got_a, got_b, near_sib))
    far_own, far_sib, g_f, u_f, bias_f = back_call(
        back_far_kernel, "back_far", got_a, got_b, swap(got_a), swap(got_b), wu, wd, slope_f
    )
    sent_a, sent_b = combine(far_own, swap(far_sib))
    u_f, sent_a, sent_b = lax.optimization_barrier((u_f, sent_a, sent_b))
    grad_down = (dot_first(act_n, g_n) + dot_first(act_f, g_f)).astype(bf16)
    grad_up = (dot_first(u_n, rows_n) + dot_first(u_f, rows_f)).astype(bf16)
    grads = pack(grad_up, grad_down)
    back_a, back_b = behind(sent_a), ahead(sent_b)
    grads, back_a, back_b = lax.optimization_barrier((grads, back_a, back_b))
    owned = exchange(grads.reshape(128, GRAD_UNITS, 8, 128))
    input_grad, keep, give = attend_back(
        place, near_own, swap(near_sib), back_a, back_b, second, n1, inv1,
        row(gain_attn), ctx, w_out, nrm, scl, wave, wavet, ks, vs, tapt, collide, live, block_input,
        w_value, sums, bias_n, bias_f,
    )
    pair = (keep.astype(f32) + swap(give).astype(f32)).astype(bf16)
    pair = pair.reshape(128, PACK // 128, 8, 128)
    owned = sum_ffn(owned)
    pair, owned = lax.optimization_barrier((pair, owned))
    two = jnp.stack([owned, lax.ppermute(owned, "dp", [(i, (i + 8) % 16) for i in range(n_dp)])])
    summed = sum_rest(exchange(pair))
    summed, two = lax.optimization_barrier((summed, two))
    opposite = lax.ppermute(two, "dp", [(i, shift(i, 2)) for i in range(n_dp)])
    ffn_own = jnp.stack([two, ahead(two), opposite, behind(two)])
    back = exchange(summed).reshape(PACK, 8, 128)
    back, ffn_own = lax.optimization_barrier((back, ffn_own))
    ffn_own = ffn_own.reshape(8, CLASSES, GRAD_UNITS, 8, 128)
    g_up, g_down = final_ffn(place, ffn_own, swap(ffn_own))
    g_wv, g_bv, g_conv, g_wo, g_bo, g_ga, g_sa, g_bup, g_bd, g_gf, g_sf = final(
        place, back, swap(back)
    )
    return (
        block_output, input_grad, g_wv, g_bv, g_conv, g_wo, g_bo, g_ga, g_sa, g_up, g_bup, g_down,
        g_bd, g_gf, g_sf,
    )


def solution(mesh):
    rows = P(ALL, None)
    return jax.shard_map(
        body,
        mesh=mesh,
        in_specs=(
            rows, P(), P(), P(), P(), P(), P(), P(),
            P(None, "tensor"), P("tensor"), P("tensor", None), P(), P(), P(),
            rows, rows, P(ALL), rows, rows,
        ),
        out_specs=(
            rows, rows, P(), P(), P(), P(), P(), P(), P(),
            P(None, "tensor"), P("tensor"), P("tensor", None), P(), P(), P(),
        ),
        check_vma=False,
    )
```

```python
import math

import jax
import jax.numpy as jnp
from jax import lax
from jax.experimental import pallas as pl
from jax.experimental.pallas import tpu as pltpu
from jax.sharding import PartitionSpec as P

HEADS = 12
SETS = 32
ROWS = 256
WIDTH = 768
HEAD_DIM = 64
COLS = WIDTH // 128
TAPS = 65
MARGIN = 32
DFT_LEN = 384
FREQ = 256
LIVE_FREQ = DFT_LEN // 2 + 1
CLASSES = 4
SUB = 96
PIECE = 24
PIECES = SUB // PIECE
UNITS = 10
GRAD_UNITS = 9
HIDDEN = 768
HALF = ROWS // 2
TALL = 848
TALL_TILES = TALL // 8
PACK = 640
ALL = ("dp", "tensor")

bf16 = jnp.bfloat16
f32 = jnp.float32
i32 = jnp.int32

VMEM = pl.BlockSpec(memory_space=pltpu.VMEM)
SMEM = pl.BlockSpec(memory_space=pltpu.SMEM)
HBM = pl.BlockSpec(memory_space=pltpu.HBM)


def shape(dims, dtype):
    return jax.ShapeDtypeStruct(dims, dtype)


def params(mib):
    return pltpu.CompilerParams(vmem_limit_bytes=mib << 20)


def dot(a, b):
    return lax.dot_general(a, b, (((1,), (0,)), ((), ())), preferred_element_type=f32)


def dot_last(a, b):
    return lax.dot_general(a, b, (((1,), (1,)), ((), ())), preferred_element_type=f32)


def dot_first(a, b):
    return lax.dot_general(a, b, (((0,), (0,)), ((), ())), preferred_element_type=f32)


def lanes(dims):
    return lax.broadcasted_iota(i32, dims, len(dims) - 1)


def norm_rows(r):
    mean = jnp.mean(r, axis=-1, keepdims=True)
    centred = r - mean
    inv = lax.rsqrt(jnp.mean(centred * centred, axis=-1, keepdims=True) + 1e-05)
    return centred * inv, inv


def norm_back(g, n, inv, gain):
    e = g * gain
    return (
        e - jnp.mean(e, axis=-1, keepdims=True) - n * jnp.mean(e * n, axis=-1, keepdims=True)
    ) * inv


class Staged:
    def __init__(self, ref, buf, sem, incoming):
        pair = (ref, buf) if incoming else (buf, ref)
        self.buf = buf
        self.copy = pltpu.make_async_copy(*pair, sem)
        self.incoming = incoming
        self.pending = True
        if incoming:
            self.copy.start()

    def ready(self):
        if self.pending:
            self.copy.wait()
            self.pending = False

    def leave(self):
        if self.pending:
            self.copy.start()
            self.pending = False

    def __getitem__(self, index):
        if self.incoming:
            self.ready()
        return self.buf[index]

    def __setitem__(self, index, value):
        self.buf[index] = value


class StagedPair:
    def __init__(self, ref, buf, sems):
        self.buf = buf
        self.copies = [pltpu.make_async_copy(ref.at[i], buf.at[i], sems.at[i]) for i in range(2)]
        self.pending = [True, True]
        for copy in self.copies:
            copy.start()

    def ready(self):
        for i in range(2):
            if self.pending[i]:
                self.copies[i].wait()
                self.pending[i] = False

    def __getitem__(self, index):
        i = index[0]
        if self.pending[i]:
            self.copies[i].wait()
            self.pending[i] = False
        return self.buf[index]


def staged_call(kernel, name, mib, ins, outs, scratch=()):
    spec = {"smem": SMEM, "vmem": VMEM, "hbm": HBM, "pair": HBM}
    arrays = [a for _, a in ins]
    kinds = [k for k, _ in ins] + [k for k, _ in outs]
    avals = arrays + [o for _, o in outs]
    staged = [i for i, k in enumerate(kinds) if k in ("hbm", "pair")]
    n_in = len(ins)

    if not staged:
        return pl.pallas_call(
            kernel,
            out_shape=tuple(o for _, o in outs),
            in_specs=[spec[k] for k, _ in ins],
            out_specs=tuple(spec[k] for k, _ in outs),
            scratch_shapes=list(scratch),
            compiler_params=params(mib),
            name=name,
        )(*arrays)

    def run(*refs):
        refs = list(refs)
        sems = refs.pop()
        split = len(refs) - len(staged)
        bufs = refs[split:]
        refs = refs[:split]
        for n, i in enumerate(staged):
            if kinds[i] == "pair":
                refs[i] = StagedPair(refs[i], bufs[n], sems.at[n])
            else:
                refs[i] = Staged(refs[i], bufs[n], sems.at[n, 0], i < n_in)
        kernel(*refs)
        for i in staged:
            if i < n_in:
                refs[i].ready()
            else:
                refs[i].leave()
        for i in staged:
            if i >= n_in:
                refs[i].copy.wait()

    buffers = [pltpu.VMEM(avals[i].shape, avals[i].dtype) for i in staged]
    arrays = [
        a if k in ("smem", "vmem") else pltpu.with_memory_space_constraint(a, pltpu.HBM)
        for k, a in ins
    ]
    return pl.pallas_call(
        run,
        out_shape=tuple(pltpu.HBM(o.shape, o.dtype) if k == "hbm" else o for k, o in outs),
        in_specs=[spec[k] for k, _ in ins],
        out_specs=tuple(spec[k] for k, _ in outs),
        scratch_shapes=[*scratch, *buffers, pltpu.SemaphoreType.DMA((len(staged), 2))],
        compiler_params=params(mib),
        name=name,
    )(*arrays)


def prep_kernel(place, up_ref, down_ref, bias_hbm, out_ref, half, piece, bias_ref, sems):
    rep = place[0] % 8
    is_up = place[0] < 8
    at = pl.ds(pl.multiple_of(rep % 2 * 384, 128), 384)
    up = pltpu.make_async_copy(up_ref.at[at, :], half, sems.at[0])
    down = pltpu.make_async_copy(down_ref.at[:, at], half, sems.at[0])
    bias_copy = pltpu.make_async_copy(bias_hbm, bias_ref, sems.at[33])
    bias_copy.start()

    @pl.when(is_up)
    def _():
        up.start()

    @pl.when(jnp.logical_not(is_up))
    def _():
        down.start()

    n = lax.broadcasted_iota(i32, (SUB, 384), 0)
    q = sum((n >= PIECE * k).astype(i32) for k in range(1, CLASSES))
    unit = (SUB - PIECE) * q + n + PIECE * (rep // 2)
    pick = jnp.where(unit == lanes((SUB, 384)), 1.0, 0.0).astype(bf16)
    scale = jnp.where(is_up & (rep % 2 == 0), 1.0, 0.0)
    bias_copy.wait()
    bias = jnp.broadcast_to(bias_ref[...].astype(f32) * scale, (16, 384)).astype(bf16)
    column = dot_last(pick, bias)[:, 0:1]

    def fill(rows):
        for k in range(CLASSES):
            rs = slice(PIECE * k, PIECE * k + PIECE)
            for j in range(3):
                part = rows[rs, j * 128 : j * 128 + 128].reshape(3, 8, 128)
                piece[k, 3 * j : 3 * j + 3] = part.astype(bf16)
            col = jnp.broadcast_to(column[rs], (PIECE, 128)).reshape(3, 8, 128)
            lane = lanes((8, 128))
            tile = jnp.where(lane == 0, col[0], jnp.where(lane == 1, col[1], col[2]))
            piece[k, UNITS - 1] = tile.astype(bf16)

    @pl.when(is_up)
    def _():
        up.wait()
        fill(dot_last(pick, half[...]))

    @pl.when(jnp.logical_not(is_up))
    def _():
        down.wait()
        fill(dot(pick, half[...]))

    copies = [
        pltpu.make_async_copy(piece, out_ref.at[g, :, t], sems.at[1 + 8 * g + t])
        for g in range(4)
        for t in range(8)
    ]
    for copy in copies:
        copy.start()
    for copy in copies:
        copy.wait()


def prep(place, w_up, w_down, b_up):
    out = pl.pallas_call(
        prep_kernel,
        out_shape=pltpu.HBM((4, CLASSES, 8, UNITS, 8, 128), bf16),
        in_specs=[SMEM, HBM, HBM, HBM],
        out_specs=HBM,
        scratch_shapes=[
            pltpu.VMEM((384, 384), bf16),
            pltpu.VMEM((CLASSES, UNITS, 8, 128), bf16),
            pltpu.VMEM((384,), bf16),
            pltpu.SemaphoreType.DMA((34,)),
        ],
        compiler_params=params(16),
        name="prep",
    )(
        place,
        pltpu.with_memory_space_constraint(w_up, pltpu.HBM),
        pltpu.with_memory_space_constraint(w_down, pltpu.HBM),
        pltpu.with_memory_space_constraint(b_up, pltpu.HBM),
    )
    return out.reshape(128, UNITS, 8, 128)


def segment_ends(len_ref):
    e0 = len_ref[0, 0]
    e1 = e0 + len_ref[0, 1]
    return e0, e1, e1 + len_ref[0, 2]


def segment_of(p, ends):
    return sum((p >= e).astype(i32) for e in ends)


def turn(product):
    r = product.astype(f32) * (1.0 / DFT_LEN)
    m = product - DFT_LEN * jnp.round(r).astype(i32)
    x = m.astype(f32) * (2.0 * math.pi / DFT_LEN)
    z = x * x
    c = 1.0
    s = 1.0
    for k in range(8, 0, -1):
        c = 1.0 - z * c * (1.0 / ((2 * k - 1) * (2 * k)))
        s = 1.0 - z * s * (1.0 / ((2 * k) * (2 * k + 1)))
    return c, x * s


def attend_kernel(
    len_ref, x_ref, wv_ref, bv_ref, taps_ref, wo_ref, bo_ref, ga_ref, sa_ref, q_ref, k_ref, live_ref,
    n_ref, inv_ref, low_ref, low_a, low_b, ctx_ref, col_ref, nrm_ref, scl_ref, wave_ref, wavet_ref, ks_ref, vs_ref,
    tapt_ref, live_out, qw, kb, jn, tapbuf, mix, mskd,
):
    ends = segment_ends(len_ref)
    square = (ROWS, ROWS)
    rows_i = lax.broadcasted_iota(i32, square, 0)
    lanes_i = lax.broadcasted_iota(i32, square, 1)
    jn[...] = jnp.where(segment_of(rows_i, ends) == segment_of(lanes_i, ends), 1.0 / SETS, 0.0)
    d = lax.broadcasted_iota(i32, (384, 128), 0) - 4 * lax.broadcasted_iota(i32, (384, 128), 1)
    w_lo = jnp.where(d == 0, 1.0, jnp.where(d == 1, 256.0, 0.0)).astype(bf16)
    w_hi = jnp.where(d == 2, 1.0, jnp.where(d == 3, 256.0, 0.0)).astype(bf16)
    q_codes = q_ref[...].astype(f32).astype(bf16)
    k_codes = k_ref[...].astype(f32).astype(bf16)
    qw[...] = dot(q_codes, w_lo).astype(i32) | (dot(q_codes, w_hi).astype(i32) << 16)
    kw = dot(k_codes, w_lo).T.astype(i32) | (dot(k_codes, w_hi).T.astype(i32) << 16)
    for r in range(96):
        for j in range(2):
            kb[r, j] = jnp.broadcast_to(kw[r : r + 1, j * 128 : j * 128 + 128], (8, 128))
    low7 = jnp.int32(0x7F7F7F7F)
    ones = jnp.int32(0x01010101)
    byte2 = jnp.int32(0x00FF00FF)
    tile_rows = 16
    groups = tile_rows // 8

    def tile(rt, carry):
        rs = pl.ds(pl.multiple_of(rt * tile_rows, tile_rows), tile_rows)
        qt = qw[rs, :]
        for h in range(HEADS):
            acc = [[jnp.zeros((8, 128), i32) for _ in range(2)] for _ in range(groups)]
            for g in range(8):
                c = h * 8 + g
                qc = [
                    jnp.broadcast_to(qt[t * 8 : t * 8 + 8, c : c + 1], (8, 128))
                    for t in range(groups)
                ]
                for j in range(2):
                    kk = kb[c, j]
                    for t in range(groups):
                        x = qc[t] ^ kk
                        y = ((x & low7) + low7) | x
                        acc[t][j] = acc[t][j] + (lax.shift_right_logical(y, 7) & ones)
            for j in range(2):
                parts = []
                for t in range(groups):
                    z = acc[t][j]
                    z = (z & byte2) + (lax.shift_right_logical(z, 8) & byte2)
                    z = (z & jnp.int32(0xFFFF)) + lax.shift_right_logical(z, 16)
                    parts.append((SETS - z).astype(f32))
                m = jnp.concatenate(parts, axis=0) * jn[rs, j * 128 : j * 128 + 128]
                col_ref[h, rs, j * 128 : j * 128 + 128] = m.astype(bf16)
        return carry

    lax.fori_loop(0, ROWS // tile_rows, tile, 0)

    col_ref.leave()

    dims = (FREQ, ROWS)
    f = lax.broadcasted_iota(i32, dims, 0)
    p = lax.broadcasted_iota(i32, dims, 1)
    c, s = turn(f * (p + MARGIN * segment_of(p, ends)))
    ok = f < LIVE_FREQ
    wave_ref[0:FREQ] = jnp.where(ok, c, 0.0).astype(bf16)
    wave_ref[FREQ:] = jnp.where(ok, s, 0.0).astype(bf16)
    p = lax.broadcasted_iota(i32, dims, 0)
    f = lax.broadcasted_iota(i32, dims, 1)
    c, s = turn(f * (p + MARGIN * segment_of(p, ends)))
    ok = f < LIVE_FREQ
    wavet_ref[:, 0:FREQ] = jnp.where(ok, c, 0.0).astype(bf16)
    wavet_ref[:, FREQ:] = jnp.where(ok, s, 0.0).astype(bf16)
    dims = (FREQ, 128)
    f = lax.broadcasted_iota(i32, dims, 0)
    c, s = turn(f * (lax.broadcasted_iota(i32, dims, 1) - MARGIN))
    tap_c = c.astype(bf16)
    tap_s = s.astype(bf16)
    dims = (128, FREQ)
    f = lax.broadcasted_iota(i32, dims, 1)
    c, s = turn(f * (lax.broadcasted_iota(i32, dims, 0) - MARGIN))
    tapt_ref[:, 0:FREQ] = c.astype(bf16)
    tapt_ref[:, FREQ:] = s.astype(bf16)
    tapbuf[...] = jnp.zeros(tapbuf.shape, f32)
    tapbuf[0:TAPS] = taps_ref[...].astype(f32)
    kernel = tapbuf[...].astype(bf16)
    f = lax.broadcasted_iota(i32, (FREQ, 1), 0)
    weight = jnp.where((f == 0) | (f == DFT_LEN // 2), 1.0 / DFT_LEN, 2.0 / DFT_LEN)
    weight = jnp.where(f < LIVE_FREQ, weight, 0.0)
    k_cos = dot(tap_c, kernel) * weight
    k_sin = dot(tap_s, kernel) * weight
    ks_ref[0:FREQ] = k_cos
    ks_ref[FREQ:] = k_sin

    live = jnp.broadcast_to(live_ref[...].astype(f32), (8, ROWS)).T[:, 0:1]
    live_out[...] = jnp.broadcast_to(live, (ROWS, 128))
    values = (dot(x_ref[...], wv_ref[...]) + bv_ref[...].astype(f32)).astype(bf16).astype(f32)
    mskd[...] = (values * live).astype(bf16)
    masked = mskd[...]
    spec = dot(wave_ref[...], masked)
    vs_ref[...] = spec.astype(bf16)
    v_cos = spec[0:FREQ]
    v_sin = spec[FREQ:]
    first_head = lanes((ROWS, 128)) < HEAD_DIM
    y_cos = (k_cos * v_cos + k_sin * v_sin).astype(bf16)
    y_sin = (k_cos * v_sin - k_sin * v_cos).astype(bf16)
    conv = dot(wavet_ref[:, 0:FREQ], y_cos) + dot(wavet_ref[:, FREQ:], y_sin)
    for done in (wave_ref, wavet_ref, tapt_ref, ks_ref, live_out, vs_ref):
        done.leave()

    def heads(b, carry):
        cs = pl.ds(pl.multiple_of(b * 128, 128), 128)
        block = mskd[:, cs]
        m = jnp.where(first_head, dot(col_ref[2 * b], block), dot(col_ref[2 * b + 1], block))
        sq = m * m
        one = jnp.sum(jnp.where(first_head, sq, 0.0), axis=1, keepdims=True)
        two = jnp.sum(jnp.where(first_head, 0.0, sq), axis=1, keepdims=True)
        scale = lax.rsqrt(jnp.where(first_head, one, two) * (1.0 / HEAD_DIM) + 1e-06)
        scl_ref[:, cs] = scale
        nrm = m * scale
        nrm_ref[:, cs] = nrm.astype(bf16)
        mix[:, cs] = nrm
        return carry

    lax.fori_loop(0, COLS, heads, 0)
    context = (mix[...] + conv).astype(bf16)
    ctx_ref[...] = context
    for done in (scl_ref, nrm_ref, ctx_ref):
        done.leave()
    attended = dot(context, wo_ref[...]) + bo_ref[...].astype(f32)
    n, inv = norm_rows(x_ref[...].astype(f32) + attended)
    n_ref[...] = n
    inv_ref[...] = jnp.broadcast_to(inv, (ROWS, 128))
    low = (n * ga_ref[...].astype(f32) + sa_ref[...].astype(f32)).astype(bf16)
    low_ref[...] = low
    low_a[...] = low[0:HALF]
    low_b[...] = low[HALF:]


def attend(seq_lengths, x, wv, bv, taps, wo, bo, ga, sa, q, k, live):
    wide = (ROWS, WIDTH)
    half = (HALF, WIDTH)
    h = "hbm"
    v = "vmem"
    return staged_call(
        attend_kernel, "attend", 36,
        [
            ("smem", seq_lengths), (h, x), (h, wv), (v, bv), (v, taps), (h, wo), (v, bo), (v, ga),
            (v, sa), (h, q), (h, k), (v, live),
        ],
        [
            (h, shape(wide, f32)), (h, shape((ROWS, 128), f32)), (v, shape(wide, bf16)),
            (v, shape(half, bf16)), (v, shape(half, bf16)), (h, shape(wide, bf16)),
            (h, shape((HEADS, ROWS, ROWS), bf16)), (h, shape(wide, bf16)), (h, shape(wide, f32)),
            (h, shape((2 * FREQ, ROWS), bf16)), (h, shape((ROWS, 2 * FREQ), bf16)),
            (h, shape((2 * FREQ, WIDTH), f32)), (h, shape((2 * FREQ, WIDTH), bf16)),
            (h, shape((128, 2 * FREQ), bf16)), (h, shape((ROWS, 128), f32)),
        ],
        [
            pltpu.VMEM((ROWS, 128), i32),
            pltpu.VMEM((96, 2, 8, 128), i32),
            pltpu.VMEM((ROWS, ROWS), f32),
            pltpu.VMEM((128, WIDTH), f32),
            pltpu.VMEM(wide, f32),
            pltpu.VMEM(wide, bf16),
        ],
    )


def unpack(ref, m, out):
    for a in range(PIECES):
        rs = slice(a * 192, a * 192 + 192)
        for ct in range(COLS):
            first = 3 * (ct % 3)
            part = ref[m, a, ct // 3, :, first : first + 3].astype(f32)
            out[rs, ct * 128 : ct * 128 + 128] = part.reshape(192, 128).astype(bf16)


def unpack_bias(ref, out):
    for a in range(PIECES):
        tile = ref[0, a, 0, :, UNITS - 1].astype(f32)
        lane = lanes(tile.shape)
        parts = [jnp.where(lane == rt, tile, 0.0)[:, None] for rt in range(3)]
        column = jnp.concatenate(parts, axis=1).reshape(192, 128)
        out[a * 192 : a * 192 + 192, WIDTH:] = column.astype(bf16)


def ffn_blocks(rows, wu, wd, act, slope, acc):
    acc[...] = jnp.zeros(acc.shape, f32)

    def block(i, carry):
        hs = pl.ds(pl.multiple_of(i * 256, 256), 256)
        upper = dot_last(rows[...], wu[hs, :])
        cdf = 0.5 * (1.0 + lax.erf(upper * math.sqrt(0.5)))
        a = (upper * cdf).astype(bf16)
        act[:, hs] = a
        density = jnp.exp(-0.5 * upper * upper) * (1.0 / math.sqrt(2.0 * math.pi))
        slope[:, hs] = (cdf + upper * density).astype(bf16)
        acc[...] += dot(a, wd[hs, :])
        return carry

    lax.fori_loop(0, HIDDEN // 256, block, 0)


def ffn_far_kernel(
    got_a, got_b, sib_a, sib_b, w, act, slope, part_own, part_sib, rows_out, wu, wd, rows, acc,
):
    for i, ref in enumerate((got_a, got_b, sib_a, sib_b)):
        rows[i * HALF : i * HALF + HALF, 0:WIDTH] = ref[...]
    rows[:, WIDTH:] = jnp.where(lanes((2 * ROWS, 128)) < 3, 1.0, 0.0).astype(bf16)
    rows_out[...] = rows[:, 0:WIDTH]
    unpack(w, 0, wu)
    unpack_bias(w, wu)
    unpack(w, 1, wd)
    ffn_blocks(rows, wu, wd, act, slope, acc)
    part_own[...] = acc[0:ROWS]
    part_sib[...] = acc[ROWS:].astype(bf16)


def ffn_near_kernel(own, sib, wu, wd, act, slope, part_own, part_sib, rows_out, rows, acc):
    rows[0:ROWS, 0:WIDTH] = own[...]
    rows[ROWS:, 0:WIDTH] = sib[...]
    rows[:, WIDTH:] = jnp.where(lanes((2 * ROWS, 128)) < 3, 1.0, 0.0).astype(bf16)
    rows_out[...] = rows[:, 0:WIDTH]
    ffn_blocks(rows, wu, wd, act, slope, acc)
    part_own[...] = acc[0:ROWS]
    part_sib[...] = acc[ROWS:].astype(bf16)


def ffn_call(kernel, name, ins, outs):
    wide = (ROWS, WIDTH)
    tall = shape((2 * ROWS, WIDTH), bf16)
    return staged_call(
        kernel, name, 24, ins,
        [("vmem", o) for o in (tall, tall, shape(wide, f32), shape(wide, bf16), tall, *outs)],
        [pltpu.VMEM((2 * ROWS, WIDTH + 128), bf16), pltpu.VMEM((2 * ROWS, WIDTH), f32)],
    )


def ffn_far(got_a, got_b, sib_a, sib_b, weights):
    rows = [("vmem", a) for a in (got_a, got_b, sib_a, sib_b)]
    return ffn_call(
        ffn_far_kernel, "ffn_far", [*rows, ("pair", weights)],
        [shape((HIDDEN, WIDTH + 128), bf16), shape((HIDDEN, WIDTH), bf16)],
    )


def ffn_near(*args):
    return ffn_call(ffn_near_kernel, "ffn_near", [("vmem", a) for a in args], [])


def combine_kernel(own, got, out_a, out_b):
    total = (own[...] + got[...].astype(f32)).astype(bf16)
    out_a[...] = total[0:HALF]
    out_b[...] = total[HALF:]


def combine(own, got):
    half = shape((HALF, WIDTH), bf16)
    return pl.pallas_call(
        combine_kernel,
        out_shape=(half, half),
        in_specs=[VMEM] * 2,
        out_specs=(VMEM,) * 2,
        compiler_params=params(32),
        name="combine",
    )(own, got)


def gather_rows(own, near, far_a, far_b):
    far = jnp.concatenate([far_a[...], far_b[...]], axis=0)
    return own[...] + near[...].astype(f32) + far.astype(f32)


def middle_kernel(
    n1, own, near, far_a, far_b, bd, ga, sa, gf, sf, og, out, second, low, low_a, low_b, sums,
):
    first = n1[...] * ga[...].astype(f32) + sa[...].astype(f32)
    n, inv = norm_rows(first + gather_rows(own, near, far_a, far_b) + bd[...].astype(f32))
    gain = gf[...].astype(f32)
    out[...] = (n * gain + sf[...].astype(f32)).astype(bf16)
    g = og[...].astype(f32)
    grad = norm_back(g, n, inv, gain)
    second[...] = grad
    grad_low = grad.astype(bf16)
    low[...] = grad_low
    low_a[...] = grad_low[0:HALF]
    low_b[...] = grad_low[HALF:]
    sums[0:1] = jnp.sum(grad_low.astype(f32), axis=0, keepdims=True)
    sums[1:2] = jnp.sum(g * n, axis=0, keepdims=True)
    sums[2:3] = jnp.sum(g, axis=0, keepdims=True)
    sums[3:8] = jnp.zeros((5, WIDTH), f32)


def middle(*args):
    wide = (ROWS, WIDTH)
    half = (HALF, WIDTH)
    return staged_call(
        middle_kernel, "middle", 16, [("vmem", a) for a in args],
        [
            ("hbm", shape(wide, bf16)), ("hbm", shape(wide, f32)), ("vmem", shape(wide, bf16)),
            ("vmem", shape(half, bf16)), ("vmem", shape(half, bf16)), ("hbm", shape((8, WIDTH), f32)),
        ],
    )


def back_blocks(g, wu, wd, slope, u_out, bias, acc):
    acc[...] = jnp.zeros(acc.shape, f32)
    bias[...] = jnp.zeros((8, HIDDEN), f32)

    def block(i, carry):
        hs = pl.ds(pl.multiple_of(i * 256, 256), 256)
        u = (dot_last(g[...], wd[hs, :]) * slope[:, hs].astype(f32)).astype(bf16)
        u_out[:, hs] = u
        bias[0:1, hs] = jnp.sum(u.astype(f32), axis=0, keepdims=True)
        acc[...] += dot(u, wu[hs, 0:WIDTH])
        return carry

    lax.fori_loop(0, HIDDEN // 256, block, 0)


def back_near_kernel(own, sib, wu, wd, slope, first_own, first_sib, g, u, bias, acc):
    g[0:ROWS] = own[...]
    g[ROWS:] = sib[...]
    back_blocks(g, wu, wd, slope, u, bias, acc)
    first_own[...] = acc[0:ROWS]
    first_sib[...] = acc[ROWS:].astype(bf16)


def back_far_kernel(
    got_a, got_b, sib_a, sib_b, wu, wd, slope, first_own, first_sib, g, u, bias, acc,
):
    for i, ref in enumerate((got_a, got_b, sib_a, sib_b)):
        g[i * HALF : i * HALF + HALF] = ref[...]
    back_blocks(g, wu, wd, slope, u, bias, acc)
    first_own[...] = acc[0:ROWS]
    first_sib[...] = acc[ROWS:].astype(bf16)


def back_call(kernel, name, *args):
    wide = (ROWS, WIDTH)
    tall = shape((2 * ROWS, WIDTH), bf16)
    return staged_call(
        kernel, name, 20, [("vmem", a) for a in args],
        [
            ("hbm" if name == "back_near" else "vmem", shape(wide, f32)), ("vmem", shape(wide, bf16)),
            ("vmem", tall), ("vmem", tall), ("hbm", shape((8, HIDDEN), f32)),
        ],
        [pltpu.VMEM((2 * ROWS, WIDTH), f32)],
    )


def pack_kernel(gu, gd, grads):
    for a in range(PIECES):
        rs = slice(a * 192, a * 192 + 192)
        for ct in range(COLS):
            cs = slice(ct * 128, ct * 128 + 128)
            us = slice(3 * (ct % 3), 3 * (ct % 3) + 3)
            up = gu[rs, cs].astype(f32).reshape(8, 3, 8, 128)
            down = gd[rs, cs].astype(f32).reshape(8, 3, 8, 128)
            grads[0, a, ct // 3, :, us] = up.astype(bf16)
            grads[1, a, ct // 3, :, us] = down.astype(bf16)


def pack(*args):
    return staged_call(
        pack_kernel, "pack", 12, [("vmem", a) for a in args],
        [("hbm", shape((2, PIECES, 2, 8, GRAD_UNITS, 8, 128), bf16))],
    )[0]


def back_kernel(
    place, own, near, far_a, far_b, second, n1, inv1, ga, ctx, wo, nrm, scl, wave, wavet, ks, vs, tapt, col, live, x,
    wv, sums, bias_n, bias_f, in_grad, keep, give, buf_a, buf_b, mb,
):
    first_grad = second[...] + gather_rows(own, near, far_a, far_b)
    n = n1[...]
    buf_a[768 + 2 : 768 + 3] = jnp.sum(first_grad * n, axis=0, keepdims=True)
    buf_a[768 + 3 : 768 + 4] = jnp.sum(first_grad, axis=0, keepdims=True)
    resid = norm_back(first_grad, n, inv1[...][:, 0:1], ga[...].astype(f32))
    ag = resid.astype(bf16)
    buf_a[768 + 1 : 768 + 2] = jnp.sum(ag.astype(f32), axis=0, keepdims=True)
    buf_a[768 + 4 : 768 + 7] = sums[0:3]
    buf_a[768 + 7 :] = jnp.zeros((TALL - 775, WIDTH), f32)
    mine = lax.broadcasted_iota(i32, (8, WIDTH), 0) == place[0] % CLASSES
    bias = jnp.broadcast_to(bias_n[0:1] + bias_f[0:1], (8, WIDTH))
    buf_a[776:784] = jnp.where(mine, bias, 0.0)
    buf_b[0:768] = dot_first(ctx[...], ag)
    cg = dot_last(ag, wo[...])
    mb[...] = cg
    first_head = lanes((ROWS, 128)) < HEAD_DIM
    nrm.ready()
    scl.ready()
    col.ready()

    def heads(b, carry):
        cs = pl.ds(pl.multiple_of(b * 128, 128), 128)
        c = mb[:, cs]
        m = nrm[:, cs].astype(f32)
        prod = c * m
        one = jnp.sum(jnp.where(first_head, prod, 0.0), axis=1, keepdims=True)
        two = jnp.sum(jnp.where(first_head, 0.0, prod), axis=1, keepdims=True)
        mean = jnp.where(first_head, one, two) * (1.0 / HEAD_DIM)
        block = (scl[:, cs] * (c - m * mean)).astype(bf16)
        mb[:, cs] = jnp.where(
            first_head, dot_first(col[2 * b], block), dot_first(col[2 * b + 1], block)
        )
        return carry

    lax.fori_loop(0, COLS, heads, 0)
    spec = dot(wave[...], cg.astype(bf16))
    g_cos = spec[0:FREQ]
    g_sin = spec[FREQ:]
    k_cos = ks[0:FREQ]
    k_sin = ks[FREQ:]
    z_cos = (k_cos * g_cos - k_sin * g_sin).astype(bf16)
    z_sin = (k_cos * g_sin + k_sin * g_cos).astype(bf16)
    conv = dot(wavet[:, 0:FREQ], z_cos) + dot(wavet[:, FREQ:], z_sin)
    v_cos = vs[0:FREQ].astype(f32)
    v_sin = vs[FREQ:].astype(f32)
    f = lax.broadcasted_iota(i32, (FREQ, 1), 0)
    weight = jnp.where((f == 0) | (f == DFT_LEN // 2), 1.0 / DFT_LEN, 2.0 / DFT_LEN)
    weight = jnp.where(f < LIVE_FREQ, weight, 0.0)
    re = ((g_cos * v_cos + g_sin * v_sin) * weight).astype(bf16)
    im = ((g_cos * v_sin - g_sin * v_cos) * weight).astype(bf16)
    gk = dot(tapt[:, 0:FREQ], re) + dot(tapt[:, FREQ:], im)
    buf_b[768:] = jnp.zeros((TALL - 768, WIDTH), f32)
    buf_b[768 : 768 + TAPS] = gk[0:TAPS]
    vg = ((mb[...] + conv) * live[...][:, 0:1]).astype(bf16)
    buf_a[768:769] = jnp.sum(vg.astype(f32), axis=0, keepdims=True)
    buf_a[0:768] = dot_first(x[...], vg)
    in_grad[...] = resid + dot_last(vg, wv[...])

    def write(kept, given):
        for ct in range(COLS):
            cs = slice(ct * 128, ct * 128 + 128)
            ts = slice(ct * TALL_TILES, ct * TALL_TILES + TALL_TILES)
            keep[ts] = kept[:, cs].reshape(TALL_TILES, 8, 128).astype(bf16)
            give[ts] = given[:, cs].reshape(TALL_TILES, 8, 128).astype(bf16)

    rest = PACK - COLS * TALL_TILES
    keep[PACK - rest :] = jnp.zeros((rest, 8, 128), bf16)
    give[PACK - rest :] = jnp.zeros((rest, 8, 128), bf16)

    @pl.when(place[0] % 2 == 0)
    def _():
        write(buf_a, buf_b)

    @pl.when(place[0] % 2 == 1)
    def _():
        write(buf_b, buf_a)


def attend_back(*args):
    wide = (ROWS, WIDTH)
    packed = shape((PACK, 8, 128), bf16)
    kinds = ["smem"] + ["hbm"] * (len(args) - 1)
    for i in (2, 3, 4, 8):
        kinds[i] = "vmem"
    return staged_call(
        back_kernel, "attend_back", 40, list(zip(kinds, args, strict=True)),
        [("hbm", shape(wide, f32)), ("vmem", packed), ("vmem", packed)],
        [
            pltpu.VMEM((TALL, WIDTH), f32),
            pltpu.VMEM((TALL, WIDTH), f32),
            pltpu.VMEM(wide, f32),
        ],
    )


def sum_ffn_kernel(got, out, acc):
    step = pl.program_id(0)

    @pl.when(step == 0)
    def _():
        acc[...] = jnp.zeros(acc.shape, f32)

    for q in range(CLASSES):
        total = acc[q]
        for t in range(8):
            total = total + got[q * 8 + t].astype(f32)
        acc[q] = total

    @pl.when(step == 3)
    def _():
        out[...] = acc[...].astype(bf16)


def sum_ffn(got):
    return pl.pallas_call(
        sum_ffn_kernel,
        grid=(4,),
        out_shape=shape((CLASSES, GRAD_UNITS, 8, 128), bf16),
        in_specs=[pl.BlockSpec((32, GRAD_UNITS, 8, 128), lambda i: (i, 0, 0, 0))],
        out_specs=pl.BlockSpec((CLASSES, GRAD_UNITS, 8, 128), lambda i: (0, 0, 0, 0)),
        scratch_shapes=[pltpu.VMEM((CLASSES, GRAD_UNITS, 8, 128), f32)],
        compiler_params=params(32),
        name="sum_ffn",
    )(got)


def sum_rest_kernel(got, out):
    per = PACK // 128
    total = [jnp.zeros((per, 8, 128), f32) for _ in range(2)]
    for i in range(8):
        for c in range(2):
            for t in range(8):
                total[c] = total[c] + got[i * 16 + c * 8 + t].astype(f32)
    low = [t.astype(bf16) for t in total]
    for i in range(8):
        for c in range(2):
            for t in range(8):
                out[i * 16 + c * 8 + t] = low[c]


def sum_rest(got):
    return pl.pallas_call(
        sum_rest_kernel,
        out_shape=shape(got.shape, bf16),
        in_specs=[VMEM],
        out_specs=VMEM,
        compiler_params=params(32),
        name="sum_rest",
    )(got)


def final_ffn_kernel(place, ffn_own, ffn_oth, g_up, g_down, tall):
    ct = pl.program_id(0)
    core = place[0] % 2

    def index(m, a):
        return (m + place[0] // 8) % 2 * 4 + (place[0] // 2 % 4 + 4 - a) % 4

    def spread(ref):
        for a in range(PIECES):
            up = ref[index(0, a)].astype(f32)
            down = ref[index(1, a)].astype(f32)
            for q in range(CLASSES):
                rs = slice(SUB * q + PIECE * a, SUB * q + PIECE * a + PIECE)
                tall[rs, :] = up[q].reshape(PIECE, 128)
                g_down[rs, :] = down[q].reshape(PIECE, 128)

    @pl.when(ct // 3 == core)
    def _():
        spread(ffn_own)

    @pl.when(ct // 3 != core)
    def _():
        spread(ffn_oth)

    g_up[...] = tall[...].T


def final_ffn(place, ffn_own, ffn_oth):
    units = pl.BlockSpec((8, CLASSES, 3, 8, 128), lambda i: (0, 0, i % 3, 0, 0))
    return pl.pallas_call(
        final_ffn_kernel,
        grid=(COLS,),
        out_shape=(shape((768, 384), f32), shape((384, 768), f32)),
        in_specs=[SMEM, units, units],
        out_specs=(
            pl.BlockSpec((128, 384), lambda i: (i, 0)),
            pl.BlockSpec((384, 128), lambda i: (0, i)),
        ),
        scratch_shapes=[pltpu.VMEM((384, 128), f32)],
        compiler_params=params(16),
        name="final_ffn",
    )(place, ffn_own, ffn_oth)


def final_kernel(
    place, own, other, g_wv, g_bv, g_conv, g_wo, g_bo, g_ga, g_sa, g_bup, g_bd, g_gf, g_sf, vecs,
    bias, line,
):
    ct = pl.program_id(0)

    def write(a, b):
        g_wv[...] = a[0:96].astype(f32).reshape(768, 128)
        vecs[ct] = a[96].astype(f32)
        bias[ct] = a[97].astype(f32)
        g_wo[...] = b[0:96].astype(f32).reshape(768, 128)
        g_conv[...] = b[96:105].astype(f32).reshape(72, 128)[0:TAPS]

    @pl.when(place[0] % 2 == 0)
    def _():
        write(own, other)

    @pl.when(place[0] % 2 == 1)
    def _():
        write(other, own)

    @pl.when(ct == COLS - 1)
    def _():
        for j, ref in enumerate((g_bv, g_bo, g_ga, g_sa, g_bd, g_gf, g_sf)):
            for i in range(COLS):
                ref[i * 128 : i * 128 + 128] = vecs[i, j]
        n = lanes((128, 128))
        a = (n >= PIECE).astype(i32) + (n >= 2 * PIECE).astype(i32) + (n >= 3 * PIECE).astype(i32)
        at = (8 * a + place[1]) * PIECE + n - PIECE * a
        total = jnp.zeros((8, 128), f32)
        for i in range(COLS):
            pick = lax.broadcasted_iota(i32, (128, 128), 0) + 128 * i == at
            total = total + dot(bias[i].astype(bf16), jnp.where(pick, 1.0, 0.0).astype(bf16))
        for q in range(CLASSES):
            line[0:1, SUB * q : SUB * q + SUB] = total[q : q + 1, 0:SUB]
        g_bup[...] = line[...][0]


def final(place, own, other):
    tile = pl.BlockSpec((TALL_TILES, 8, 128), lambda i: (i, 0, 0))
    tall = pl.BlockSpec((768, 128), lambda i: (0, i))
    vec = pl.BlockSpec((WIDTH,), lambda i: (0,))
    v = shape((WIDTH,), f32)
    return pl.pallas_call(
        final_kernel,
        grid=(COLS,),
        out_shape=(
            shape((768, 768), f32), v, shape((TAPS, 768), f32), shape((768, 768), f32), v, v, v,
            shape((384,), f32), v, v, v,
        ),
        in_specs=[SMEM, tile, tile],
        out_specs=(
            tall, vec, pl.BlockSpec((TAPS, 128), lambda i: (0, i)), tall, vec, vec, vec,
            pl.BlockSpec((384,), lambda i: (0,)), vec, vec, vec,
        ),
        scratch_shapes=[
            pltpu.VMEM((COLS, 8, 128), f32),
            pltpu.VMEM((COLS, 8, 128), f32),
            pltpu.VMEM((1, 384), f32),
        ],
        compiler_params=params(16),
        name="final",
    )(place, own, other)


def body(
    block_input,
    w_value,
    b_value,
    conv_kernel,
    w_out,
    b_out,
    gain_attn,
    shift_attn,
    w_up,
    b_up,
    w_down,
    b_down,
    gain_ffn,
    shift_ffn,
    query_codes,
    key_codes,
    key_live,
    seq_lengths,
    out_grad,
):
    dp = lax.axis_index("dp")
    place = jnp.stack([dp, lax.axis_index("tensor")]).astype(i32)
    n_dp = lax.axis_size("dp")

    def shift(i, by):
        return i // 8 * 8 + (i // 2 + by) % 4 * 2 + i % 2

    def swap(x):
        return lax.ppermute(x, "dp", [(i, i ^ 1) for i in range(n_dp)])

    def ahead(x):
        return lax.ppermute(x, "dp", [(i, shift(i, 1)) for i in range(n_dp)])

    def behind(x):
        return lax.ppermute(x, "dp", [(i, shift(i, -1)) for i in range(n_dp)])

    def exchange(x):
        return lax.all_to_all(x, ALL, 0, 0, tiled=True)

    def row(v):
        return v.reshape(1, -1)

    weights = exchange(prep(place, w_up, w_down, b_up))
    weights = weights.reshape(2, PIECES, 2, 8, UNITS, 8, 128)
    (n1, inv1, low, low_a, low_b, ctx, collide, nrm, scl, wave, wavet, ks, vs, tapt, live) = attend(
        seq_lengths, block_input, w_value, row(b_value), conv_kernel, w_out, row(b_out),
        row(gain_attn), row(shift_attn), query_codes, key_codes, row(key_live),
    )
    low_sib = swap(low)
    row_a, row_b = ahead(low_a), behind(low_b)
    act_f, slope_f, far_own, far_sib, rows_f, wu, wd = ffn_far(
        row_a, row_b, swap(row_a), swap(row_b), weights
    )
    sent_a, sent_b = combine(far_own, swap(far_sib))
    wu, sent_a, sent_b = lax.optimization_barrier((wu, sent_a, sent_b))
    act_n, slope_n, near_own, near_sib, rows_n = ffn_near(low, low_sib, wu, wd)
    back_a, back_b = behind(sent_a), ahead(sent_b)
    near_sib, back_a, back_b = lax.optimization_barrier((near_sib, back_a, back_b))
    block_output, second, grad, grad_a, grad_b, sums = middle(
        n1, near_own, swap(near_sib), back_a, back_b, row(b_down), row(gain_attn),
        row(shift_attn), row(gain_ffn), row(shift_ffn), out_grad,
    )
    got_a, got_b = ahead(grad_a), behind(grad_b)
    near_own, near_sib, g_n, u_n, bias_n = back_call(
        back_near_kernel, "back_near", grad, swap(grad), wu, wd, slope_n
    )
    got_a, got_b, near_sib = lax.optimization_barrier((got_a, got_b, near_sib))
    far_own, far_sib, g_f, u_f, bias_f = back_call(
        back_far_kernel, "back_far", got_a, got_b, swap(got_a), swap(got_b), wu, wd, slope_f
    )
    sent_a, sent_b = combine(far_own, swap(far_sib))
    u_f, sent_a, sent_b = lax.optimization_barrier((u_f, sent_a, sent_b))
    grad_down = (dot_first(act_n, g_n) + dot_first(act_f, g_f)).astype(bf16)
    grad_up = (dot_first(u_n, rows_n) + dot_first(u_f, rows_f)).astype(bf16)
    grads = pack(grad_up, grad_down)
    back_a, back_b = behind(sent_a), ahead(sent_b)
    grads, back_a, back_b = lax.optimization_barrier((grads, back_a, back_b))
    owned = exchange(grads.reshape(128, GRAD_UNITS, 8, 128))
    input_grad, keep, give = attend_back(
        place, near_own, swap(near_sib), back_a, back_b, second, n1, inv1,
        row(gain_attn), ctx, w_out, nrm, scl, wave, wavet, ks, vs, tapt, collide, live, block_input,
        w_value, sums, bias_n, bias_f,
    )
    pair = (keep.astype(f32) + swap(give).astype(f32)).astype(bf16)
    pair = pair.reshape(128, PACK // 128, 8, 128)
    owned = sum_ffn(owned)
    pair, owned = lax.optimization_barrier((pair, owned))
    around = []
    for side in range(2):
        for by in range(4):
            if side or by:
                pairs = [(i, (i // 8 + side) % 2 * 8 + shift(i % 8, by)) for i in range(n_dp)]
                around.append(lax.ppermute(owned, "dp", pairs))
    summed = sum_rest(exchange(pair))
    summed, *around = lax.optimization_barrier((summed, *around))
    back = exchange(summed).reshape(PACK, 8, 128)
    ffn_own = jnp.stack([owned, *around])
    g_up, g_down = final_ffn(place, ffn_own, swap(ffn_own))
    back, g_up, g_down = lax.optimization_barrier((back, g_up, g_down))
    g_wv, g_bv, g_conv, g_wo, g_bo, g_ga, g_sa, g_bup, g_bd, g_gf, g_sf = final(
        place, back, swap(back)
    )
    return (
        block_output, input_grad, g_wv, g_bv, g_conv, g_wo, g_bo, g_ga, g_sa, g_up, g_bup, g_down,
        g_bd, g_gf, g_sf,
    )


def solution(mesh):
    rows = P(ALL, None)
    return jax.shard_map(
        body,
        mesh=mesh,
        in_specs=(
            rows, P(), P(), P(), P(), P(), P(), P(),
            P(None, "tensor"), P("tensor"), P("tensor", None), P(), P(), P(),
            rows, rows, P(ALL), rows, rows,
        ),
        out_specs=(
            rows, rows, P(), P(), P(), P(), P(), P(), P(),
            P(None, "tensor"), P("tensor"), P("tensor", None), P(), P(), P(),
        ),
        check_vma=False,
    )
```

```python
import math

import jax
import jax.numpy as jnp
from jax import lax
from jax.experimental import pallas as pl
from jax.experimental.pallas import tpu as pltpu
from jax.sharding import PartitionSpec as P

HEADS = 12
SETS = 32
ROWS = 256
WIDTH = 768
HEAD_DIM = 64
COLS = WIDTH // 128
TAPS = 65
MARGIN = 32
DFT_LEN = 384
FREQ = 256
LIVE_FREQ = DFT_LEN // 2 + 1
CLASSES = 4
SUB = 96
PIECE = 24
PIECES = SUB // PIECE
UNITS = 10
GRAD_UNITS = 9
HIDDEN = 768
HALF = ROWS // 2
TALL = 848
TALL_TILES = TALL // 8
PACK = 640
ALL = ("dp", "tensor")

bf16 = jnp.bfloat16
f32 = jnp.float32
i32 = jnp.int32

VMEM = pl.BlockSpec(memory_space=pltpu.VMEM)
SMEM = pl.BlockSpec(memory_space=pltpu.SMEM)
HBM = pl.BlockSpec(memory_space=pltpu.HBM)


def shape(dims, dtype):
    return jax.ShapeDtypeStruct(dims, dtype)


def params(mib):
    return pltpu.CompilerParams(vmem_limit_bytes=mib << 20)


def dot(a, b):
    return lax.dot_general(a, b, (((1,), (0,)), ((), ())), preferred_element_type=f32)


def dot_last(a, b):
    return lax.dot_general(a, b, (((1,), (1,)), ((), ())), preferred_element_type=f32)


def dot_first(a, b):
    return lax.dot_general(a, b, (((0,), (0,)), ((), ())), preferred_element_type=f32)


def lanes(dims):
    return lax.broadcasted_iota(i32, dims, len(dims) - 1)


def norm_rows(r):
    mean = jnp.mean(r, axis=-1, keepdims=True)
    centred = r - mean
    inv = lax.rsqrt(jnp.mean(centred * centred, axis=-1, keepdims=True) + 1e-05)
    return centred * inv, inv


def norm_back(g, n, inv, gain):
    e = g * gain
    return (
        e - jnp.mean(e, axis=-1, keepdims=True) - n * jnp.mean(e * n, axis=-1, keepdims=True)
    ) * inv


class Staged:
    def __init__(self, ref, buf, sem, incoming):
        pair = (ref, buf) if incoming else (buf, ref)
        self.buf = buf
        self.copy = pltpu.make_async_copy(*pair, sem)
        self.incoming = incoming
        self.pending = True
        if incoming:
            self.copy.start()

    def ready(self):
        if self.pending:
            self.copy.wait()
            self.pending = False

    def leave(self):
        if self.pending:
            self.copy.start()
            self.pending = False

    def __getitem__(self, index):
        if self.incoming:
            self.ready()
        return self.buf[index]

    def __setitem__(self, index, value):
        self.buf[index] = value


class StagedPair:
    def __init__(self, ref, buf, sems):
        self.buf = buf
        self.copies = [pltpu.make_async_copy(ref.at[i], buf.at[i], sems.at[i]) for i in range(2)]
        self.pending = [True, True]
        for copy in self.copies:
            copy.start()

    def ready(self):
        for i in range(2):
            if self.pending[i]:
                self.copies[i].wait()
                self.pending[i] = False

    def __getitem__(self, index):
        i = index[0]
        if self.pending[i]:
            self.copies[i].wait()
            self.pending[i] = False
        return self.buf[index]


def staged_call(kernel, name, mib, ins, outs, scratch=()):
    spec = {"smem": SMEM, "vmem": VMEM, "hbm": HBM, "pair": HBM}
    arrays = [a for _, a in ins]
    kinds = [k for k, _ in ins] + [k for k, _ in outs]
    avals = arrays + [o for _, o in outs]
    staged = [i for i, k in enumerate(kinds) if k in ("hbm", "pair")]
    n_in = len(ins)

    if not staged:
        return pl.pallas_call(
            kernel,
            out_shape=tuple(o for _, o in outs),
            in_specs=[spec[k] for k, _ in ins],
            out_specs=tuple(spec[k] for k, _ in outs),
            scratch_shapes=list(scratch),
            compiler_params=params(mib),
            name=name,
        )(*arrays)

    def run(*refs):
        refs = list(refs)
        sems = refs.pop()
        split = len(refs) - len(staged)
        bufs = refs[split:]
        refs = refs[:split]
        for n, i in enumerate(staged):
            if kinds[i] == "pair":
                refs[i] = StagedPair(refs[i], bufs[n], sems.at[n])
            else:
                refs[i] = Staged(refs[i], bufs[n], sems.at[n, 0], i < n_in)
        kernel(*refs)
        for i in staged:
            if i < n_in:
                refs[i].ready()
            else:
                refs[i].leave()
        for i in staged:
            if i >= n_in:
                refs[i].copy.wait()

    buffers = [pltpu.VMEM(avals[i].shape, avals[i].dtype) for i in staged]
    arrays = [
        a if k in ("smem", "vmem") else pltpu.with_memory_space_constraint(a, pltpu.HBM)
        for k, a in ins
    ]
    return pl.pallas_call(
        run,
        out_shape=tuple(pltpu.HBM(o.shape, o.dtype) if k == "hbm" else o for k, o in outs),
        in_specs=[spec[k] for k, _ in ins],
        out_specs=tuple(spec[k] for k, _ in outs),
        scratch_shapes=[*scratch, *buffers, pltpu.SemaphoreType.DMA((len(staged), 2))],
        compiler_params=params(mib),
        name=name,
    )(*arrays)


def prep_kernel(place, up_ref, down_ref, bias_hbm, out_ref, half, piece, bias_ref, sems):
    rep = place[0] % 8
    is_up = place[0] < 8
    at = pl.ds(pl.multiple_of(rep % 2 * 384, 128), 384)
    up = pltpu.make_async_copy(up_ref.at[at, :], half, sems.at[0])
    down = pltpu.make_async_copy(down_ref.at[:, at], half, sems.at[0])
    bias_copy = pltpu.make_async_copy(bias_hbm, bias_ref, sems.at[33])
    bias_copy.start()

    @pl.when(is_up)
    def _():
        up.start()

    @pl.when(jnp.logical_not(is_up))
    def _():
        down.start()

    n = lax.broadcasted_iota(i32, (SUB, 384), 0)
    q = sum((n >= PIECE * k).astype(i32) for k in range(1, CLASSES))
    unit = (SUB - PIECE) * q + n + PIECE * (rep // 2)
    pick = jnp.where(unit == lanes((SUB, 384)), 1.0, 0.0).astype(bf16)
    scale = jnp.where(is_up & (rep % 2 == 0), 1.0, 0.0)
    bias_copy.wait()
    bias = jnp.broadcast_to(bias_ref[...].astype(f32) * scale, (16, 384)).astype(bf16)
    column = dot_last(pick, bias)[:, 0:1]

    def fill(rows):
        for k in range(CLASSES):
            rs = slice(PIECE * k, PIECE * k + PIECE)
            for j in range(3):
                part = rows[rs, j * 128 : j * 128 + 128].reshape(3, 8, 128)
                piece[k, 3 * j : 3 * j + 3] = part.astype(bf16)
            col = jnp.broadcast_to(column[rs], (PIECE, 128)).reshape(3, 8, 128)
            lane = lanes((8, 128))
            tile = jnp.where(lane == 0, col[0], jnp.where(lane == 1, col[1], col[2]))
            piece[k, UNITS - 1] = tile.astype(bf16)

    @pl.when(is_up)
    def _():
        up.wait()
        fill(dot_last(pick, half[...]))

    @pl.when(jnp.logical_not(is_up))
    def _():
        down.wait()
        fill(dot(pick, half[...]))

    copies = [
        pltpu.make_async_copy(piece, out_ref.at[g, :, t], sems.at[1 + 8 * g + t])
        for g in range(4)
        for t in range(8)
    ]
    for copy in copies:
        copy.start()
    for copy in copies:
        copy.wait()


def prep(place, w_up, w_down, b_up):
    out = pl.pallas_call(
        prep_kernel,
        out_shape=pltpu.HBM((4, CLASSES, 8, UNITS, 8, 128), bf16),
        in_specs=[SMEM, HBM, HBM, HBM],
        out_specs=HBM,
        scratch_shapes=[
            pltpu.VMEM((384, 384), bf16),
            pltpu.VMEM((CLASSES, UNITS, 8, 128), bf16),
            pltpu.VMEM((384,), bf16),
            pltpu.SemaphoreType.DMA((34,)),
        ],
        compiler_params=params(16),
        name="prep",
    )(
        place,
        pltpu.with_memory_space_constraint(w_up, pltpu.HBM),
        pltpu.with_memory_space_constraint(w_down, pltpu.HBM),
        pltpu.with_memory_space_constraint(b_up, pltpu.HBM),
    )
    return out.reshape(128, UNITS, 8, 128)


def segment_ends(len_ref):
    e0 = len_ref[0, 0]
    e1 = e0 + len_ref[0, 1]
    return e0, e1, e1 + len_ref[0, 2]


def segment_of(p, ends):
    return sum((p >= e).astype(i32) for e in ends)


def turn(product):
    r = product.astype(f32) * (1.0 / DFT_LEN)
    m = product - DFT_LEN * jnp.round(r).astype(i32)
    x = m.astype(f32) * (2.0 * math.pi / DFT_LEN)
    z = x * x
    c = 1.0
    s = 1.0
    for k in range(8, 0, -1):
        c = 1.0 - z * c * (1.0 / ((2 * k - 1) * (2 * k)))
        s = 1.0 - z * s * (1.0 / ((2 * k) * (2 * k + 1)))
    return c, x * s


def attend_kernel(
    len_ref, x_ref, wv_ref, bv_ref, taps_ref, wo_ref, bo_ref, ga_ref, sa_ref, q_ref, k_ref, live_ref,
    n_ref, inv_ref, low_ref, low_a, low_b, ctx_ref, col_ref, nrm_ref, scl_ref, wave_ref, wavet_ref, ks_ref, vs_ref,
    tapt_ref, live_out, qw, kb, jn, tapbuf, mix, mskd,
):
    ends = segment_ends(len_ref)
    square = (ROWS, ROWS)
    rows_i = lax.broadcasted_iota(i32, square, 0)
    lanes_i = lax.broadcasted_iota(i32, square, 1)
    jn[...] = jnp.where(segment_of(rows_i, ends) == segment_of(lanes_i, ends), 1.0 / SETS, 0.0)
    d = lax.broadcasted_iota(i32, (384, 128), 0) - 4 * lax.broadcasted_iota(i32, (384, 128), 1)
    w_lo = jnp.where(d == 0, 1.0, jnp.where(d == 1, 256.0, 0.0)).astype(bf16)
    w_hi = jnp.where(d == 2, 1.0, jnp.where(d == 3, 256.0, 0.0)).astype(bf16)
    q_codes = q_ref[...].astype(f32).astype(bf16)
    k_codes = k_ref[...].astype(f32).astype(bf16)
    qw[...] = dot(q_codes, w_lo).astype(i32) | (dot(q_codes, w_hi).astype(i32) << 16)
    kw = dot(k_codes, w_lo).T.astype(i32) | (dot(k_codes, w_hi).T.astype(i32) << 16)
    for r in range(96):
        for j in range(2):
            kb[r, j] = jnp.broadcast_to(kw[r : r + 1, j * 128 : j * 128 + 128], (8, 128))
    low7 = jnp.int32(0x7F7F7F7F)
    ones = jnp.int32(0x01010101)
    byte2 = jnp.int32(0x00FF00FF)
    tile_rows = 16
    groups = tile_rows // 8

    def tile(rt, carry):
        rs = pl.ds(pl.multiple_of(rt * tile_rows, tile_rows), tile_rows)
        qt = qw[rs, :]
        for h in range(HEADS):
            acc = [[jnp.zeros((8, 128), i32) for _ in range(2)] for _ in range(groups)]
            for g in range(8):
                c = h * 8 + g
                qc = [
                    jnp.broadcast_to(qt[t * 8 : t * 8 + 8, c : c + 1], (8, 128))
                    for t in range(groups)
                ]
                for j in range(2):
                    kk = kb[c, j]
                    for t in range(groups):
                        x = qc[t] ^ kk
                        y = ((x & low7) + low7) | x
                        acc[t][j] = acc[t][j] + (lax.shift_right_logical(y, 7) & ones)
            for j in range(2):
                parts = []
                for t in range(groups):
                    z = acc[t][j]
                    z = (z & byte2) + (lax.shift_right_logical(z, 8) & byte2)
                    z = (z & jnp.int32(0xFFFF)) + lax.shift_right_logical(z, 16)
                    parts.append((SETS - z).astype(f32))
                m = jnp.concatenate(parts, axis=0) * jn[rs, j * 128 : j * 128 + 128]
                col_ref[h, rs, j * 128 : j * 128 + 128] = m.astype(bf16)
        return carry

    lax.fori_loop(0, ROWS // tile_rows, tile, 0)

    col_ref.leave()

    dims = (FREQ, ROWS)
    f = lax.broadcasted_iota(i32, dims, 0)
    p = lax.broadcasted_iota(i32, dims, 1)
    c, s = turn(f * (p + MARGIN * segment_of(p, ends)))
    ok = f < LIVE_FREQ
    wave_ref[0:FREQ] = jnp.where(ok, c, 0.0).astype(bf16)
    wave_ref[FREQ:] = jnp.where(ok, s, 0.0).astype(bf16)
    p = lax.broadcasted_iota(i32, dims, 0)
    f = lax.broadcasted_iota(i32, dims, 1)
    c, s = turn(f * (p + MARGIN * segment_of(p, ends)))
    ok = f < LIVE_FREQ
    wavet_ref[:, 0:FREQ] = jnp.where(ok, c, 0.0).astype(bf16)
    wavet_ref[:, FREQ:] = jnp.where(ok, s, 0.0).astype(bf16)
    dims = (FREQ, 128)
    f = lax.broadcasted_iota(i32, dims, 0)
    c, s = turn(f * (lax.broadcasted_iota(i32, dims, 1) - MARGIN))
    tap_c = c.astype(bf16)
    tap_s = s.astype(bf16)
    dims = (128, FREQ)
    f = lax.broadcasted_iota(i32, dims, 1)
    c, s = turn(f * (lax.broadcasted_iota(i32, dims, 0) - MARGIN))
    tapt_ref[:, 0:FREQ] = c.astype(bf16)
    tapt_ref[:, FREQ:] = s.astype(bf16)
    tapbuf[...] = jnp.zeros(tapbuf.shape, f32)
    tapbuf[0:TAPS] = taps_ref[...].astype(f32)
    kernel = tapbuf[...].astype(bf16)
    f = lax.broadcasted_iota(i32, (FREQ, 1), 0)
    weight = jnp.where((f == 0) | (f == DFT_LEN // 2), 1.0 / DFT_LEN, 2.0 / DFT_LEN)
    weight = jnp.where(f < LIVE_FREQ, weight, 0.0)
    k_cos = dot(tap_c, kernel) * weight
    k_sin = dot(tap_s, kernel) * weight
    ks_ref[0:FREQ] = k_cos
    ks_ref[FREQ:] = k_sin

    live = jnp.broadcast_to(live_ref[...].astype(f32), (8, ROWS)).T[:, 0:1]
    live_out[...] = jnp.broadcast_to(live, (ROWS, 128))
    values = (dot(x_ref[...], wv_ref[...]) + bv_ref[...].astype(f32)).astype(bf16).astype(f32)
    mskd[...] = (values * live).astype(bf16)
    masked = mskd[...]
    spec = dot(wave_ref[...], masked)
    vs_ref[...] = spec.astype(bf16)
    v_cos = spec[0:FREQ]
    v_sin = spec[FREQ:]
    first_head = lanes((ROWS, 128)) < HEAD_DIM
    y_cos = (k_cos * v_cos + k_sin * v_sin).astype(bf16)
    y_sin = (k_cos * v_sin - k_sin * v_cos).astype(bf16)
    conv = dot(wavet_ref[:, 0:FREQ], y_cos) + dot(wavet_ref[:, FREQ:], y_sin)
    for done in (wave_ref, wavet_ref, tapt_ref, ks_ref, live_out, vs_ref):
        done.leave()

    def heads(b, carry):
        cs = pl.ds(pl.multiple_of(b * 128, 128), 128)
        block = mskd[:, cs]
        m = jnp.where(first_head, dot(col_ref[2 * b], block), dot(col_ref[2 * b + 1], block))
        sq = m * m
        one = jnp.sum(jnp.where(first_head, sq, 0.0), axis=1, keepdims=True)
        two = jnp.sum(jnp.where(first_head, 0.0, sq), axis=1, keepdims=True)
        scale = lax.rsqrt(jnp.where(first_head, one, two) * (1.0 / HEAD_DIM) + 1e-06)
        scl_ref[:, cs] = scale
        nrm = m * scale
        nrm_ref[:, cs] = nrm.astype(bf16)
        mix[:, cs] = nrm
        return carry

    lax.fori_loop(0, COLS, heads, 0)
    context = (mix[...] + conv).astype(bf16)
    ctx_ref[...] = context
    for done in (scl_ref, nrm_ref, ctx_ref):
        done.leave()
    attended = dot(context, wo_ref[...]) + bo_ref[...].astype(f32)
    n, inv = norm_rows(x_ref[...].astype(f32) + attended)
    n_ref[...] = n
    inv_ref[...] = jnp.broadcast_to(inv, (ROWS, 128))
    low = (n * ga_ref[...].astype(f32) + sa_ref[...].astype(f32)).astype(bf16)
    low_ref[...] = low
    low_a[...] = low[0:HALF]
    low_b[...] = low[HALF:]


def attend(seq_lengths, x, wv, bv, taps, wo, bo, ga, sa, q, k, live):
    wide = (ROWS, WIDTH)
    half = (HALF, WIDTH)
    h = "hbm"
    v = "vmem"
    return staged_call(
        attend_kernel, "attend", 36,
        [
            ("smem", seq_lengths), (h, x), (h, wv), (v, bv), (v, taps), (h, wo), (v, bo), (v, ga),
            (v, sa), (h, q), (h, k), (v, live),
        ],
        [
            (h, shape(wide, f32)), (h, shape((ROWS, 128), f32)), (v, shape(wide, bf16)),
            (v, shape(half, bf16)), (v, shape(half, bf16)), (h, shape(wide, bf16)),
            (h, shape((HEADS, ROWS, ROWS), bf16)), (h, shape(wide, bf16)), (h, shape(wide, f32)),
            (h, shape((2 * FREQ, ROWS), bf16)), (h, shape((ROWS, 2 * FREQ), bf16)),
            (h, shape((2 * FREQ, WIDTH), f32)), (h, shape((2 * FREQ, WIDTH), bf16)),
            (h, shape((128, 2 * FREQ), bf16)), (h, shape((ROWS, 128), f32)),
        ],
        [
            pltpu.VMEM((ROWS, 128), i32),
            pltpu.VMEM((96, 2, 8, 128), i32),
            pltpu.VMEM((ROWS, ROWS), f32),
            pltpu.VMEM((128, WIDTH), f32),
            pltpu.VMEM(wide, f32),
            pltpu.VMEM(wide, bf16),
        ],
    )


def unpack(ref, m, out):
    for a in range(PIECES):
        rs = slice(a * 192, a * 192 + 192)
        for ct in range(COLS):
            first = 3 * (ct % 3)
            part = ref[m, a, ct // 3, :, first : first + 3].astype(f32)
            out[rs, ct * 128 : ct * 128 + 128] = part.reshape(192, 128).astype(bf16)


def unpack_bias(ref, out):
    for a in range(PIECES):
        tile = ref[0, a, 0, :, UNITS - 1].astype(f32)
        lane = lanes(tile.shape)
        parts = [jnp.where(lane == rt, tile, 0.0)[:, None] for rt in range(3)]
        column = jnp.concatenate(parts, axis=1).reshape(192, 128)
        out[a * 192 : a * 192 + 192, WIDTH:] = column.astype(bf16)


def ffn_blocks(rows, wu, wd, act, slope, acc):
    acc[...] = jnp.zeros(acc.shape, f32)

    def block(i, carry):
        hs = pl.ds(pl.multiple_of(i * 256, 256), 256)
        upper = dot_last(rows[...], wu[hs, :])
        cdf = 0.5 * (1.0 + lax.erf(upper * math.sqrt(0.5)))
        a = (upper * cdf).astype(bf16)
        act[:, hs] = a
        density = jnp.exp(-0.5 * upper * upper) * (1.0 / math.sqrt(2.0 * math.pi))
        slope[:, hs] = (cdf + upper * density).astype(bf16)
        acc[...] += dot(a, wd[hs, :])
        return carry

    lax.fori_loop(0, HIDDEN // 256, block, 0)


def unpack_kernel(w, wu, wd):
    unpack(w, 0, wu)
    unpack_bias(w, wu)
    unpack(w, 1, wd)


def unpack_weights(weights):
    return staged_call(
        unpack_kernel, "unpack", 12, [("pair", weights)],
        [("vmem", shape((HIDDEN, WIDTH + 128), bf16)), ("vmem", shape((HIDDEN, WIDTH), bf16))],
    )


def ffn_far_kernel(
    got_a, got_b, sib_a, sib_b, wu, wd, act, slope, part_own, part_sib, rows_out, rows, acc,
):
    for i, ref in enumerate((got_a, got_b, sib_a, sib_b)):
        rows[i * HALF : i * HALF + HALF, 0:WIDTH] = ref[...]
    rows[:, WIDTH:] = jnp.where(lanes((2 * ROWS, 128)) < 3, 1.0, 0.0).astype(bf16)
    rows_out[...] = rows[:, 0:WIDTH]
    ffn_blocks(rows, wu, wd, act, slope, acc)
    part_own[...] = acc[0:ROWS]
    part_sib[...] = acc[ROWS:].astype(bf16)


def ffn_near_kernel(own, sib, wu, wd, act, slope, part_own, part_sib, rows_out, rows, acc):
    rows[0:ROWS, 0:WIDTH] = own[...]
    rows[ROWS:, 0:WIDTH] = sib[...]
    rows[:, WIDTH:] = jnp.where(lanes((2 * ROWS, 128)) < 3, 1.0, 0.0).astype(bf16)
    rows_out[...] = rows[:, 0:WIDTH]
    ffn_blocks(rows, wu, wd, act, slope, acc)
    part_own[...] = acc[0:ROWS]
    part_sib[...] = acc[ROWS:].astype(bf16)


def ffn_call(kernel, name, *args):
    wide = (ROWS, WIDTH)
    tall = shape((2 * ROWS, WIDTH), bf16)
    outs = (tall, tall, shape(wide, f32), shape(wide, bf16), tall)
    return staged_call(
        kernel, name, 20, [("vmem", a) for a in args], [("vmem", o) for o in outs],
        [pltpu.VMEM((2 * ROWS, WIDTH + 128), bf16), pltpu.VMEM((2 * ROWS, WIDTH), f32)],
    )


def combine_kernel(own, got, out_a, out_b):
    total = (own[...] + got[...].astype(f32)).astype(bf16)
    out_a[...] = total[0:HALF]
    out_b[...] = total[HALF:]


def combine(own, got):
    half = shape((HALF, WIDTH), bf16)
    return pl.pallas_call(
        combine_kernel,
        out_shape=(half, half),
        in_specs=[VMEM] * 2,
        out_specs=(VMEM,) * 2,
        compiler_params=params(32),
        name="combine",
    )(own, got)


def gather_rows(own, near, far_a, far_b):
    far = jnp.concatenate([far_a[...], far_b[...]], axis=0)
    return own[...] + near[...].astype(f32) + far.astype(f32)


def second_norm(n1, own, near, far_a, far_b, bd, ga, sa, gf, og):
    first = n1[...] * ga[...].astype(f32) + sa[...].astype(f32)
    n, inv = norm_rows(first + gather_rows(own, near, far_a, far_b) + bd[...].astype(f32))
    g = og[...].astype(f32)
    return n, g, norm_back(g, n, inv, gf[...].astype(f32))


def middle_kernel(n1, own, near, far_a, far_b, bd, ga, sa, gf, og, low, low_a, low_b):
    grad = second_norm(n1, own, near, far_a, far_b, bd, ga, sa, gf, og)[2].astype(bf16)
    low[...] = grad
    low_a[...] = grad[0:HALF]
    low_b[...] = grad[HALF:]


def middle(*args):
    wide = shape((ROWS, WIDTH), bf16)
    half = shape((HALF, WIDTH), bf16)
    return pl.pallas_call(
        middle_kernel,
        out_shape=(wide, half, half),
        in_specs=[VMEM] * len(args),
        out_specs=(VMEM,) * 3,
        compiler_params=params(16),
        name="middle",
    )(*args)


def outputs_kernel(
    n1, own, near, far_a, far_b, bd, ga, sa, gf, og, sf, out, second, sums,
):
    n, g, grad = second_norm(n1, own, near, far_a, far_b, bd, ga, sa, gf, og)
    out[...] = (n * gf[...].astype(f32) + sf[...].astype(f32)).astype(bf16)
    second[...] = grad
    sums[0:1] = jnp.sum(grad.astype(bf16).astype(f32), axis=0, keepdims=True)
    sums[1:2] = jnp.sum(g * n, axis=0, keepdims=True)
    sums[2:3] = jnp.sum(g, axis=0, keepdims=True)
    sums[3:8] = jnp.zeros((5, WIDTH), f32)


def outputs(*args):
    wide = (ROWS, WIDTH)
    return staged_call(
        outputs_kernel, "outputs", 16, [("vmem", a) for a in args],
        [("hbm", shape(wide, bf16)), ("hbm", shape(wide, f32)), ("hbm", shape((8, WIDTH), f32))],
    )


def back_blocks(g, wu, wd, slope, u_out, bias, acc):
    acc[...] = jnp.zeros(acc.shape, f32)
    bias[...] = jnp.zeros((8, HIDDEN), f32)

    def block(i, carry):
        hs = pl.ds(pl.multiple_of(i * 256, 256), 256)
        u = (dot_last(g[...], wd[hs, :]) * slope[:, hs].astype(f32)).astype(bf16)
        u_out[:, hs] = u
        bias[0:1, hs] = jnp.sum(u.astype(f32), axis=0, keepdims=True)
        acc[...] += dot(u, wu[hs, 0:WIDTH])
        return carry

    lax.fori_loop(0, HIDDEN // 256, block, 0)


def back_near_kernel(own, sib, wu, wd, slope, first_own, first_sib, g, u, bias, acc):
    g[0:ROWS] = own[...]
    g[ROWS:] = sib[...]
    back_blocks(g, wu, wd, slope, u, bias, acc)
    first_own[...] = acc[0:ROWS]
    first_sib[...] = acc[ROWS:].astype(bf16)


def back_far_kernel(
    got_a, got_b, sib_a, sib_b, wu, wd, slope, first_own, first_sib, g, u, bias, acc,
):
    for i, ref in enumerate((got_a, got_b, sib_a, sib_b)):
        g[i * HALF : i * HALF + HALF] = ref[...]
    back_blocks(g, wu, wd, slope, u, bias, acc)
    first_own[...] = acc[0:ROWS]
    first_sib[...] = acc[ROWS:].astype(bf16)


def back_call(kernel, name, *args):
    wide = (ROWS, WIDTH)
    tall = shape((2 * ROWS, WIDTH), bf16)
    return staged_call(
        kernel, name, 20, [("vmem", a) for a in args],
        [
            ("hbm" if name == "back_near" else "vmem", shape(wide, f32)), ("vmem", shape(wide, bf16)),
            ("vmem", tall), ("vmem", tall), ("hbm", shape((8, HIDDEN), f32)),
        ],
        [pltpu.VMEM((2 * ROWS, WIDTH), f32)],
    )


def pack_kernel(gu, gd, grads):
    def piece(a, carry):
        rs = pl.ds(pl.multiple_of(a * 192, 192), 192)
        for m, ref in enumerate((gu, gd)):
            for ct in range(COLS):
                us = slice(3 * (ct % 3), 3 * (ct % 3) + 3)
                part = ref[rs, ct * 128 : ct * 128 + 128].astype(f32).reshape(8, 3, 8, 128)
                grads[m, a, ct // 3, :, us] = part.astype(bf16)
        return carry

    lax.fori_loop(0, PIECES, piece, 0)


def pack(*args):
    return staged_call(
        pack_kernel, "pack", 12, [("vmem", a) for a in args],
        [("hbm", shape((2, PIECES, 2, 8, GRAD_UNITS, 8, 128), bf16))],
    )[0]


def back_kernel(
    place, own, near, far_a, far_b, second, n1, inv1, ga, ctx, wo, nrm, scl, wave, wavet, ks, vs, tapt, col, live, x,
    wv, sums, bias_n, bias_f, in_grad, keep, give, buf_a, buf_b, mb,
):
    first_grad = second[...] + gather_rows(own, near, far_a, far_b)
    n = n1[...]
    buf_a[768 + 2 : 768 + 3] = jnp.sum(first_grad * n, axis=0, keepdims=True)
    buf_a[768 + 3 : 768 + 4] = jnp.sum(first_grad, axis=0, keepdims=True)
    resid = norm_back(first_grad, n, inv1[...][:, 0:1], ga[...].astype(f32))
    ag = resid.astype(bf16)
    buf_a[768 + 1 : 768 + 2] = jnp.sum(ag.astype(f32), axis=0, keepdims=True)
    buf_a[768 + 4 : 768 + 7] = sums[0:3]
    buf_a[768 + 7 :] = jnp.zeros((TALL - 775, WIDTH), f32)
    mine = lax.broadcasted_iota(i32, (8, WIDTH), 0) == place[0] % CLASSES
    bias = jnp.broadcast_to(bias_n[0:1] + bias_f[0:1], (8, WIDTH))
    buf_a[776:784] = jnp.where(mine, bias, 0.0)
    buf_b[0:768] = dot_first(ctx[...], ag)
    cg = dot_last(ag, wo[...])
    mb[...] = cg
    first_head = lanes((ROWS, 128)) < HEAD_DIM
    nrm.ready()
    scl.ready()
    col.ready()

    def heads(b, carry):
        cs = pl.ds(pl.multiple_of(b * 128, 128), 128)
        c = mb[:, cs]
        m = nrm[:, cs].astype(f32)
        prod = c * m
        one = jnp.sum(jnp.where(first_head, prod, 0.0), axis=1, keepdims=True)
        two = jnp.sum(jnp.where(first_head, 0.0, prod), axis=1, keepdims=True)
        mean = jnp.where(first_head, one, two) * (1.0 / HEAD_DIM)
        block = (scl[:, cs] * (c - m * mean)).astype(bf16)
        mb[:, cs] = jnp.where(
            first_head, dot_first(col[2 * b], block), dot_first(col[2 * b + 1], block)
        )
        return carry

    lax.fori_loop(0, COLS, heads, 0)
    spec = dot(wave[...], cg.astype(bf16))
    g_cos = spec[0:FREQ]
    g_sin = spec[FREQ:]
    k_cos = ks[0:FREQ]
    k_sin = ks[FREQ:]
    z_cos = (k_cos * g_cos - k_sin * g_sin).astype(bf16)
    z_sin = (k_cos * g_sin + k_sin * g_cos).astype(bf16)
    conv = dot(wavet[:, 0:FREQ], z_cos) + dot(wavet[:, FREQ:], z_sin)
    v_cos = vs[0:FREQ].astype(f32)
    v_sin = vs[FREQ:].astype(f32)
    f = lax.broadcasted_iota(i32, (FREQ, 1), 0)
    weight = jnp.where((f == 0) | (f == DFT_LEN // 2), 1.0 / DFT_LEN, 2.0 / DFT_LEN)
    weight = jnp.where(f < LIVE_FREQ, weight, 0.0)
    re = ((g_cos * v_cos + g_sin * v_sin) * weight).astype(bf16)
    im = ((g_cos * v_sin - g_sin * v_cos) * weight).astype(bf16)
    gk = dot(tapt[:, 0:FREQ], re) + dot(tapt[:, FREQ:], im)
    buf_b[768:] = jnp.zeros((TALL - 768, WIDTH), f32)
    buf_b[768 : 768 + TAPS] = gk[0:TAPS]
    vg = ((mb[...] + conv) * live[...][:, 0:1]).astype(bf16)
    buf_a[768:769] = jnp.sum(vg.astype(f32), axis=0, keepdims=True)
    buf_a[0:768] = dot_first(x[...], vg)
    in_grad[...] = resid + dot_last(vg, wv[...])

    def write(kept, given):
        for ct in range(COLS):
            cs = slice(ct * 128, ct * 128 + 128)
            ts = slice(ct * TALL_TILES, ct * TALL_TILES + TALL_TILES)
            keep[ts] = kept[:, cs].reshape(TALL_TILES, 8, 128).astype(bf16)
            give[ts] = given[:, cs].reshape(TALL_TILES, 8, 128).astype(bf16)

    rest = PACK - COLS * TALL_TILES
    keep[PACK - rest :] = jnp.zeros((rest, 8, 128), bf16)
    give[PACK - rest :] = jnp.zeros((rest, 8, 128), bf16)

    @pl.when(place[0] % 2 == 0)
    def _():
        write(buf_a, buf_b)

    @pl.when(place[0] % 2 == 1)
    def _():
        write(buf_b, buf_a)


def attend_back(*args):
    wide = (ROWS, WIDTH)
    packed = shape((PACK, 8, 128), bf16)
    kinds = ["smem"] + ["hbm"] * (len(args) - 1)
    for i in (2, 3, 4, 8):
        kinds[i] = "vmem"
    return staged_call(
        back_kernel, "attend_back", 40, list(zip(kinds, args, strict=True)),
        [("hbm", shape(wide, f32)), ("vmem", packed), ("vmem", packed)],
        [
            pltpu.VMEM((TALL, WIDTH), f32),
            pltpu.VMEM((TALL, WIDTH), f32),
            pltpu.VMEM(wide, f32),
        ],
    )


def sum_ffn_kernel(got, out, acc):
    step = pl.program_id(0)

    @pl.when(step == 0)
    def _():
        acc[...] = jnp.zeros(acc.shape, f32)

    for q in range(CLASSES):
        total = acc[q]
        for t in range(8):
            total = total + got[q * 8 + t].astype(f32)
        acc[q] = total

    @pl.when(step == 3)
    def _():
        out[...] = acc[...].astype(bf16)


def sum_ffn(got):
    return pl.pallas_call(
        sum_ffn_kernel,
        grid=(4,),
        out_shape=shape((CLASSES, GRAD_UNITS, 8, 128), bf16),
        in_specs=[pl.BlockSpec((32, GRAD_UNITS, 8, 128), lambda i: (i, 0, 0, 0))],
        out_specs=pl.BlockSpec((CLASSES, GRAD_UNITS, 8, 128), lambda i: (0, 0, 0, 0)),
        scratch_shapes=[pltpu.VMEM((CLASSES, GRAD_UNITS, 8, 128), f32)],
        compiler_params=params(32),
        name="sum_ffn",
    )(got)


def sum_rest_kernel(got, out):
    per = PACK // 128
    total = [jnp.zeros((per, 8, 128), f32) for _ in range(2)]
    for i in range(8):
        for c in range(2):
            for t in range(8):
                total[c] = total[c] + got[i * 16 + c * 8 + t].astype(f32)
    low = [t.astype(bf16) for t in total]
    for i in range(8):
        for c in range(2):
            for t in range(8):
                out[i * 16 + c * 8 + t] = low[c]


def sum_rest(got):
    return pl.pallas_call(
        sum_rest_kernel,
        out_shape=shape(got.shape, bf16),
        in_specs=[VMEM],
        out_specs=VMEM,
        compiler_params=params(32),
        name="sum_rest",
    )(got)


def final_ffn_kernel(place, ffn_own, ffn_oth, g_up, g_down, tall):
    ct = pl.program_id(0)
    core = place[0] % 2

    def index(m, a):
        return (m + place[0] // 8) % 2 * 4 + (place[0] // 2 % 4 + 4 - a) % 4

    def spread(ref):
        for a in range(PIECES):
            up = ref[index(0, a)].astype(f32)
            down = ref[index(1, a)].astype(f32)
            for q in range(CLASSES):
                rs = slice(SUB * q + PIECE * a, SUB * q + PIECE * a + PIECE)
                tall[rs, :] = up[q].reshape(PIECE, 128)
                g_down[rs, :] = down[q].reshape(PIECE, 128)

    @pl.when(ct // 3 == core)
    def _():
        spread(ffn_own)

    @pl.when(ct // 3 != core)
    def _():
        spread(ffn_oth)

    g_up[...] = tall[...].T


def final_ffn(place, ffn_own, ffn_oth):
    units = pl.BlockSpec((8, CLASSES, 3, 8, 128), lambda i: (0, 0, i % 3, 0, 0))
    return pl.pallas_call(
        final_ffn_kernel,
        grid=(COLS,),
        out_shape=(shape((768, 384), f32), shape((384, 768), f32)),
        in_specs=[SMEM, units, units],
        out_specs=(
            pl.BlockSpec((128, 384), lambda i: (i, 0)),
            pl.BlockSpec((384, 128), lambda i: (0, i)),
        ),
        scratch_shapes=[pltpu.VMEM((384, 128), f32)],
        compiler_params=params(16),
        name="final_ffn",
    )(place, ffn_own, ffn_oth)


def final_kernel(
    place, own, other, g_wv, g_bv, g_conv, g_wo, g_bo, g_ga, g_sa, g_bup, g_bd, g_gf, g_sf, vecs,
    bias, line,
):
    ct = pl.program_id(0)

    def write(a, b):
        g_wv[...] = a[0:96].astype(f32).reshape(768, 128)
        vecs[ct] = a[96].astype(f32)
        bias[ct] = a[97].astype(f32)
        g_wo[...] = b[0:96].astype(f32).reshape(768, 128)
        g_conv[...] = b[96:105].astype(f32).reshape(72, 128)[0:TAPS]

    @pl.when(place[0] % 2 == 0)
    def _():
        write(own, other)

    @pl.when(place[0] % 2 == 1)
    def _():
        write(other, own)

    @pl.when(ct == COLS - 1)
    def _():
        for j, ref in enumerate((g_bv, g_bo, g_ga, g_sa, g_bd, g_gf, g_sf)):
            for i in range(COLS):
                ref[i * 128 : i * 128 + 128] = vecs[i, j]
        n = lanes((128, 128))
        a = (n >= PIECE).astype(i32) + (n >= 2 * PIECE).astype(i32) + (n >= 3 * PIECE).astype(i32)
        at = (8 * a + place[1]) * PIECE + n - PIECE * a
        total = jnp.zeros((8, 128), f32)
        for i in range(COLS):
            pick = lax.broadcasted_iota(i32, (128, 128), 0) + 128 * i == at
            total = total + dot(bias[i].astype(bf16), jnp.where(pick, 1.0, 0.0).astype(bf16))
        for q in range(CLASSES):
            line[0:1, SUB * q : SUB * q + SUB] = total[q : q + 1, 0:SUB]
        g_bup[...] = line[...][0]


def final(place, own, other):
    tile = pl.BlockSpec((TALL_TILES, 8, 128), lambda i: (i, 0, 0))
    tall = pl.BlockSpec((768, 128), lambda i: (0, i))
    vec = pl.BlockSpec((WIDTH,), lambda i: (0,))
    v = shape((WIDTH,), f32)
    return pl.pallas_call(
        final_kernel,
        grid=(COLS,),
        out_shape=(
            shape((768, 768), f32), v, shape((TAPS, 768), f32), shape((768, 768), f32), v, v, v,
            shape((384,), f32), v, v, v,
        ),
        in_specs=[SMEM, tile, tile],
        out_specs=(
            tall, vec, pl.BlockSpec((TAPS, 128), lambda i: (0, i)), tall, vec, vec, vec,
            pl.BlockSpec((384,), lambda i: (0,)), vec, vec, vec,
        ),
        scratch_shapes=[
            pltpu.VMEM((COLS, 8, 128), f32),
            pltpu.VMEM((COLS, 8, 128), f32),
            pltpu.VMEM((1, 384), f32),
        ],
        compiler_params=params(16),
        name="final",
    )(place, own, other)


def body(
    block_input,
    w_value,
    b_value,
    conv_kernel,
    w_out,
    b_out,
    gain_attn,
    shift_attn,
    w_up,
    b_up,
    w_down,
    b_down,
    gain_ffn,
    shift_ffn,
    query_codes,
    key_codes,
    key_live,
    seq_lengths,
    out_grad,
):
    dp = lax.axis_index("dp")
    place = jnp.stack([dp, lax.axis_index("tensor")]).astype(i32)
    n_dp = lax.axis_size("dp")

    def shift(i, by):
        return i // 8 * 8 + (i // 2 + by) % 4 * 2 + i % 2

    def swap(x):
        return lax.ppermute(x, "dp", [(i, i ^ 1) for i in range(n_dp)])

    def ahead(x):
        return lax.ppermute(x, "dp", [(i, shift(i, 1)) for i in range(n_dp)])

    def behind(x):
        return lax.ppermute(x, "dp", [(i, shift(i, -1)) for i in range(n_dp)])

    def exchange(x):
        return lax.all_to_all(x, ALL, 0, 0, tiled=True)

    def row(v):
        return v.reshape(1, -1)

    weights = exchange(prep(place, w_up, w_down, b_up))
    weights = weights.reshape(2, PIECES, 2, 8, UNITS, 8, 128)
    (n1, inv1, low, low_a, low_b, ctx, collide, nrm, scl, wave, wavet, ks, vs, tapt, live) = attend(
        seq_lengths, block_input, w_value, row(b_value), conv_kernel, w_out, row(b_out),
        row(gain_attn), row(shift_attn), query_codes, key_codes, row(key_live),
    )
    low_sib = swap(low)
    row_a, row_b = ahead(low_a), behind(low_b)
    wu, wd = unpack_weights(weights)
    act_f, slope_f, far_own, far_sib, rows_f = ffn_call(
        ffn_far_kernel, "ffn_far", row_a, row_b, swap(row_a), swap(row_b), wu, wd
    )
    sent_a, sent_b = combine(far_own, swap(far_sib))
    wu, sent_a, sent_b = lax.optimization_barrier((wu, sent_a, sent_b))
    act_n, slope_n, near_own, near_sib, rows_n = ffn_call(
        ffn_near_kernel, "ffn_near", low, low_sib, wu, wd
    )
    back_a, back_b = behind(sent_a), ahead(sent_b)
    near_sib, back_a, back_b = lax.optimization_barrier((near_sib, back_a, back_b))
    second_args = (
        n1, near_own, swap(near_sib), back_a, back_b, row(b_down), row(gain_attn), row(shift_attn),
        row(gain_ffn), out_grad,
    )
    grad, grad_a, grad_b = middle(*second_args)
    got_a, got_b = ahead(grad_a), behind(grad_b)
    near_own, near_sib, g_n, u_n, bias_n = back_call(
        back_near_kernel, "back_near", grad, swap(grad), wu, wd, slope_n
    )
    block_output, second, sums = outputs(*second_args, row(shift_ffn))
    got_a, got_b, near_sib, second = lax.optimization_barrier((got_a, got_b, near_sib, second))
    far_own, far_sib, g_f, u_f, bias_f = back_call(
        back_far_kernel, "back_far", got_a, got_b, swap(got_a), swap(got_b), wu, wd, slope_f
    )
    sent_a, sent_b = combine(far_own, swap(far_sib))
    u_f, sent_a, sent_b = lax.optimization_barrier((u_f, sent_a, sent_b))
    grad_down = (dot_first(act_n, g_n) + dot_first(act_f, g_f)).astype(bf16)
    grad_up = (dot_first(u_n, rows_n) + dot_first(u_f, rows_f)).astype(bf16)
    grads = pack(grad_up, grad_down)
    back_a, back_b = behind(sent_a), ahead(sent_b)
    grads, back_a, back_b = lax.optimization_barrier((grads, back_a, back_b))
    owned = exchange(grads.reshape(128, GRAD_UNITS, 8, 128))
    input_grad, keep, give = attend_back(
        place, near_own, swap(near_sib), back_a, back_b, second, n1, inv1,
        row(gain_attn), ctx, w_out, nrm, scl, wave, wavet, ks, vs, tapt, collide, live, block_input,
        w_value, sums, bias_n, bias_f,
    )
    pair = (keep.astype(f32) + swap(give).astype(f32)).astype(bf16)
    pair = pair.reshape(128, PACK // 128, 8, 128)
    owned = sum_ffn(owned)
    pair, owned = lax.optimization_barrier((pair, owned))
    around = []
    for side in range(2):
        for by in range(4):
            if side or by:
                pairs = [(i, (i // 8 + side) % 2 * 8 + shift(i % 8, by)) for i in range(n_dp)]
                around.append(lax.ppermute(owned, "dp", pairs))
    summed = sum_rest(exchange(pair))
    summed, *around = lax.optimization_barrier((summed, *around))
    back = exchange(summed).reshape(PACK, 8, 128)
    ffn_own = jnp.stack([owned, *around])
    g_up, g_down = final_ffn(place, ffn_own, swap(ffn_own))
    back, g_up, g_down = lax.optimization_barrier((back, g_up, g_down))
    g_wv, g_bv, g_conv, g_wo, g_bo, g_ga, g_sa, g_bup, g_bd, g_gf, g_sf = final(
        place, back, swap(back)
    )
    return (
        block_output, input_grad, g_wv, g_bv, g_conv, g_wo, g_bo, g_ga, g_sa, g_up, g_bup, g_down,
        g_bd, g_gf, g_sf,
    )


def solution(mesh):
    rows = P(ALL, None)
    return jax.shard_map(
        body,
        mesh=mesh,
        in_specs=(
            rows, P(), P(), P(), P(), P(), P(), P(),
            P(None, "tensor"), P("tensor"), P("tensor", None), P(), P(), P(),
            rows, rows, P(ALL), rows, rows,
        ),
        out_specs=(
            rows, rows, P(), P(), P(), P(), P(), P(), P(),
            P(None, "tensor"), P("tensor"), P("tensor", None), P(), P(), P(),
        ),
        check_vma=False,
    )
```

```python
import math

import jax
import jax.numpy as jnp
from jax import lax
from jax.experimental import pallas as pl
from jax.experimental.pallas import tpu as pltpu
from jax.sharding import PartitionSpec as P

HEADS = 12
SETS = 32
ROWS = 256
WIDTH = 768
HEAD_DIM = 64
COLS = WIDTH // 128
TAPS = 65
MARGIN = 32
DFT_LEN = 384
FREQ = 256
LIVE_FREQ = DFT_LEN // 2 + 1
CLASSES = 4
SUB = 96
PIECE = 24
PIECES = SUB // PIECE
UNITS = 10
GRAD_UNITS = 9
HIDDEN = 768
TALL = 848
TALL_TILES = TALL // 8
PACK = 640
ALL = ("dp", "tensor")

bf16 = jnp.bfloat16
f32 = jnp.float32
i32 = jnp.int32

VMEM = pl.BlockSpec(memory_space=pltpu.VMEM)
SMEM = pl.BlockSpec(memory_space=pltpu.SMEM)
HBM = pl.BlockSpec(memory_space=pltpu.HBM)


def shape(dims, dtype):
    return jax.ShapeDtypeStruct(dims, dtype)


def params(mib):
    return pltpu.CompilerParams(vmem_limit_bytes=mib << 20)


def dot(a, b):
    return lax.dot_general(a, b, (((1,), (0,)), ((), ())), preferred_element_type=f32)


def dot_last(a, b):
    return lax.dot_general(a, b, (((1,), (1,)), ((), ())), preferred_element_type=f32)


def dot_first(a, b):
    return lax.dot_general(a, b, (((0,), (0,)), ((), ())), preferred_element_type=f32)


def lanes(dims):
    return lax.broadcasted_iota(i32, dims, len(dims) - 1)


def norm_rows(r):
    mean = jnp.mean(r, axis=-1, keepdims=True)
    centred = r - mean
    inv = lax.rsqrt(jnp.mean(centred * centred, axis=-1, keepdims=True) + 1e-05)
    return centred * inv, inv


def norm_back(g, n, inv, gain):
    e = g * gain
    return (
        e - jnp.mean(e, axis=-1, keepdims=True) - n * jnp.mean(e * n, axis=-1, keepdims=True)
    ) * inv


class Staged:
    def __init__(self, ref, buf, sem, incoming):
        pair = (ref, buf) if incoming else (buf, ref)
        self.buf = buf
        self.copy = pltpu.make_async_copy(*pair, sem)
        self.incoming = incoming
        self.pending = True
        if incoming:
            self.copy.start()

    def ready(self):
        if self.pending:
            self.copy.wait()
            self.pending = False

    def leave(self):
        if self.pending:
            self.copy.start()
            self.pending = False

    def __getitem__(self, index):
        if self.incoming:
            self.ready()
        return self.buf[index]

    def __setitem__(self, index, value):
        self.buf[index] = value


class StagedPair:
    def __init__(self, ref, buf, sems):
        self.buf = buf
        self.copies = [pltpu.make_async_copy(ref.at[i], buf.at[i], sems.at[i]) for i in range(2)]
        self.pending = [True, True]
        for copy in self.copies:
            copy.start()

    def ready(self):
        for i in range(2):
            if self.pending[i]:
                self.copies[i].wait()
                self.pending[i] = False

    def __getitem__(self, index):
        i = index[0]
        if self.pending[i]:
            self.copies[i].wait()
            self.pending[i] = False
        return self.buf[index]


def staged_call(kernel, name, mib, ins, outs, scratch=()):
    spec = {"smem": SMEM, "vmem": VMEM, "hbm": HBM, "pair": HBM}
    arrays = [a for _, a in ins]
    kinds = [k for k, _ in ins] + [k for k, _ in outs]
    avals = arrays + [o for _, o in outs]
    staged = [i for i, k in enumerate(kinds) if k in ("hbm", "pair")]
    n_in = len(ins)

    if not staged:
        return pl.pallas_call(
            kernel,
            out_shape=tuple(o for _, o in outs),
            in_specs=[spec[k] for k, _ in ins],
            out_specs=tuple(spec[k] for k, _ in outs),
            scratch_shapes=list(scratch),
            compiler_params=params(mib),
            name=name,
        )(*arrays)

    def run(*refs):
        refs = list(refs)
        sems = refs.pop()
        split = len(refs) - len(staged)
        bufs = refs[split:]
        refs = refs[:split]
        for n, i in enumerate(staged):
            if kinds[i] == "pair":
                refs[i] = StagedPair(refs[i], bufs[n], sems.at[n])
            else:
                refs[i] = Staged(refs[i], bufs[n], sems.at[n, 0], i < n_in)
        kernel(*refs)
        for i in staged:
            if i < n_in:
                refs[i].ready()
            else:
                refs[i].leave()
        for i in staged:
            if i >= n_in:
                refs[i].copy.wait()

    buffers = [pltpu.VMEM(avals[i].shape, avals[i].dtype) for i in staged]
    arrays = [
        a if k in ("smem", "vmem") else pltpu.with_memory_space_constraint(a, pltpu.HBM)
        for k, a in ins
    ]
    return pl.pallas_call(
        run,
        out_shape=tuple(pltpu.HBM(o.shape, o.dtype) if k == "hbm" else o for k, o in outs),
        in_specs=[spec[k] for k, _ in ins],
        out_specs=tuple(spec[k] for k, _ in outs),
        scratch_shapes=[*scratch, *buffers, pltpu.SemaphoreType.DMA((len(staged), 2))],
        compiler_params=params(mib),
        name=name,
    )(*arrays)


def prep_kernel(place, up_ref, down_ref, bias_hbm, out_ref, half, piece, bias_ref, sems):
    rep = place[0] % 8
    is_up = place[0] < 8
    at = pl.ds(pl.multiple_of(rep % 2 * 384, 128), 384)
    up = pltpu.make_async_copy(up_ref.at[at, :], half, sems.at[0])
    down = pltpu.make_async_copy(down_ref.at[:, at], half, sems.at[0])
    bias_copy = pltpu.make_async_copy(bias_hbm, bias_ref, sems.at[33])
    bias_copy.start()

    @pl.when(is_up)
    def _():
        up.start()

    @pl.when(jnp.logical_not(is_up))
    def _():
        down.start()

    n = lax.broadcasted_iota(i32, (SUB, 384), 0)
    q = sum((n >= PIECE * k).astype(i32) for k in range(1, CLASSES))
    unit = (SUB - PIECE) * q + n + PIECE * (rep // 2)
    pick = jnp.where(unit == lanes((SUB, 384)), 1.0, 0.0).astype(bf16)
    scale = jnp.where(is_up & (rep % 2 == 0), 1.0, 0.0)
    bias_copy.wait()
    bias = jnp.broadcast_to(bias_ref[...].astype(f32) * scale, (16, 384)).astype(bf16)
    column = dot_last(pick, bias)[:, 0:1]

    def fill(rows):
        for k in range(CLASSES):
            rs = slice(PIECE * k, PIECE * k + PIECE)
            for j in range(3):
                part = rows[rs, j * 128 : j * 128 + 128].reshape(3, 8, 128)
                piece[k, 3 * j : 3 * j + 3] = part.astype(bf16)
            col = jnp.broadcast_to(column[rs], (PIECE, 128)).reshape(3, 8, 128)
            lane = lanes((8, 128))
            tile = jnp.where(lane == 0, col[0], jnp.where(lane == 1, col[1], col[2]))
            piece[k, UNITS - 1] = tile.astype(bf16)

    @pl.when(is_up)
    def _():
        up.wait()
        fill(dot_last(pick, half[...]))

    @pl.when(jnp.logical_not(is_up))
    def _():
        down.wait()
        fill(dot(pick, half[...]))

    copies = [
        pltpu.make_async_copy(piece, out_ref.at[g, :, t], sems.at[1 + 8 * g + t])
        for g in range(4)
        for t in range(8)
    ]
    for copy in copies:
        copy.start()
    for copy in copies:
        copy.wait()


def prep(place, w_up, w_down, b_up):
    out = pl.pallas_call(
        prep_kernel,
        out_shape=pltpu.HBM((4, CLASSES, 8, UNITS, 8, 128), bf16),
        in_specs=[SMEM, HBM, HBM, HBM],
        out_specs=HBM,
        scratch_shapes=[
            pltpu.VMEM((384, 384), bf16),
            pltpu.VMEM((CLASSES, UNITS, 8, 128), bf16),
            pltpu.VMEM((384,), bf16),
            pltpu.SemaphoreType.DMA((34,)),
        ],
        compiler_params=params(16),
        name="prep",
    )(
        place,
        pltpu.with_memory_space_constraint(w_up, pltpu.HBM),
        pltpu.with_memory_space_constraint(w_down, pltpu.HBM),
        pltpu.with_memory_space_constraint(b_up, pltpu.HBM),
    )
    return out.reshape(128, UNITS, 8, 128)


def segment_ends(len_ref):
    e0 = len_ref[0, 0]
    e1 = e0 + len_ref[0, 1]
    return e0, e1, e1 + len_ref[0, 2]


def segment_of(p, ends):
    return sum((p >= e).astype(i32) for e in ends)


def turn(product):
    r = product.astype(f32) * (1.0 / DFT_LEN)
    m = product - DFT_LEN * jnp.round(r).astype(i32)
    x = m.astype(f32) * (2.0 * math.pi / DFT_LEN)
    z = x * x
    c = 1.0
    s = 1.0
    for k in range(8, 0, -1):
        c = 1.0 - z * c * (1.0 / ((2 * k - 1) * (2 * k)))
        s = 1.0 - z * s * (1.0 / ((2 * k) * (2 * k + 1)))
    return c, x * s


def attend_kernel(
    len_ref, x_ref, wv_ref, bv_ref, taps_ref, wo_ref, bo_ref, ga_ref, sa_ref, q_ref, k_ref, live_ref,
    n_ref, inv_ref, low_ref, ctx_ref, col_ref, nrm_ref, scl_ref, wave_ref, wavet_ref, ks_ref, vs_ref,
    tapt_ref, live_out, qw, kb, jn, tapbuf, mix, mskd,
):
    ends = segment_ends(len_ref)
    square = (ROWS, ROWS)
    rows_i = lax.broadcasted_iota(i32, square, 0)
    lanes_i = lax.broadcasted_iota(i32, square, 1)
    jn[...] = jnp.where(segment_of(rows_i, ends) == segment_of(lanes_i, ends), 1.0 / SETS, 0.0)
    d = lax.broadcasted_iota(i32, (384, 128), 0) - 4 * lax.broadcasted_iota(i32, (384, 128), 1)
    w_lo = jnp.where(d == 0, 1.0, jnp.where(d == 1, 256.0, 0.0)).astype(bf16)
    w_hi = jnp.where(d == 2, 1.0, jnp.where(d == 3, 256.0, 0.0)).astype(bf16)
    q_codes = q_ref[...].astype(f32).astype(bf16)
    k_codes = k_ref[...].astype(f32).astype(bf16)
    qw[...] = dot(q_codes, w_lo).astype(i32) | (dot(q_codes, w_hi).astype(i32) << 16)
    kw = dot(k_codes, w_lo).T.astype(i32) | (dot(k_codes, w_hi).T.astype(i32) << 16)
    for r in range(96):
        for j in range(2):
            kb[r, j] = jnp.broadcast_to(kw[r : r + 1, j * 128 : j * 128 + 128], (8, 128))
    low7 = jnp.int32(0x7F7F7F7F)
    ones = jnp.int32(0x01010101)
    byte2 = jnp.int32(0x00FF00FF)
    tile_rows = 16
    groups = tile_rows // 8

    def tile(rt, carry):
        rs = pl.ds(pl.multiple_of(rt * tile_rows, tile_rows), tile_rows)
        qt = qw[rs, :]
        for h in range(HEADS):
            acc = [[jnp.zeros((8, 128), i32) for _ in range(2)] for _ in range(groups)]
            for g in range(8):
                c = h * 8 + g
                qc = [
                    jnp.broadcast_to(qt[t * 8 : t * 8 + 8, c : c + 1], (8, 128))
                    for t in range(groups)
                ]
                for j in range(2):
                    kk = kb[c, j]
                    for t in range(groups):
                        x = qc[t] ^ kk
                        y = ((x & low7) + low7) | x
                        acc[t][j] = acc[t][j] + (lax.shift_right_logical(y, 7) & ones)
            for j in range(2):
                parts = []
                for t in range(groups):
                    z = acc[t][j]
                    z = (z & byte2) + (lax.shift_right_logical(z, 8) & byte2)
                    z = (z & jnp.int32(0xFFFF)) + lax.shift_right_logical(z, 16)
                    parts.append((SETS - z).astype(f32))
                m = jnp.concatenate(parts, axis=0) * jn[rs, j * 128 : j * 128 + 128]
                col_ref[h, rs, j * 128 : j * 128 + 128] = m.astype(bf16)
        return carry

    lax.fori_loop(0, ROWS // tile_rows, tile, 0)

    col_ref.leave()

    dims = (FREQ, ROWS)
    f = lax.broadcasted_iota(i32, dims, 0)
    p = lax.broadcasted_iota(i32, dims, 1)
    c, s = turn(f * (p + MARGIN * segment_of(p, ends)))
    ok = f < LIVE_FREQ
    wave_ref[0:FREQ] = jnp.where(ok, c, 0.0).astype(bf16)
    wave_ref[FREQ:] = jnp.where(ok, s, 0.0).astype(bf16)
    p = lax.broadcasted_iota(i32, dims, 0)
    f = lax.broadcasted_iota(i32, dims, 1)
    c, s = turn(f * (p + MARGIN * segment_of(p, ends)))
    ok = f < LIVE_FREQ
    wavet_ref[:, 0:FREQ] = jnp.where(ok, c, 0.0).astype(bf16)
    wavet_ref[:, FREQ:] = jnp.where(ok, s, 0.0).astype(bf16)
    dims = (FREQ, 128)
    f = lax.broadcasted_iota(i32, dims, 0)
    c, s = turn(f * (lax.broadcasted_iota(i32, dims, 1) - MARGIN))
    tap_c = c.astype(bf16)
    tap_s = s.astype(bf16)
    dims = (128, FREQ)
    f = lax.broadcasted_iota(i32, dims, 1)
    c, s = turn(f * (lax.broadcasted_iota(i32, dims, 0) - MARGIN))
    tapt_ref[:, 0:FREQ] = c.astype(bf16)
    tapt_ref[:, FREQ:] = s.astype(bf16)
    tapbuf[...] = jnp.zeros(tapbuf.shape, f32)
    tapbuf[0:TAPS] = taps_ref[...].astype(f32)
    kernel = tapbuf[...].astype(bf16)
    f = lax.broadcasted_iota(i32, (FREQ, 1), 0)
    weight = jnp.where((f == 0) | (f == DFT_LEN // 2), 1.0 / DFT_LEN, 2.0 / DFT_LEN)
    weight = jnp.where(f < LIVE_FREQ, weight, 0.0)
    k_cos = dot(tap_c, kernel) * weight
    k_sin = dot(tap_s, kernel) * weight
    ks_ref[0:FREQ] = k_cos
    ks_ref[FREQ:] = k_sin

    live = jnp.broadcast_to(live_ref[...].astype(f32), (8, ROWS)).T[:, 0:1]
    live_out[...] = jnp.broadcast_to(live, (ROWS, 128))
    values = (dot(x_ref[...], wv_ref[...]) + bv_ref[...].astype(f32)).astype(bf16).astype(f32)
    mskd[...] = (values * live).astype(bf16)
    masked = mskd[...]
    spec = dot(wave_ref[...], masked)
    vs_ref[...] = spec.astype(bf16)
    v_cos = spec[0:FREQ]
    v_sin = spec[FREQ:]
    first_head = lanes((ROWS, 128)) < HEAD_DIM
    y_cos = (k_cos * v_cos + k_sin * v_sin).astype(bf16)
    y_sin = (k_cos * v_sin - k_sin * v_cos).astype(bf16)
    conv = dot(wavet_ref[:, 0:FREQ], y_cos) + dot(wavet_ref[:, FREQ:], y_sin)
    for done in (wave_ref, wavet_ref, tapt_ref, ks_ref, live_out, vs_ref):
        done.leave()

    def heads(b, carry):
        cs = pl.ds(pl.multiple_of(b * 128, 128), 128)
        block = mskd[:, cs]
        m = jnp.where(first_head, dot(col_ref[2 * b], block), dot(col_ref[2 * b + 1], block))
        sq = m * m
        one = jnp.sum(jnp.where(first_head, sq, 0.0), axis=1, keepdims=True)
        two = jnp.sum(jnp.where(first_head, 0.0, sq), axis=1, keepdims=True)
        scale = lax.rsqrt(jnp.where(first_head, one, two) * (1.0 / HEAD_DIM) + 1e-06)
        scl_ref[:, cs] = scale
        nrm = m * scale
        nrm_ref[:, cs] = nrm.astype(bf16)
        mix[:, cs] = nrm
        return carry

    lax.fori_loop(0, COLS, heads, 0)
    context = (mix[...] + conv).astype(bf16)
    ctx_ref[...] = context
    for done in (scl_ref, nrm_ref, ctx_ref):
        done.leave()
    attended = dot(context, wo_ref[...]) + bo_ref[...].astype(f32)
    n, inv = norm_rows(x_ref[...].astype(f32) + attended)
    n_ref[...] = n
    inv_ref[...] = jnp.broadcast_to(inv, (ROWS, 128))
    low_ref[...] = (n * ga_ref[...].astype(f32) + sa_ref[...].astype(f32)).astype(bf16)


def attend(seq_lengths, x, wv, bv, taps, wo, bo, ga, sa, q, k, live):
    wide = (ROWS, WIDTH)
    h = "hbm"
    v = "vmem"
    return staged_call(
        attend_kernel, "attend", 36,
        [
            ("smem", seq_lengths), (h, x), (h, wv), (v, bv), (v, taps), (h, wo), (v, bo), (v, ga),
            (v, sa), (h, q), (h, k), (v, live),
        ],
        [
            (h, shape(wide, f32)), (h, shape((ROWS, 128), f32)), (v, shape(wide, bf16)),
            (h, shape(wide, bf16)),
            (h, shape((HEADS, ROWS, ROWS), bf16)), (h, shape(wide, bf16)), (h, shape(wide, f32)),
            (h, shape((2 * FREQ, ROWS), bf16)), (h, shape((ROWS, 2 * FREQ), bf16)),
            (h, shape((2 * FREQ, WIDTH), f32)), (h, shape((2 * FREQ, WIDTH), bf16)),
            (h, shape((128, 2 * FREQ), bf16)), (h, shape((ROWS, 128), f32)),
        ],
        [
            pltpu.VMEM((ROWS, 128), i32),
            pltpu.VMEM((96, 2, 8, 128), i32),
            pltpu.VMEM((ROWS, ROWS), f32),
            pltpu.VMEM((128, WIDTH), f32),
            pltpu.VMEM(wide, f32),
            pltpu.VMEM(wide, bf16),
        ],
    )


def unpack(ref, m, out):
    for a in range(PIECES):
        rs = slice(a * 192, a * 192 + 192)
        for ct in range(COLS):
            first = 3 * (ct % 3)
            part = ref[m, a, ct // 3, :, first : first + 3].astype(f32)
            out[rs, ct * 128 : ct * 128 + 128] = part.reshape(192, 128).astype(bf16)


def unpack_bias(ref, out):
    for a in range(PIECES):
        tile = ref[0, a, 0, :, UNITS - 1].astype(f32)
        lane = lanes(tile.shape)
        parts = [jnp.where(lane == rt, tile, 0.0)[:, None] for rt in range(3)]
        column = jnp.concatenate(parts, axis=1).reshape(192, 128)
        out[a * 192 : a * 192 + 192, WIDTH:] = column.astype(bf16)


def ffn_blocks(rows, wu, wd, act, slope, acc):
    acc[...] = jnp.zeros(acc.shape, f32)

    def block(i, carry):
        hs = pl.ds(pl.multiple_of(i * 256, 256), 256)
        upper = dot_last(rows[...], wu[hs, :])
        cdf = 0.5 * (1.0 + lax.erf(upper * math.sqrt(0.5)))
        a = (upper * cdf).astype(bf16)
        act[:, hs] = a
        density = jnp.exp(-0.5 * upper * upper) * (1.0 / math.sqrt(2.0 * math.pi))
        slope[:, hs] = (cdf + upper * density).astype(bf16)
        acc[...] += dot(a, wd[hs, :])
        return carry

    lax.fori_loop(0, HIDDEN // 256, block, 0)


def unpack_kernel(w, wu, wd):
    unpack(w, 0, wu)
    unpack_bias(w, wu)
    unpack(w, 1, wd)


def unpack_weights(weights):
    return staged_call(
        unpack_kernel, "unpack", 12, [("pair", weights)],
        [("vmem", shape((HIDDEN, WIDTH + 128), bf16)), ("vmem", shape((HIDDEN, WIDTH), bf16))],
    )


def ffn_kernel(own, sib, wu, wd, act, slope, part_own, part_sib, rows_out, rows, acc):
    rows[0:ROWS, 0:WIDTH] = own[...]
    rows[ROWS:, 0:WIDTH] = sib[...]
    rows[:, WIDTH:] = jnp.where(lanes((2 * ROWS, 128)) < 3, 1.0, 0.0).astype(bf16)
    rows_out[...] = rows[:, 0:WIDTH]
    ffn_blocks(rows, wu, wd, act, slope, acc)
    part_own[...] = acc[0:ROWS]
    part_sib[...] = acc[ROWS:].astype(bf16)


def ffn(*args):
    wide = (ROWS, WIDTH)
    tall = shape((2 * ROWS, WIDTH), bf16)
    outs = (tall, tall, shape(wide, f32), shape(wide, bf16), tall)
    return staged_call(
        ffn_kernel, "ffn", 20, [("vmem", a) for a in args], [("vmem", o) for o in outs],
        [pltpu.VMEM((2 * ROWS, WIDTH + 128), bf16), pltpu.VMEM((2 * ROWS, WIDTH), f32)],
    )


def combine_kernel(own, got, out):
    out[...] = (own[...] + got[...].astype(f32)).astype(bf16)


def combine(own, got):
    return pl.pallas_call(
        combine_kernel,
        out_shape=shape((ROWS, WIDTH), bf16),
        in_specs=[VMEM] * 2,
        out_specs=VMEM,
        compiler_params=params(16),
        name="combine",
    )(own, got)


def gather_rows(own, near, far):
    return own[...] + near[...].astype(f32) + far[...].astype(f32)


def second_norm(n1, own, near, far, bd, ga, sa, gf, og):
    first = n1[...] * ga[...].astype(f32) + sa[...].astype(f32)
    n, inv = norm_rows(first + gather_rows(own, near, far) + bd[...].astype(f32))
    g = og[...].astype(f32)
    return n, g, norm_back(g, n, inv, gf[...].astype(f32))


def middle_kernel(n1, own, near, far, bd, ga, sa, gf, og, low):
    low[...] = second_norm(n1, own, near, far, bd, ga, sa, gf, og)[2].astype(bf16)


def middle(*args):
    return pl.pallas_call(
        middle_kernel,
        out_shape=shape((ROWS, WIDTH), bf16),
        in_specs=[VMEM] * len(args),
        out_specs=VMEM,
        compiler_params=params(16),
        name="middle",
    )(*args)


def outputs_kernel(
    n1, own, near, far, bd, ga, sa, gf, og, sf, out, second, sums,
):
    n, g, grad = second_norm(n1, own, near, far, bd, ga, sa, gf, og)
    out[...] = (n * gf[...].astype(f32) + sf[...].astype(f32)).astype(bf16)
    second[...] = grad
    sums[0:1] = jnp.sum(grad.astype(bf16).astype(f32), axis=0, keepdims=True)
    sums[1:2] = jnp.sum(g * n, axis=0, keepdims=True)
    sums[2:3] = jnp.sum(g, axis=0, keepdims=True)
    sums[3:8] = jnp.zeros((5, WIDTH), f32)


def outputs(*args):
    wide = (ROWS, WIDTH)
    return staged_call(
        outputs_kernel, "outputs", 16, [("vmem", a) for a in args],
        [("hbm", shape(wide, bf16)), ("hbm", shape(wide, f32)), ("hbm", shape((8, WIDTH), f32))],
    )


def back_blocks(g, wu, wd, slope, u_out, bias, acc):
    acc[...] = jnp.zeros(acc.shape, f32)
    bias[...] = jnp.zeros((8, HIDDEN), f32)

    def block(i, carry):
        hs = pl.ds(pl.multiple_of(i * 256, 256), 256)
        u = (dot_last(g[...], wd[hs, :]) * slope[:, hs].astype(f32)).astype(bf16)
        u_out[:, hs] = u
        bias[0:1, hs] = jnp.sum(u.astype(f32), axis=0, keepdims=True)
        acc[...] += dot(u, wu[hs, 0:WIDTH])
        return carry

    lax.fori_loop(0, HIDDEN // 256, block, 0)


def back_ffn_kernel(own, sib, wu, wd, slope, first_own, first_sib, g, u, bias, acc):
    g[0:ROWS] = own[...]
    g[ROWS:] = sib[...]
    back_blocks(g, wu, wd, slope, u, bias, acc)
    first_own[...] = acc[0:ROWS]
    first_sib[...] = acc[ROWS:].astype(bf16)


def back_ffn(name, *args):
    wide = (ROWS, WIDTH)
    tall = shape((2 * ROWS, WIDTH), bf16)
    return staged_call(
        back_ffn_kernel, name, 20, [("vmem", a) for a in args],
        [
            ("hbm" if name == "back_near" else "vmem", shape(wide, f32)), ("vmem", shape(wide, bf16)),
            ("vmem", tall), ("vmem", tall), ("hbm", shape((8, HIDDEN), f32)),
        ],
        [pltpu.VMEM((2 * ROWS, WIDTH), f32)],
    )


def pack_kernel(gu, gd, grads):
    def piece(a, carry):
        rs = pl.ds(pl.multiple_of(a * 192, 192), 192)
        for m, ref in enumerate((gu, gd)):
            for ct in range(COLS):
                us = slice(3 * (ct % 3), 3 * (ct % 3) + 3)
                part = ref[rs, ct * 128 : ct * 128 + 128].astype(f32).reshape(8, 3, 8, 128)
                grads[m, a, ct // 3, :, us] = part.astype(bf16)
        return carry

    lax.fori_loop(0, PIECES, piece, 0)


def pack(*args):
    return staged_call(
        pack_kernel, "pack", 12, [("vmem", a) for a in args],
        [("hbm", shape((2, PIECES, 2, 8, GRAD_UNITS, 8, 128), bf16))],
    )[0]


def back_kernel(
    place, own, near, far, second, n1, inv1, ga, ctx, wo, nrm, scl, wave, wavet, ks, vs, tapt, col, live, x,
    wv, sums, bias_n, bias_f, in_grad, keep, give, buf_a, buf_b, mb,
):
    first_grad = second[...] + gather_rows(own, near, far)
    n = n1[...]
    buf_a[768 + 2 : 768 + 3] = jnp.sum(first_grad * n, axis=0, keepdims=True)
    buf_a[768 + 3 : 768 + 4] = jnp.sum(first_grad, axis=0, keepdims=True)
    resid = norm_back(first_grad, n, inv1[...][:, 0:1], ga[...].astype(f32))
    ag = resid.astype(bf16)
    buf_a[768 + 1 : 768 + 2] = jnp.sum(ag.astype(f32), axis=0, keepdims=True)
    buf_a[768 + 4 : 768 + 7] = sums[0:3]
    buf_a[768 + 7 :] = jnp.zeros((TALL - 775, WIDTH), f32)
    mine = lax.broadcasted_iota(i32, (8, WIDTH), 0) == place[0] % CLASSES
    bias = jnp.broadcast_to(bias_n[0:1] + bias_f[0:1], (8, WIDTH))
    buf_a[776:784] = jnp.where(mine, bias, 0.0)
    buf_b[0:768] = dot_first(ctx[...], ag)
    cg = dot_last(ag, wo[...])
    mb[...] = cg
    first_head = lanes((ROWS, 128)) < HEAD_DIM
    nrm.ready()
    scl.ready()
    col.ready()

    def heads(b, carry):
        cs = pl.ds(pl.multiple_of(b * 128, 128), 128)
        c = mb[:, cs]
        m = nrm[:, cs].astype(f32)
        prod = c * m
        one = jnp.sum(jnp.where(first_head, prod, 0.0), axis=1, keepdims=True)
        two = jnp.sum(jnp.where(first_head, 0.0, prod), axis=1, keepdims=True)
        mean = jnp.where(first_head, one, two) * (1.0 / HEAD_DIM)
        block = (scl[:, cs] * (c - m * mean)).astype(bf16)
        mb[:, cs] = jnp.where(
            first_head, dot_first(col[2 * b], block), dot_first(col[2 * b + 1], block)
        )
        return carry

    lax.fori_loop(0, COLS, heads, 0)
    spec = dot(wave[...], cg.astype(bf16))
    g_cos = spec[0:FREQ]
    g_sin = spec[FREQ:]
    k_cos = ks[0:FREQ]
    k_sin = ks[FREQ:]
    z_cos = (k_cos * g_cos - k_sin * g_sin).astype(bf16)
    z_sin = (k_cos * g_sin + k_sin * g_cos).astype(bf16)
    conv = dot(wavet[:, 0:FREQ], z_cos) + dot(wavet[:, FREQ:], z_sin)
    v_cos = vs[0:FREQ].astype(f32)
    v_sin = vs[FREQ:].astype(f32)
    f = lax.broadcasted_iota(i32, (FREQ, 1), 0)
    weight = jnp.where((f == 0) | (f == DFT_LEN // 2), 1.0 / DFT_LEN, 2.0 / DFT_LEN)
    weight = jnp.where(f < LIVE_FREQ, weight, 0.0)
    re = ((g_cos * v_cos + g_sin * v_sin) * weight).astype(bf16)
    im = ((g_cos * v_sin - g_sin * v_cos) * weight).astype(bf16)
    gk = dot(tapt[:, 0:FREQ], re) + dot(tapt[:, FREQ:], im)
    buf_b[768:] = jnp.zeros((TALL - 768, WIDTH), f32)
    buf_b[768 : 768 + TAPS] = gk[0:TAPS]
    vg = ((mb[...] + conv) * live[...][:, 0:1]).astype(bf16)
    buf_a[768:769] = jnp.sum(vg.astype(f32), axis=0, keepdims=True)
    buf_a[0:768] = dot_first(x[...], vg)
    in_grad[...] = resid + dot_last(vg, wv[...])

    def write(kept, given):
        for ct in range(COLS):
            cs = slice(ct * 128, ct * 128 + 128)
            ts = slice(ct * TALL_TILES, ct * TALL_TILES + TALL_TILES)
            keep[ts] = kept[:, cs].reshape(TALL_TILES, 8, 128).astype(bf16)
            give[ts] = given[:, cs].reshape(TALL_TILES, 8, 128).astype(bf16)

    rest = PACK - COLS * TALL_TILES
    keep[PACK - rest :] = jnp.zeros((rest, 8, 128), bf16)
    give[PACK - rest :] = jnp.zeros((rest, 8, 128), bf16)

    @pl.when(place[0] % 2 == 0)
    def _():
        write(buf_a, buf_b)

    @pl.when(place[0] % 2 == 1)
    def _():
        write(buf_b, buf_a)


def attend_back(*args):
    wide = (ROWS, WIDTH)
    packed = shape((PACK, 8, 128), bf16)
    kinds = ["smem"] + ["hbm"] * (len(args) - 1)
    for i in (2, 3, 7):
        kinds[i] = "vmem"
    return staged_call(
        back_kernel, "attend_back", 40, list(zip(kinds, args, strict=True)),
        [("hbm", shape(wide, f32)), ("vmem", packed), ("vmem", packed)],
        [
            pltpu.VMEM((TALL, WIDTH), f32),
            pltpu.VMEM((TALL, WIDTH), f32),
            pltpu.VMEM(wide, f32),
        ],
    )


def sum_ffn_kernel(got, out, acc):
    step = pl.program_id(0)

    @pl.when(step == 0)
    def _():
        acc[...] = jnp.zeros(acc.shape, f32)

    for q in range(CLASSES):
        total = acc[q]
        for t in range(8):
            total = total + got[q * 8 + t].astype(f32)
        acc[q] = total

    @pl.when(step == 3)
    def _():
        out[...] = acc[...].astype(bf16)


def sum_ffn(got):
    return pl.pallas_call(
        sum_ffn_kernel,
        grid=(4,),
        out_shape=shape((CLASSES, GRAD_UNITS, 8, 128), bf16),
        in_specs=[pl.BlockSpec((32, GRAD_UNITS, 8, 128), lambda i: (i, 0, 0, 0))],
        out_specs=pl.BlockSpec((CLASSES, GRAD_UNITS, 8, 128), lambda i: (0, 0, 0, 0)),
        scratch_shapes=[pltpu.VMEM((CLASSES, GRAD_UNITS, 8, 128), f32)],
        compiler_params=params(32),
        name="sum_ffn",
    )(got)


def sum_rest_kernel(got, out):
    per = PACK // 128
    total = [jnp.zeros((per, 8, 128), f32) for _ in range(2)]
    for i in range(8):
        for c in range(2):
            for t in range(8):
                total[c] = total[c] + got[i * 16 + c * 8 + t].astype(f32)
    low = [t.astype(bf16) for t in total]
    for i in range(8):
        for c in range(2):
            for t in range(8):
                out[i * 16 + c * 8 + t] = low[c]


def sum_rest(got):
    return pl.pallas_call(
        sum_rest_kernel,
        out_shape=shape(got.shape, bf16),
        in_specs=[VMEM],
        out_specs=VMEM,
        compiler_params=params(32),
        name="sum_rest",
    )(got)


def final_ffn_kernel(place, ffn_own, ffn_oth, g_up, g_down, tall):
    ct = pl.program_id(0)
    core = place[0] % 2
    x_lo = place[0] // 8
    half = ct // 3

    def spread(up_ref, down_ref):
        for a in range(PIECES):
            at = (place[0] // 2 % 4 + 4 - a) % 4 * 2
            up = up_ref[at + (half + x_lo) % 2].astype(f32)
            down = down_ref[at + (half + x_lo + 1) % 2].astype(f32)
            for q in range(CLASSES):
                rs = slice(SUB * q + PIECE * a, SUB * q + PIECE * a + PIECE)
                tall[rs, :] = up[q].reshape(PIECE, 128)
                g_down[rs, :] = down[q].reshape(PIECE, 128)

    @pl.when(x_lo == core)
    def _():
        spread(ffn_own, ffn_oth)

    @pl.when(x_lo != core)
    def _():
        spread(ffn_oth, ffn_own)

    g_up[...] = tall[...].T


def final_ffn(place, ffn_own, ffn_oth):
    units = pl.BlockSpec((8, CLASSES, 3, 8, 128), lambda i: (0, 0, i % 3, 0, 0))
    return pl.pallas_call(
        final_ffn_kernel,
        grid=(COLS,),
        out_shape=(shape((768, 384), f32), shape((384, 768), f32)),
        in_specs=[SMEM, units, units],
        out_specs=(
            pl.BlockSpec((128, 384), lambda i: (i, 0)),
            pl.BlockSpec((384, 128), lambda i: (0, i)),
        ),
        scratch_shapes=[pltpu.VMEM((384, 128), f32)],
        compiler_params=params(16),
        name="final_ffn",
    )(place, ffn_own, ffn_oth)


def final_kernel(
    place, own, other, g_wv, g_bv, g_conv, g_wo, g_bo, g_ga, g_sa, g_bup, g_bd, g_gf, g_sf, vecs,
    bias, line,
):
    ct = pl.program_id(0)

    def write(a, b):
        g_wv[...] = a[0:96].astype(f32).reshape(768, 128)
        vecs[ct] = a[96].astype(f32)
        bias[ct] = a[97].astype(f32)
        g_wo[...] = b[0:96].astype(f32).reshape(768, 128)
        g_conv[...] = b[96:105].astype(f32).reshape(72, 128)[0:TAPS]

    @pl.when(place[0] % 2 == 0)
    def _():
        write(own, other)

    @pl.when(place[0] % 2 == 1)
    def _():
        write(other, own)

    @pl.when(ct == COLS - 1)
    def _():
        for j, ref in enumerate((g_bv, g_bo, g_ga, g_sa, g_bd, g_gf, g_sf)):
            for i in range(COLS):
                ref[i * 128 : i * 128 + 128] = vecs[i, j]
        n = lanes((128, 128))
        a = (n >= PIECE).astype(i32) + (n >= 2 * PIECE).astype(i32) + (n >= 3 * PIECE).astype(i32)
        at = (8 * a + place[1]) * PIECE + n - PIECE * a
        total = jnp.zeros((8, 128), f32)
        for i in range(COLS):
            pick = lax.broadcasted_iota(i32, (128, 128), 0) + 128 * i == at
            total = total + dot(bias[i].astype(bf16), jnp.where(pick, 1.0, 0.0).astype(bf16))
        for q in range(CLASSES):
            line[0:1, SUB * q : SUB * q + SUB] = total[q : q + 1, 0:SUB]
        g_bup[...] = line[...][0]


def final(place, own, other):
    tile = pl.BlockSpec((TALL_TILES, 8, 128), lambda i: (i, 0, 0))
    tall = pl.BlockSpec((768, 128), lambda i: (0, i))
    vec = pl.BlockSpec((WIDTH,), lambda i: (0,))
    v = shape((WIDTH,), f32)
    return pl.pallas_call(
        final_kernel,
        grid=(COLS,),
        out_shape=(
            shape((768, 768), f32), v, shape((TAPS, 768), f32), shape((768, 768), f32), v, v, v,
            shape((384,), f32), v, v, v,
        ),
        in_specs=[SMEM, tile, tile],
        out_specs=(
            tall, vec, pl.BlockSpec((TAPS, 128), lambda i: (0, i)), tall, vec, vec, vec,
            pl.BlockSpec((384,), lambda i: (0,)), vec, vec, vec,
        ),
        scratch_shapes=[
            pltpu.VMEM((COLS, 8, 128), f32),
            pltpu.VMEM((COLS, 8, 128), f32),
            pltpu.VMEM((1, 384), f32),
        ],
        compiler_params=params(16),
        name="final",
    )(place, own, other)


def body(
    block_input,
    w_value,
    b_value,
    conv_kernel,
    w_out,
    b_out,
    gain_attn,
    shift_attn,
    w_up,
    b_up,
    w_down,
    b_down,
    gain_ffn,
    shift_ffn,
    query_codes,
    key_codes,
    key_live,
    seq_lengths,
    out_grad,
):
    dp = lax.axis_index("dp")
    place = jnp.stack([dp, lax.axis_index("tensor")]).astype(i32)
    n_dp = lax.axis_size("dp")

    def shift(i, by):
        return i // 8 * 8 + (i // 2 + by) % 4 * 2 + i % 2

    def swap(x):
        return lax.ppermute(x, "dp", [(i, i ^ 1) for i in range(n_dp)])

    def away(x):
        pairs = [(i, shift(i, 1 - i % 2 * 2)) for i in range(n_dp)]
        return lax.ppermute(x, "dp", pairs)

    def home(x):
        pairs = [(shift(i, 1 - i % 2 * 2), i) for i in range(n_dp)]
        return lax.ppermute(x, "dp", pairs)

    def exchange(x):
        return lax.all_to_all(x, ALL, 0, 0, tiled=True)

    def row(v):
        return v.reshape(1, -1)

    weights = exchange(prep(place, w_up, w_down, b_up))
    weights = weights.reshape(2, PIECES, 2, 8, UNITS, 8, 128)
    (n1, inv1, low, ctx, collide, nrm, scl, wave, wavet, ks, vs, tapt, live) = attend(
        seq_lengths, block_input, w_value, row(b_value), conv_kernel, w_out, row(b_out),
        row(gain_attn), row(shift_attn), query_codes, key_codes, row(key_live),
    )
    low_sib = swap(low)
    got = away(low)
    wu, wd = unpack_weights(weights)
    act_f, slope_f, far_own, far_sib, rows_f = ffn(got, swap(got), wu, wd)
    sent = combine(far_own, swap(far_sib))
    wu, sent = lax.optimization_barrier((wu, sent))
    act_n, slope_n, near_own, near_sib, rows_n = ffn(low, low_sib, wu, wd)
    near_sib, far = lax.optimization_barrier((near_sib, home(sent)))
    second_args = (
        n1, near_own, swap(near_sib), far, row(b_down), row(gain_attn), row(shift_attn),
        row(gain_ffn), out_grad,
    )
    grad = middle(*second_args)
    got = away(grad)
    near_own, near_sib, g_n, u_n, bias_n = back_ffn("back_near", grad, swap(grad), wu, wd, slope_n)
    block_output, second, sums = outputs(*second_args, row(shift_ffn))
    got, near_sib, second = lax.optimization_barrier((got, near_sib, second))
    far_own, far_sib, g_f, u_f, bias_f = back_ffn("back_far", got, swap(got), wu, wd, slope_f)
    sent = combine(far_own, swap(far_sib))
    u_f, sent = lax.optimization_barrier((u_f, sent))
    grad_down = (dot_first(act_n, g_n) + dot_first(act_f, g_f)).astype(bf16)
    grad_up = (dot_first(u_n, rows_n) + dot_first(u_f, rows_f)).astype(bf16)
    grads, far = lax.optimization_barrier((pack(grad_up, grad_down), home(sent)))
    owned = exchange(grads.reshape(128, GRAD_UNITS, 8, 128))
    input_grad, keep, give = attend_back(
        place, near_own, swap(near_sib), far, second, n1, inv1,
        row(gain_attn), ctx, w_out, nrm, scl, wave, wavet, ks, vs, tapt, collide, live, block_input,
        w_value, sums, bias_n, bias_f,
    )
    pair = (keep.astype(f32) + swap(give).astype(f32)).astype(bf16)
    pair = pair.reshape(128, PACK // 128, 8, 128)
    owned = sum_ffn(owned)
    pair, owned = lax.optimization_barrier((pair, owned))
    both = jnp.stack([owned, swap(owned)])
    around = []
    for by in range(4):
        pairs = [(i, (i // 8 ^ i % 2) * 8 + shift(i % 8, by)) for i in range(n_dp)]
        around.append(lax.ppermute(both, "dp", pairs))
    summed = sum_rest(exchange(pair))
    summed, *around = lax.optimization_barrier((summed, *around))
    back = exchange(summed).reshape(PACK, 8, 128)
    ffn_own = jnp.stack(around).reshape(8, CLASSES, GRAD_UNITS, 8, 128)
    g_up, g_down = final_ffn(place, ffn_own, swap(ffn_own))
    back, g_up, g_down = lax.optimization_barrier((back, g_up, g_down))
    g_wv, g_bv, g_conv, g_wo, g_bo, g_ga, g_sa, g_bup, g_bd, g_gf, g_sf = final(
        place, back, swap(back)
    )
    return (
        block_output, input_grad, g_wv, g_bv, g_conv, g_wo, g_bo, g_ga, g_sa, g_up, g_bup, g_down,
        g_bd, g_gf, g_sf,
    )


def solution(mesh):
    rows = P(ALL, None)
    return jax.shard_map(
        body,
        mesh=mesh,
        in_specs=(
            rows, P(), P(), P(), P(), P(), P(), P(),
            P(None, "tensor"), P("tensor"), P("tensor", None), P(), P(), P(),
            rows, rows, P(ALL), rows, rows,
        ),
        out_specs=(
            rows, rows, P(), P(), P(), P(), P(), P(), P(),
            P(None, "tensor"), P("tensor"), P("tensor", None), P(), P(), P(),
        ),
        check_vma=False,
    )
```

```python
import math

import jax
import jax.numpy as jnp
from jax import lax
from jax.experimental import pallas as pl
from jax.experimental.pallas import tpu as pltpu
from jax.sharding import PartitionSpec as P

HEADS = 12
SETS = 32
ROWS = 256
WIDTH = 768
HEAD_DIM = 64
COLS = WIDTH // 128
TAPS = 65
MARGIN = 32
DFT_LEN = 384
FREQ = 256
LIVE_FREQ = DFT_LEN // 2 + 1
CLASSES = 4
SUB = 96
PIECE = 24
PIECES = SUB // PIECE
UNITS = 10
GRAD_UNITS = 9
HIDDEN = 768
TALL = 848
TALL_TILES = TALL // 8
PACK = 640
ALL = ("dp", "tensor")

bf16 = jnp.bfloat16
f32 = jnp.float32
i32 = jnp.int32

VMEM = pl.BlockSpec(memory_space=pltpu.VMEM)
SMEM = pl.BlockSpec(memory_space=pltpu.SMEM)
HBM = pl.BlockSpec(memory_space=pltpu.HBM)


def shape(dims, dtype):
    return jax.ShapeDtypeStruct(dims, dtype)


def params(mib):
    return pltpu.CompilerParams(vmem_limit_bytes=mib << 20)


def dot(a, b):
    return lax.dot_general(a, b, (((1,), (0,)), ((), ())), preferred_element_type=f32)


def dot_last(a, b):
    return lax.dot_general(a, b, (((1,), (1,)), ((), ())), preferred_element_type=f32)


def dot_first(a, b):
    return lax.dot_general(a, b, (((0,), (0,)), ((), ())), preferred_element_type=f32)


def lanes(dims):
    return lax.broadcasted_iota(i32, dims, len(dims) - 1)


def norm_rows(r):
    mean = jnp.mean(r, axis=-1, keepdims=True)
    centred = r - mean
    inv = lax.rsqrt(jnp.mean(centred * centred, axis=-1, keepdims=True) + 1e-05)
    return centred * inv, inv


def norm_back(g, n, inv, gain):
    e = g * gain
    return (
        e - jnp.mean(e, axis=-1, keepdims=True) - n * jnp.mean(e * n, axis=-1, keepdims=True)
    ) * inv


class Staged:
    def __init__(self, ref, buf, sem, incoming):
        pair = (ref, buf) if incoming else (buf, ref)
        self.buf = buf
        self.copy = pltpu.make_async_copy(*pair, sem)
        self.incoming = incoming
        self.pending = True
        if incoming:
            self.copy.start()

    def ready(self):
        if self.pending:
            self.copy.wait()
            self.pending = False

    def leave(self):
        if self.pending:
            self.copy.start()
            self.pending = False

    def __getitem__(self, index):
        if self.incoming:
            self.ready()
        return self.buf[index]

    def __setitem__(self, index, value):
        self.buf[index] = value


class StagedPair:
    def __init__(self, ref, buf, sems):
        self.buf = buf
        self.copies = [pltpu.make_async_copy(ref.at[i], buf.at[i], sems.at[i]) for i in range(2)]
        self.pending = [True, True]
        for copy in self.copies:
            copy.start()

    def ready(self):
        for i in range(2):
            if self.pending[i]:
                self.copies[i].wait()
                self.pending[i] = False

    def __getitem__(self, index):
        i = index[0]
        if self.pending[i]:
            self.copies[i].wait()
            self.pending[i] = False
        return self.buf[index]


def staged_call(kernel, name, mib, ins, outs, scratch=()):
    spec = {"smem": SMEM, "vmem": VMEM, "hbm": HBM, "pair": HBM}
    arrays = [a for _, a in ins]
    kinds = [k for k, _ in ins] + [k for k, _ in outs]
    avals = arrays + [o for _, o in outs]
    staged = [i for i, k in enumerate(kinds) if k in ("hbm", "pair")]
    n_in = len(ins)

    if not staged:
        return pl.pallas_call(
            kernel,
            out_shape=tuple(o for _, o in outs),
            in_specs=[spec[k] for k, _ in ins],
            out_specs=tuple(spec[k] for k, _ in outs),
            scratch_shapes=list(scratch),
            compiler_params=params(mib),
            name=name,
        )(*arrays)

    def run(*refs):
        refs = list(refs)
        sems = refs.pop()
        split = len(refs) - len(staged)
        bufs = refs[split:]
        refs = refs[:split]
        for n, i in enumerate(staged):
            if kinds[i] == "pair":
                refs[i] = StagedPair(refs[i], bufs[n], sems.at[n])
            else:
                refs[i] = Staged(refs[i], bufs[n], sems.at[n, 0], i < n_in)
        kernel(*refs)
        for i in staged:
            if i < n_in:
                refs[i].ready()
            else:
                refs[i].leave()
        for i in staged:
            if i >= n_in:
                refs[i].copy.wait()

    buffers = [pltpu.VMEM(avals[i].shape, avals[i].dtype) for i in staged]
    arrays = [
        a if k in ("smem", "vmem") else pltpu.with_memory_space_constraint(a, pltpu.HBM)
        for k, a in ins
    ]
    return pl.pallas_call(
        run,
        out_shape=tuple(pltpu.HBM(o.shape, o.dtype) if k == "hbm" else o for k, o in outs),
        in_specs=[spec[k] for k, _ in ins],
        out_specs=tuple(spec[k] for k, _ in outs),
        scratch_shapes=[*scratch, *buffers, pltpu.SemaphoreType.DMA((len(staged), 2))],
        compiler_params=params(mib),
        name=name,
    )(*arrays)


def prep_kernel(place, up_ref, down_ref, bias_hbm, out_ref, half, piece, bias_ref, sems):
    rep = place[0] % 8
    is_up = place[0] < 8
    at = pl.ds(pl.multiple_of(rep % 2 * 384, 128), 384)
    up = pltpu.make_async_copy(up_ref.at[at, :], half, sems.at[0])
    down = pltpu.make_async_copy(down_ref.at[:, at], half, sems.at[0])
    bias_copy = pltpu.make_async_copy(bias_hbm, bias_ref, sems.at[33])
    bias_copy.start()

    @pl.when(is_up)
    def _():
        up.start()

    @pl.when(jnp.logical_not(is_up))
    def _():
        down.start()

    n = lax.broadcasted_iota(i32, (SUB, 384), 0)
    q = sum((n >= PIECE * k).astype(i32) for k in range(1, CLASSES))
    unit = (SUB - PIECE) * q + n + PIECE * (rep // 2)
    pick = jnp.where(unit == lanes((SUB, 384)), 1.0, 0.0).astype(bf16)
    scale = jnp.where(is_up & (rep % 2 == 0), 1.0, 0.0)
    bias_copy.wait()
    bias = jnp.broadcast_to(bias_ref[...].astype(f32) * scale, (16, 384)).astype(bf16)
    column = dot_last(pick, bias)[:, 0:1]

    def fill(rows):
        for k in range(CLASSES):
            rs = slice(PIECE * k, PIECE * k + PIECE)
            for j in range(3):
                part = rows[rs, j * 128 : j * 128 + 128].reshape(3, 8, 128)
                piece[k, 3 * j : 3 * j + 3] = part.astype(bf16)
            col = jnp.broadcast_to(column[rs], (PIECE, 128)).reshape(3, 8, 128)
            lane = lanes((8, 128))
            tile = jnp.where(lane == 0, col[0], jnp.where(lane == 1, col[1], col[2]))
            piece[k, UNITS - 1] = tile.astype(bf16)

    @pl.when(is_up)
    def _():
        up.wait()
        fill(dot_last(pick, half[...]))

    @pl.when(jnp.logical_not(is_up))
    def _():
        down.wait()
        fill(dot(pick, half[...]))

    copies = [
        pltpu.make_async_copy(piece, out_ref.at[g, :, t], sems.at[1 + 8 * g + t])
        for g in range(4)
        for t in range(8)
    ]
    for copy in copies:
        copy.start()
    for copy in copies:
        copy.wait()


def prep(place, w_up, w_down, b_up):
    out = pl.pallas_call(
        prep_kernel,
        out_shape=pltpu.HBM((4, CLASSES, 8, UNITS, 8, 128), bf16),
        in_specs=[SMEM, HBM, HBM, HBM],
        out_specs=HBM,
        scratch_shapes=[
            pltpu.VMEM((384, 384), bf16),
            pltpu.VMEM((CLASSES, UNITS, 8, 128), bf16),
            pltpu.VMEM((384,), bf16),
            pltpu.SemaphoreType.DMA((34,)),
        ],
        compiler_params=params(16),
        name="prep",
    )(
        place,
        pltpu.with_memory_space_constraint(w_up, pltpu.HBM),
        pltpu.with_memory_space_constraint(w_down, pltpu.HBM),
        pltpu.with_memory_space_constraint(b_up, pltpu.HBM),
    )
    return out.reshape(128, UNITS, 8, 128)


def segment_ends(len_ref):
    e0 = len_ref[0, 0]
    e1 = e0 + len_ref[0, 1]
    return e0, e1, e1 + len_ref[0, 2]


def segment_of(p, ends):
    return sum((p >= e).astype(i32) for e in ends)


def turn(product):
    r = product.astype(f32) * (1.0 / DFT_LEN)
    m = product - DFT_LEN * jnp.round(r).astype(i32)
    x = m.astype(f32) * (2.0 * math.pi / DFT_LEN)
    z = x * x
    c = 1.0
    s = 1.0
    for k in range(8, 0, -1):
        c = 1.0 - z * c * (1.0 / ((2 * k - 1) * (2 * k)))
        s = 1.0 - z * s * (1.0 / ((2 * k) * (2 * k + 1)))
    return c, x * s


def attend_kernel(
    len_ref, x_ref, wv_ref, bv_ref, taps_ref, wo_ref, bo_ref, ga_ref, sa_ref, q_ref, k_ref, live_ref,
    n_ref, inv_ref, low_ref, ctx_ref, col_ref, nrm_ref, scl_ref, wave_ref, wavet_ref, ks_ref, vs_ref,
    tapt_ref, live_out, qw, kb, jn, tapbuf, mix, mskd,
):
    ends = segment_ends(len_ref)
    square = (ROWS, ROWS)
    rows_i = lax.broadcasted_iota(i32, square, 0)
    lanes_i = lax.broadcasted_iota(i32, square, 1)
    jn[...] = jnp.where(segment_of(rows_i, ends) == segment_of(lanes_i, ends), 1.0 / SETS, 0.0)
    d = lax.broadcasted_iota(i32, (384, 128), 0) - 4 * lax.broadcasted_iota(i32, (384, 128), 1)
    w_lo = jnp.where(d == 0, 1.0, jnp.where(d == 1, 256.0, 0.0)).astype(bf16)
    w_hi = jnp.where(d == 2, 1.0, jnp.where(d == 3, 256.0, 0.0)).astype(bf16)
    q_codes = q_ref[...].astype(f32).astype(bf16)
    k_codes = k_ref[...].astype(f32).astype(bf16)
    qw[...] = dot(q_codes, w_lo).astype(i32) | (dot(q_codes, w_hi).astype(i32) << 16)
    kw = dot(k_codes, w_lo).T.astype(i32) | (dot(k_codes, w_hi).T.astype(i32) << 16)
    for r in range(96):
        for j in range(2):
            kb[r, j] = jnp.broadcast_to(kw[r : r + 1, j * 128 : j * 128 + 128], (8, 128))
    low7 = jnp.int32(0x7F7F7F7F)
    ones = jnp.int32(0x01010101)
    byte2 = jnp.int32(0x00FF00FF)
    tile_rows = 16
    groups = tile_rows // 8

    def tile(rt, carry):
        rs = pl.ds(pl.multiple_of(rt * tile_rows, tile_rows), tile_rows)
        qt = qw[rs, :]
        for h in range(HEADS):
            acc = [[jnp.zeros((8, 128), i32) for _ in range(2)] for _ in range(groups)]
            for g in range(8):
                c = h * 8 + g
                qc = [
                    jnp.broadcast_to(qt[t * 8 : t * 8 + 8, c : c + 1], (8, 128))
                    for t in range(groups)
                ]
                for j in range(2):
                    kk = kb[c, j]
                    for t in range(groups):
                        x = qc[t] ^ kk
                        y = ((x & low7) + low7) | x
                        acc[t][j] = acc[t][j] + (lax.shift_right_logical(y, 7) & ones)
            for j in range(2):
                parts = []
                for t in range(groups):
                    z = acc[t][j]
                    z = (z & byte2) + (lax.shift_right_logical(z, 8) & byte2)
                    z = (z & jnp.int32(0xFFFF)) + lax.shift_right_logical(z, 16)
                    parts.append((SETS - z).astype(f32))
                m = jnp.concatenate(parts, axis=0) * jn[rs, j * 128 : j * 128 + 128]
                col_ref[h, rs, j * 128 : j * 128 + 128] = m.astype(bf16)
        return carry

    lax.fori_loop(0, ROWS // tile_rows, tile, 0)

    col_ref.leave()

    dims = (FREQ, ROWS)
    f = lax.broadcasted_iota(i32, dims, 0)
    p = lax.broadcasted_iota(i32, dims, 1)
    c, s = turn(f * (p + MARGIN * segment_of(p, ends)))
    ok = f < LIVE_FREQ
    wave_ref[0:FREQ] = jnp.where(ok, c, 0.0).astype(bf16)
    wave_ref[FREQ:] = jnp.where(ok, s, 0.0).astype(bf16)
    p = lax.broadcasted_iota(i32, dims, 0)
    f = lax.broadcasted_iota(i32, dims, 1)
    c, s = turn(f * (p + MARGIN * segment_of(p, ends)))
    ok = f < LIVE_FREQ
    wavet_ref[:, 0:FREQ] = jnp.where(ok, c, 0.0).astype(bf16)
    wavet_ref[:, FREQ:] = jnp.where(ok, s, 0.0).astype(bf16)
    dims = (FREQ, 128)
    f = lax.broadcasted_iota(i32, dims, 0)
    c, s = turn(f * (lax.broadcasted_iota(i32, dims, 1) - MARGIN))
    tap_c = c.astype(bf16)
    tap_s = s.astype(bf16)
    dims = (128, FREQ)
    f = lax.broadcasted_iota(i32, dims, 1)
    c, s = turn(f * (lax.broadcasted_iota(i32, dims, 0) - MARGIN))
    tapt_ref[:, 0:FREQ] = c.astype(bf16)
    tapt_ref[:, FREQ:] = s.astype(bf16)
    tapbuf[...] = jnp.zeros(tapbuf.shape, f32)
    tapbuf[0:TAPS] = taps_ref[...].astype(f32)
    kernel = tapbuf[...].astype(bf16)
    f = lax.broadcasted_iota(i32, (FREQ, 1), 0)
    weight = jnp.where((f == 0) | (f == DFT_LEN // 2), 1.0 / DFT_LEN, 2.0 / DFT_LEN)
    weight = jnp.where(f < LIVE_FREQ, weight, 0.0)
    k_cos = dot(tap_c, kernel) * weight
    k_sin = dot(tap_s, kernel) * weight
    ks_ref[0:FREQ] = k_cos
    ks_ref[FREQ:] = k_sin

    live = jnp.broadcast_to(live_ref[...].astype(f32), (8, ROWS)).T[:, 0:1]
    live_out[...] = jnp.broadcast_to(live, (ROWS, 128))
    values = (dot(x_ref[...], wv_ref[...]) + bv_ref[...].astype(f32)).astype(bf16).astype(f32)
    mskd[...] = (values * live).astype(bf16)
    masked = mskd[...]
    spec = dot(wave_ref[...], masked)
    vs_ref[...] = spec.astype(bf16)
    v_cos = spec[0:FREQ]
    v_sin = spec[FREQ:]
    first_head = lanes((ROWS, 128)) < HEAD_DIM
    y_cos = (k_cos * v_cos + k_sin * v_sin).astype(bf16)
    y_sin = (k_cos * v_sin - k_sin * v_cos).astype(bf16)
    conv = dot(wavet_ref[:, 0:FREQ], y_cos) + dot(wavet_ref[:, FREQ:], y_sin)
    for done in (wave_ref, wavet_ref, tapt_ref, ks_ref, live_out, vs_ref):
        done.leave()

    def heads(b, carry):
        cs = pl.ds(pl.multiple_of(b * 128, 128), 128)
        block = mskd[:, cs]
        m = jnp.where(first_head, dot(col_ref[2 * b], block), dot(col_ref[2 * b + 1], block))
        sq = m * m
        one = jnp.sum(jnp.where(first_head, sq, 0.0), axis=1, keepdims=True)
        two = jnp.sum(jnp.where(first_head, 0.0, sq), axis=1, keepdims=True)
        scale = lax.rsqrt(jnp.where(first_head, one, two) * (1.0 / HEAD_DIM) + 1e-06)
        scl_ref[:, cs] = scale
        nrm = m * scale
        nrm_ref[:, cs] = nrm.astype(bf16)
        mix[:, cs] = nrm
        return carry

    lax.fori_loop(0, COLS, heads, 0)
    context = (mix[...] + conv).astype(bf16)
    ctx_ref[...] = context
    for done in (scl_ref, nrm_ref, ctx_ref):
        done.leave()
    attended = dot(context, wo_ref[...]) + bo_ref[...].astype(f32)
    n, inv = norm_rows(x_ref[...].astype(f32) + attended)
    n_ref[...] = n
    inv_ref[...] = jnp.broadcast_to(inv, (ROWS, 128))
    low_ref[...] = (n * ga_ref[...].astype(f32) + sa_ref[...].astype(f32)).astype(bf16)


def attend(seq_lengths, x, wv, bv, taps, wo, bo, ga, sa, q, k, live):
    wide = (ROWS, WIDTH)
    h = "hbm"
    v = "vmem"
    return staged_call(
        attend_kernel, "attend", 36,
        [
            ("smem", seq_lengths), (h, x), (h, wv), (v, bv), (v, taps), (h, wo), (v, bo), (v, ga),
            (v, sa), (h, q), (h, k), (v, live),
        ],
        [
            (h, shape(wide, f32)), (h, shape((ROWS, 128), f32)), (v, shape(wide, bf16)),
            (h, shape(wide, bf16)),
            (h, shape((HEADS, ROWS, ROWS), bf16)), (h, shape(wide, bf16)), (h, shape(wide, f32)),
            (h, shape((2 * FREQ, ROWS), bf16)), (h, shape((ROWS, 2 * FREQ), bf16)),
            (h, shape((2 * FREQ, WIDTH), f32)), (h, shape((2 * FREQ, WIDTH), bf16)),
            (h, shape((128, 2 * FREQ), bf16)), (h, shape((ROWS, 128), f32)),
        ],
        [
            pltpu.VMEM((ROWS, 128), i32),
            pltpu.VMEM((96, 2, 8, 128), i32),
            pltpu.VMEM((ROWS, ROWS), f32),
            pltpu.VMEM((128, WIDTH), f32),
            pltpu.VMEM(wide, f32),
            pltpu.VMEM(wide, bf16),
        ],
    )


def unpack(ref, m, out):
    for a in range(PIECES):
        rs = slice(a * 192, a * 192 + 192)
        for ct in range(COLS):
            first = 3 * (ct % 3)
            part = ref[m, a, ct // 3, :, first : first + 3].astype(f32)
            out[rs, ct * 128 : ct * 128 + 128] = part.reshape(192, 128).astype(bf16)


def unpack_bias(ref, out):
    for a in range(PIECES):
        tile = ref[0, a, 0, :, UNITS - 1].astype(f32)
        lane = lanes(tile.shape)
        parts = [jnp.where(lane == rt, tile, 0.0)[:, None] for rt in range(3)]
        column = jnp.concatenate(parts, axis=1).reshape(192, 128)
        out[a * 192 : a * 192 + 192, WIDTH:] = column.astype(bf16)


def ffn_blocks(rows, wu, wd, act, slope, acc):
    acc[...] = jnp.zeros(acc.shape, f32)

    def block(i, carry):
        hs = pl.ds(pl.multiple_of(i * 256, 256), 256)
        upper = dot_last(rows[...], wu[hs, :])
        cdf = 0.5 * (1.0 + lax.erf(upper * math.sqrt(0.5)))
        a = (upper * cdf).astype(bf16)
        act[:, hs] = a
        density = jnp.exp(-0.5 * upper * upper) * (1.0 / math.sqrt(2.0 * math.pi))
        slope[:, hs] = (cdf + upper * density).astype(bf16)
        acc[...] += dot(a, wd[hs, :])
        return carry

    lax.fori_loop(0, HIDDEN // 256, block, 0)


def unpack_kernel(w, wu, wd):
    unpack(w, 0, wu)
    unpack_bias(w, wu)
    unpack(w, 1, wd)


def unpack_weights(weights):
    return staged_call(
        unpack_kernel, "unpack", 12, [("pair", weights)],
        [("vmem", shape((HIDDEN, WIDTH + 128), bf16)), ("vmem", shape((HIDDEN, WIDTH), bf16))],
    )


def ffn_kernel(own, sib, wu, wd, act, slope, part_own, part_sib, rows_out, rows, acc):
    rows[0:ROWS, 0:WIDTH] = own[...]
    rows[ROWS:, 0:WIDTH] = sib[...]
    rows[:, WIDTH:] = jnp.where(lanes((2 * ROWS, 128)) < 3, 1.0, 0.0).astype(bf16)
    rows_out[...] = rows[:, 0:WIDTH]
    ffn_blocks(rows, wu, wd, act, slope, acc)
    part_own[...] = acc[0:ROWS]
    part_sib[...] = acc[ROWS:].astype(bf16)


def ffn(*args):
    wide = (ROWS, WIDTH)
    tall = shape((2 * ROWS, WIDTH), bf16)
    outs = (tall, tall, shape(wide, f32), shape(wide, bf16), tall)
    return staged_call(
        ffn_kernel, "ffn", 20, [("vmem", a) for a in args], [("vmem", o) for o in outs],
        [pltpu.VMEM((2 * ROWS, WIDTH + 128), bf16), pltpu.VMEM((2 * ROWS, WIDTH), f32)],
    )


def combine_kernel(own, got, out):
    out[...] = (own[...] + got[...].astype(f32)).astype(bf16)


def combine(own, got):
    return pl.pallas_call(
        combine_kernel,
        out_shape=shape((ROWS, WIDTH), bf16),
        in_specs=[VMEM] * 2,
        out_specs=VMEM,
        compiler_params=params(16),
        name="combine",
    )(own, got)


def gather_rows(own, near, far):
    return own[...] + near[...].astype(f32) + far[...].astype(f32)


def second_norm(n1, own, near, far, bd, ga, sa, gf, og):
    first = n1[...] * ga[...].astype(f32) + sa[...].astype(f32)
    n, inv = norm_rows(first + gather_rows(own, near, far) + bd[...].astype(f32))
    g = og[...].astype(f32)
    return n, g, norm_back(g, n, inv, gf[...].astype(f32))


def middle_kernel(n1, own, near, far, bd, ga, sa, gf, og, low):
    low[...] = second_norm(n1, own, near, far, bd, ga, sa, gf, og)[2].astype(bf16)


def middle(*args):
    return pl.pallas_call(
        middle_kernel,
        out_shape=shape((ROWS, WIDTH), bf16),
        in_specs=[VMEM] * len(args),
        out_specs=VMEM,
        compiler_params=params(16),
        name="middle",
    )(*args)


def outputs_kernel(
    n1, own, near, far, bd, ga, sa, gf, og, sf, out, second, sums,
):
    n, g, grad = second_norm(n1, own, near, far, bd, ga, sa, gf, og)
    out[...] = (n * gf[...].astype(f32) + sf[...].astype(f32)).astype(bf16)
    second[...] = grad
    sums[0:1] = jnp.sum(grad.astype(bf16).astype(f32), axis=0, keepdims=True)
    sums[1:2] = jnp.sum(g * n, axis=0, keepdims=True)
    sums[2:3] = jnp.sum(g, axis=0, keepdims=True)
    sums[3:8] = jnp.zeros((5, WIDTH), f32)


def outputs(*args):
    wide = (ROWS, WIDTH)
    return staged_call(
        outputs_kernel, "outputs", 16, [("vmem", a) for a in args],
        [("hbm", shape(wide, bf16)), ("hbm", shape(wide, f32)), ("hbm", shape((8, WIDTH), f32))],
    )


def back_blocks(g, wu, wd, slope, u_out, bias, acc):
    acc[...] = jnp.zeros(acc.shape, f32)
    bias[...] = jnp.zeros((8, HIDDEN), f32)

    def block(i, carry):
        hs = pl.ds(pl.multiple_of(i * 256, 256), 256)
        u = (dot_last(g[...], wd[hs, :]) * slope[:, hs].astype(f32)).astype(bf16)
        u_out[:, hs] = u
        bias[0:1, hs] = jnp.sum(u.astype(f32), axis=0, keepdims=True)
        acc[...] += dot(u, wu[hs, 0:WIDTH])
        return carry

    lax.fori_loop(0, HIDDEN // 256, block, 0)


def back_ffn_kernel(own, sib, wu, wd, slope, first_own, first_sib, g, u, bias, acc):
    g[0:ROWS] = own[...]
    g[ROWS:] = sib[...]
    back_blocks(g, wu, wd, slope, u, bias, acc)
    first_own[...] = acc[0:ROWS]
    first_sib[...] = acc[ROWS:].astype(bf16)


def back_ffn(name, *args):
    wide = (ROWS, WIDTH)
    tall = shape((2 * ROWS, WIDTH), bf16)
    return staged_call(
        back_ffn_kernel, name, 20, [("vmem", a) for a in args],
        [
            ("hbm" if name == "back_near" else "vmem", shape(wide, f32)), ("vmem", shape(wide, bf16)),
            ("vmem", tall), ("vmem", tall), ("hbm", shape((8, HIDDEN), f32)),
        ],
        [pltpu.VMEM((2 * ROWS, WIDTH), f32)],
    )


def pack_kernel(gu, gd, grads):
    def piece(a, carry):
        rs = pl.ds(pl.multiple_of(a * 192, 192), 192)
        for m, ref in enumerate((gu, gd)):
            for ct in range(COLS):
                us = slice(3 * (ct % 3), 3 * (ct % 3) + 3)
                part = ref[rs, ct * 128 : ct * 128 + 128].astype(f32).reshape(8, 3, 8, 128)
                grads[m, a, ct // 3, :, us] = part.astype(bf16)
        return carry

    lax.fori_loop(0, PIECES, piece, 0)


def pack(*args):
    return staged_call(
        pack_kernel, "pack", 12, [("vmem", a) for a in args],
        [("hbm", shape((2, PIECES, 2, 8, GRAD_UNITS, 8, 128), bf16))],
    )[0]


def back_kernel(
    place, own, near, far, second, n1, inv1, ga, ctx, wo, nrm, scl, wave, wavet, ks, vs, tapt, col, live, x,
    wv, sums, bias_n, bias_f, in_grad, keep, give, buf_a, buf_b, mb,
):
    first_grad = second[...] + gather_rows(own, near, far)
    n = n1[...]
    buf_a[768 + 2 : 768 + 3] = jnp.sum(first_grad * n, axis=0, keepdims=True)
    buf_a[768 + 3 : 768 + 4] = jnp.sum(first_grad, axis=0, keepdims=True)
    resid = norm_back(first_grad, n, inv1[...][:, 0:1], ga[...].astype(f32))
    ag = resid.astype(bf16)
    buf_a[768 + 1 : 768 + 2] = jnp.sum(ag.astype(f32), axis=0, keepdims=True)
    buf_a[768 + 4 : 768 + 7] = sums[0:3]
    buf_a[768 + 7 :] = jnp.zeros((TALL - 775, WIDTH), f32)
    mine = lax.broadcasted_iota(i32, (8, WIDTH), 0) == place[0] % CLASSES
    bias = jnp.broadcast_to(bias_n[0:1] + bias_f[0:1], (8, WIDTH))
    buf_a[776:784] = jnp.where(mine, bias, 0.0)
    buf_b[0:768] = dot_first(ctx[...], ag)
    cg = dot_last(ag, wo[...])
    mb[...] = cg
    first_head = lanes((ROWS, 128)) < HEAD_DIM
    nrm.ready()
    scl.ready()
    col.ready()

    def heads(b, carry):
        cs = pl.ds(pl.multiple_of(b * 128, 128), 128)
        c = mb[:, cs]
        m = nrm[:, cs].astype(f32)
        prod = c * m
        one = jnp.sum(jnp.where(first_head, prod, 0.0), axis=1, keepdims=True)
        two = jnp.sum(jnp.where(first_head, 0.0, prod), axis=1, keepdims=True)
        mean = jnp.where(first_head, one, two) * (1.0 / HEAD_DIM)
        block = (scl[:, cs] * (c - m * mean)).astype(bf16)
        mb[:, cs] = jnp.where(
            first_head, dot_first(col[2 * b], block), dot_first(col[2 * b + 1], block)
        )
        return carry

    lax.fori_loop(0, COLS, heads, 0)
    spec = dot(wave[...], cg.astype(bf16))
    g_cos = spec[0:FREQ]
    g_sin = spec[FREQ:]
    k_cos = ks[0:FREQ]
    k_sin = ks[FREQ:]
    z_cos = (k_cos * g_cos - k_sin * g_sin).astype(bf16)
    z_sin = (k_cos * g_sin + k_sin * g_cos).astype(bf16)
    conv = dot(wavet[:, 0:FREQ], z_cos) + dot(wavet[:, FREQ:], z_sin)
    v_cos = vs[0:FREQ].astype(f32)
    v_sin = vs[FREQ:].astype(f32)
    f = lax.broadcasted_iota(i32, (FREQ, 1), 0)
    weight = jnp.where((f == 0) | (f == DFT_LEN // 2), 1.0 / DFT_LEN, 2.0 / DFT_LEN)
    weight = jnp.where(f < LIVE_FREQ, weight, 0.0)
    re = ((g_cos * v_cos + g_sin * v_sin) * weight).astype(bf16)
    im = ((g_cos * v_sin - g_sin * v_cos) * weight).astype(bf16)
    gk = dot(tapt[:, 0:FREQ], re) + dot(tapt[:, FREQ:], im)
    buf_b[768:] = jnp.zeros((TALL - 768, WIDTH), f32)
    buf_b[768 : 768 + TAPS] = gk[0:TAPS]
    vg = ((mb[...] + conv) * live[...][:, 0:1]).astype(bf16)
    buf_a[768:769] = jnp.sum(vg.astype(f32), axis=0, keepdims=True)
    buf_a[0:768] = dot_first(x[...], vg)
    in_grad[...] = resid + dot_last(vg, wv[...])

    def write(kept, given):
        for ct in range(COLS):
            cs = slice(ct * 128, ct * 128 + 128)
            ts = slice(ct * TALL_TILES, ct * TALL_TILES + TALL_TILES)
            keep[ts] = kept[:, cs].reshape(TALL_TILES, 8, 128).astype(bf16)
            give[ts] = given[:, cs].reshape(TALL_TILES, 8, 128).astype(bf16)

    rest = PACK - COLS * TALL_TILES
    keep[PACK - rest :] = jnp.zeros((rest, 8, 128), bf16)
    give[PACK - rest :] = jnp.zeros((rest, 8, 128), bf16)

    @pl.when(place[0] % 2 == 0)
    def _():
        write(buf_a, buf_b)

    @pl.when(place[0] % 2 == 1)
    def _():
        write(buf_b, buf_a)


def attend_back(*args):
    wide = (ROWS, WIDTH)
    packed = shape((PACK, 8, 128), bf16)
    kinds = ["smem"] + ["hbm"] * (len(args) - 1)
    for i in (2, 3, 7):
        kinds[i] = "vmem"
    return staged_call(
        back_kernel, "attend_back", 40, list(zip(kinds, args, strict=True)),
        [("hbm", shape(wide, f32)), ("vmem", packed), ("vmem", packed)],
        [
            pltpu.VMEM((TALL, WIDTH), f32),
            pltpu.VMEM((TALL, WIDTH), f32),
            pltpu.VMEM(wide, f32),
        ],
    )


def sum_ffn_kernel(got, out, acc):
    step = pl.program_id(0)

    @pl.when(step == 0)
    def _():
        acc[...] = jnp.zeros(acc.shape, f32)

    for q in range(CLASSES):
        total = acc[q]
        for t in range(8):
            total = total + got[q * 8 + t].astype(f32)
        acc[q] = total

    @pl.when(step == 3)
    def _():
        out[...] = acc[...].astype(bf16)


def sum_ffn(got):
    return pl.pallas_call(
        sum_ffn_kernel,
        grid=(4,),
        out_shape=shape((CLASSES, GRAD_UNITS, 8, 128), bf16),
        in_specs=[pl.BlockSpec((32, GRAD_UNITS, 8, 128), lambda i: (i, 0, 0, 0))],
        out_specs=pl.BlockSpec((CLASSES, GRAD_UNITS, 8, 128), lambda i: (0, 0, 0, 0)),
        scratch_shapes=[pltpu.VMEM((CLASSES, GRAD_UNITS, 8, 128), f32)],
        compiler_params=params(32),
        name="sum_ffn",
    )(got)


def sum_rest_kernel(got, out):
    per = PACK // 128
    total = [jnp.zeros((per, 8, 128), f32) for _ in range(2)]
    for i in range(8):
        for c in range(2):
            for t in range(8):
                total[c] = total[c] + got[i * 16 + c * 8 + t].astype(f32)
    low = [t.astype(bf16) for t in total]
    for i in range(8):
        for c in range(2):
            for t in range(8):
                out[i * 16 + c * 8 + t] = low[c]


def sum_rest(got):
    return pl.pallas_call(
        sum_rest_kernel,
        out_shape=shape(got.shape, bf16),
        in_specs=[VMEM],
        out_specs=VMEM,
        compiler_params=params(32),
        name="sum_rest",
    )(got)


def final_ffn_kernel(place, ffn_own, ffn_oth, g_up, g_down, tall):
    ct = pl.program_id(0)
    core = place[0] % 2
    x_lo = place[0] // 8
    half = ct // 3

    def spread(up_ref, down_ref):
        for a in range(PIECES):
            at = (place[0] // 2 % 4 + 4 - a) % 4 * 2
            up = up_ref[at + (half + x_lo) % 2].astype(f32)
            down = down_ref[at + (half + x_lo + 1) % 2].astype(f32)
            for q in range(CLASSES):
                rs = slice(SUB * q + PIECE * a, SUB * q + PIECE * a + PIECE)
                tall[rs, :] = up[q].reshape(PIECE, 128)
                g_down[rs, :] = down[q].reshape(PIECE, 128)

    @pl.when(x_lo == core)
    def _():
        spread(ffn_own, ffn_oth)

    @pl.when(x_lo != core)
    def _():
        spread(ffn_oth, ffn_own)

    g_up[...] = tall[...].T


def final_ffn(place, ffn_own, ffn_oth):
    units = pl.BlockSpec((8, CLASSES, 3, 8, 128), lambda i: (0, 0, i % 3, 0, 0))
    return pl.pallas_call(
        final_ffn_kernel,
        grid=(COLS,),
        out_shape=(shape((768, 384), f32), shape((384, 768), f32)),
        in_specs=[SMEM, units, units],
        out_specs=(
            pl.BlockSpec((128, 384), lambda i: (i, 0)),
            pl.BlockSpec((384, 128), lambda i: (0, i)),
        ),
        scratch_shapes=[pltpu.VMEM((384, 128), f32)],
        compiler_params=params(16),
        name="final_ffn",
    )(place, ffn_own, ffn_oth)


def final_kernel(
    place, own, other, g_wv, g_bv, g_conv, g_wo, g_bo, g_ga, g_sa, g_bup, g_bd, g_gf, g_sf, vecs,
    bias, line,
):
    step = pl.program_id(0)

    def write(a, b):
        for j in range(3):
            cs = slice(j * 128, j * 128 + 128)
            at = j * TALL_TILES
            g_wv[:, cs] = a[at : at + 96].astype(f32).reshape(768, 128)
            vecs[step * 3 + j] = a[at + 96].astype(f32)
            bias[step * 3 + j] = a[at + 97].astype(f32)
            g_wo[:, cs] = b[at : at + 96].astype(f32).reshape(768, 128)
            g_conv[:, cs] = b[at + 96 : at + 105].astype(f32).reshape(72, 128)[0:TAPS]

    @pl.when(place[0] % 2 == 0)
    def _():
        write(own, other)

    @pl.when(place[0] % 2 == 1)
    def _():
        write(other, own)

    @pl.when(step == COLS // 3 - 1)
    def _():
        for j, ref in enumerate((g_bv, g_bo, g_ga, g_sa, g_bd, g_gf, g_sf)):
            for i in range(COLS):
                ref[i * 128 : i * 128 + 128] = vecs[i, j]
        n = lanes((128, 128))
        a = (n >= PIECE).astype(i32) + (n >= 2 * PIECE).astype(i32) + (n >= 3 * PIECE).astype(i32)
        at = (8 * a + place[1]) * PIECE + n - PIECE * a
        total = jnp.zeros((8, 128), f32)
        for i in range(COLS):
            pick = lax.broadcasted_iota(i32, (128, 128), 0) + 128 * i == at
            total = total + dot(bias[i].astype(bf16), jnp.where(pick, 1.0, 0.0).astype(bf16))
        for q in range(CLASSES):
            line[0:1, SUB * q : SUB * q + SUB] = total[q : q + 1, 0:SUB]
        g_bup[...] = line[...][0]


def final(place, own, other):
    tile = pl.BlockSpec((3 * TALL_TILES, 8, 128), lambda i: (i, 0, 0))
    tall = pl.BlockSpec((768, 384), lambda i: (0, i))
    vec = pl.BlockSpec((WIDTH,), lambda i: (0,))
    v = shape((WIDTH,), f32)
    return pl.pallas_call(
        final_kernel,
        grid=(COLS // 3,),
        out_shape=(
            shape((768, 768), f32), v, shape((TAPS, 768), f32), shape((768, 768), f32), v, v, v,
            shape((384,), f32), v, v, v,
        ),
        in_specs=[SMEM, tile, tile],
        out_specs=(
            tall, vec, pl.BlockSpec((TAPS, 384), lambda i: (0, i)), tall, vec, vec, vec,
            pl.BlockSpec((384,), lambda i: (0,)), vec, vec, vec,
        ),
        scratch_shapes=[
            pltpu.VMEM((COLS, 8, 128), f32),
            pltpu.VMEM((COLS, 8, 128), f32),
            pltpu.VMEM((1, 384), f32),
        ],
        compiler_params=params(16),
        name="final",
    )(place, own, other)


def body(
    block_input,
    w_value,
    b_value,
    conv_kernel,
    w_out,
    b_out,
    gain_attn,
    shift_attn,
    w_up,
    b_up,
    w_down,
    b_down,
    gain_ffn,
    shift_ffn,
    query_codes,
    key_codes,
    key_live,
    seq_lengths,
    out_grad,
):
    dp = lax.axis_index("dp")
    place = jnp.stack([dp, lax.axis_index("tensor")]).astype(i32)
    n_dp = lax.axis_size("dp")

    def shift(i, by):
        return i // 8 * 8 + (i // 2 + by) % 4 * 2 + i % 2

    def swap(x):
        return lax.ppermute(x, "dp", [(i, i ^ 1) for i in range(n_dp)])

    def away(x):
        pairs = [(i, shift(i, 1 - i % 2 * 2)) for i in range(n_dp)]
        return lax.ppermute(x, "dp", pairs)

    def home(x):
        pairs = [(shift(i, 1 - i % 2 * 2), i) for i in range(n_dp)]
        return lax.ppermute(x, "dp", pairs)

    def exchange(x):
        return lax.all_to_all(x, ALL, 0, 0, tiled=True)

    def row(v):
        return v.reshape(1, -1)

    weights = exchange(prep(place, w_up, w_down, b_up))
    weights = weights.reshape(2, PIECES, 2, 8, UNITS, 8, 128)
    (n1, inv1, low, ctx, collide, nrm, scl, wave, wavet, ks, vs, tapt, live) = attend(
        seq_lengths, block_input, w_value, row(b_value), conv_kernel, w_out, row(b_out),
        row(gain_attn), row(shift_attn), query_codes, key_codes, row(key_live),
    )
    low_sib = swap(low)
    got = away(low)
    wu, wd = unpack_weights(weights)
    act_f, slope_f, far_own, far_sib, rows_f = ffn(got, swap(got), wu, wd)
    sent = combine(far_own, swap(far_sib))
    wu, sent = lax.optimization_barrier((wu, sent))
    act_n, slope_n, near_own, near_sib, rows_n = ffn(low, low_sib, wu, wd)
    near_sib, far = lax.optimization_barrier((near_sib, home(sent)))
    second_args = (
        n1, near_own, swap(near_sib), far, row(b_down), row(gain_attn), row(shift_attn),
        row(gain_ffn), out_grad,
    )
    grad = middle(*second_args)
    got = away(grad)
    near_own, near_sib, g_n, u_n, bias_n = back_ffn("back_near", grad, swap(grad), wu, wd, slope_n)
    block_output, second, sums = outputs(*second_args, row(shift_ffn))
    got, near_sib, second = lax.optimization_barrier((got, near_sib, second))
    far_own, far_sib, g_f, u_f, bias_f = back_ffn("back_far", got, swap(got), wu, wd, slope_f)
    sent = combine(far_own, swap(far_sib))
    u_f, sent = lax.optimization_barrier((u_f, sent))
    grad_down = (dot_first(act_n, g_n) + dot_first(act_f, g_f)).astype(bf16)
    grad_up = (dot_first(u_n, rows_n) + dot_first(u_f, rows_f)).astype(bf16)
    grads, far = lax.optimization_barrier((pack(grad_up, grad_down), home(sent)))
    owned = exchange(grads.reshape(128, GRAD_UNITS, 8, 128))
    input_grad, keep, give = attend_back(
        place, near_own, swap(near_sib), far, second, n1, inv1,
        row(gain_attn), ctx, w_out, nrm, scl, wave, wavet, ks, vs, tapt, collide, live, block_input,
        w_value, sums, bias_n, bias_f,
    )
    pair = (keep.astype(f32) + swap(give).astype(f32)).astype(bf16)
    pair = pair.reshape(128, PACK // 128, 8, 128)
    owned = sum_ffn(owned)
    pair, owned = lax.optimization_barrier((pair, owned))
    both = jnp.stack([owned, swap(owned)])
    around = []
    for by in range(4):
        pairs = [(i, (i // 8 ^ i % 2) * 8 + shift(i % 8, by)) for i in range(n_dp)]
        around.append(lax.ppermute(both, "dp", pairs))
    summed = sum_rest(exchange(pair))
    summed, *around = lax.optimization_barrier((summed, *around))
    back = exchange(summed).reshape(PACK, 8, 128)
    ffn_own = jnp.stack(around).reshape(8, CLASSES, GRAD_UNITS, 8, 128)
    g_up, g_down = final_ffn(place, ffn_own, swap(ffn_own))
    back, g_up, g_down = lax.optimization_barrier((back, g_up, g_down))
    g_wv, g_bv, g_conv, g_wo, g_bo, g_ga, g_sa, g_bup, g_bd, g_gf, g_sf = final(
        place, back, swap(back)
    )
    return (
        block_output, input_grad, g_wv, g_bv, g_conv, g_wo, g_bo, g_ga, g_sa, g_up, g_bup, g_down,
        g_bd, g_gf, g_sf,
    )


def solution(mesh):
    rows = P(ALL, None)
    return jax.shard_map(
        body,
        mesh=mesh,
        in_specs=(
            rows, P(), P(), P(), P(), P(), P(), P(),
            P(None, "tensor"), P("tensor"), P("tensor", None), P(), P(), P(),
            rows, rows, P(ALL), rows, rows,
        ),
        out_specs=(
            rows, rows, P(), P(), P(), P(), P(), P(), P(),
            P(None, "tensor"), P("tensor"), P("tensor", None), P(), P(), P(),
        ),
        check_vma=False,
    )
```

```python
import math

import jax
import jax.numpy as jnp
from jax import lax
from jax.experimental import pallas as pl
from jax.experimental.pallas import tpu as pltpu
from jax.sharding import PartitionSpec as P

HEADS = 12
SETS = 32
ROWS = 256
WIDTH = 768
HEAD_DIM = 64
COLS = WIDTH // 128
TAPS = 65
MARGIN = 32
DFT_LEN = 384
FREQ = 256
LIVE_FREQ = DFT_LEN // 2 + 1
CLASSES = 4
SUB = 96
PIECE = 24
PIECES = SUB // PIECE
UNITS = 10
GRAD_UNITS = 9
HIDDEN = 768
TALL = 848
TALL_TILES = TALL // 8
PACK = 640
ALL = ("dp", "tensor")

bf16 = jnp.bfloat16
f32 = jnp.float32
i32 = jnp.int32

VMEM = pl.BlockSpec(memory_space=pltpu.VMEM)
SMEM = pl.BlockSpec(memory_space=pltpu.SMEM)
HBM = pl.BlockSpec(memory_space=pltpu.HBM)


def shape(dims, dtype):
    return jax.ShapeDtypeStruct(dims, dtype)


def params(mib):
    return pltpu.CompilerParams(vmem_limit_bytes=mib << 20)


def dot(a, b):
    return lax.dot_general(a, b, (((1,), (0,)), ((), ())), preferred_element_type=f32)


def dot_last(a, b):
    return lax.dot_general(a, b, (((1,), (1,)), ((), ())), preferred_element_type=f32)


def dot_first(a, b):
    return lax.dot_general(a, b, (((0,), (0,)), ((), ())), preferred_element_type=f32)


def lanes(dims):
    return lax.broadcasted_iota(i32, dims, len(dims) - 1)


def norm_rows(r):
    mean = jnp.mean(r, axis=-1, keepdims=True)
    centred = r - mean
    inv = lax.rsqrt(jnp.mean(centred * centred, axis=-1, keepdims=True) + 1e-05)
    return centred * inv, inv


def norm_back(g, n, inv, gain):
    e = g * gain
    return (
        e - jnp.mean(e, axis=-1, keepdims=True) - n * jnp.mean(e * n, axis=-1, keepdims=True)
    ) * inv


class Staged:
    def __init__(self, ref, buf, sem, incoming):
        pair = (ref, buf) if incoming else (buf, ref)
        self.buf = buf
        self.copy = pltpu.make_async_copy(*pair, sem)
        self.incoming = incoming
        self.pending = True
        if incoming:
            self.copy.start()

    def ready(self):
        if self.pending:
            self.copy.wait()
            self.pending = False

    def leave(self):
        if self.pending:
            self.copy.start()
            self.pending = False

    def __getitem__(self, index):
        if self.incoming:
            self.ready()
        return self.buf[index]

    def __setitem__(self, index, value):
        self.buf[index] = value


class StagedPair:
    def __init__(self, ref, buf, sems):
        self.buf = buf
        self.copies = [pltpu.make_async_copy(ref.at[i], buf.at[i], sems.at[i]) for i in range(2)]
        self.pending = [True, True]
        for copy in self.copies:
            copy.start()

    def ready(self):
        for i in range(2):
            if self.pending[i]:
                self.copies[i].wait()
                self.pending[i] = False

    def __getitem__(self, index):
        i = index[0]
        if self.pending[i]:
            self.copies[i].wait()
            self.pending[i] = False
        return self.buf[index]


def staged_call(kernel, name, mib, ins, outs, scratch=()):
    spec = {"smem": SMEM, "vmem": VMEM, "hbm": HBM, "pair": HBM}
    arrays = [a for _, a in ins]
    kinds = [k for k, _ in ins] + [k for k, _ in outs]
    avals = arrays + [o for _, o in outs]
    staged = [i for i, k in enumerate(kinds) if k in ("hbm", "pair")]
    n_in = len(ins)

    if not staged:
        return pl.pallas_call(
            kernel,
            out_shape=tuple(o for _, o in outs),
            in_specs=[spec[k] for k, _ in ins],
            out_specs=tuple(spec[k] for k, _ in outs),
            scratch_shapes=list(scratch),
            compiler_params=params(mib),
            name=name,
        )(*arrays)

    def run(*refs):
        refs = list(refs)
        sems = refs.pop()
        split = len(refs) - len(staged)
        bufs = refs[split:]
        refs = refs[:split]
        for n, i in enumerate(staged):
            if kinds[i] == "pair":
                refs[i] = StagedPair(refs[i], bufs[n], sems.at[n])
            else:
                refs[i] = Staged(refs[i], bufs[n], sems.at[n, 0], i < n_in)
        kernel(*refs)
        for i in staged:
            if i < n_in:
                refs[i].ready()
            else:
                refs[i].leave()
        for i in staged:
            if i >= n_in:
                refs[i].copy.wait()

    buffers = [pltpu.VMEM(avals[i].shape, avals[i].dtype) for i in staged]
    arrays = [
        a if k in ("smem", "vmem") else pltpu.with_memory_space_constraint(a, pltpu.HBM)
        for k, a in ins
    ]
    return pl.pallas_call(
        run,
        out_shape=tuple(pltpu.HBM(o.shape, o.dtype) if k == "hbm" else o for k, o in outs),
        in_specs=[spec[k] for k, _ in ins],
        out_specs=tuple(spec[k] for k, _ in outs),
        scratch_shapes=[*scratch, *buffers, pltpu.SemaphoreType.DMA((len(staged), 2))],
        compiler_params=params(mib),
        name=name,
    )(*arrays)


def prep_kernel(place, up_ref, down_ref, bias_hbm, out_ref, half, piece, bias_ref, sems):
    rep = place[0] % 8
    is_up = place[0] < 8
    at = pl.ds(pl.multiple_of(rep % 2 * 384, 128), 384)
    up = pltpu.make_async_copy(up_ref.at[at, :], half, sems.at[0])
    down = pltpu.make_async_copy(down_ref.at[:, at], half, sems.at[0])
    bias_copy = pltpu.make_async_copy(bias_hbm, bias_ref, sems.at[33])
    bias_copy.start()

    @pl.when(is_up)
    def _():
        up.start()

    @pl.when(jnp.logical_not(is_up))
    def _():
        down.start()

    n = lax.broadcasted_iota(i32, (SUB, 384), 0)
    q = sum((n >= PIECE * k).astype(i32) for k in range(1, CLASSES))
    unit = (SUB - PIECE) * q + n + PIECE * (rep // 2)
    pick = jnp.where(unit == lanes((SUB, 384)), 1.0, 0.0).astype(bf16)
    scale = jnp.where(is_up & (rep % 2 == 0), 1.0, 0.0)
    bias_copy.wait()
    bias = jnp.broadcast_to(bias_ref[...].astype(f32) * scale, (16, 384)).astype(bf16)
    column = dot_last(pick, bias)[:, 0:1]

    def fill(rows):
        for k in range(CLASSES):
            rs = slice(PIECE * k, PIECE * k + PIECE)
            for j in range(3):
                part = rows[rs, j * 128 : j * 128 + 128].reshape(3, 8, 128)
                piece[k, 3 * j : 3 * j + 3] = part.astype(bf16)
            col = jnp.broadcast_to(column[rs], (PIECE, 128)).reshape(3, 8, 128)
            lane = lanes((8, 128))
            tile = jnp.where(lane == 0, col[0], jnp.where(lane == 1, col[1], col[2]))
            piece[k, UNITS - 1] = tile.astype(bf16)

    @pl.when(is_up)
    def _():
        up.wait()
        fill(dot_last(pick, half[...]))

    @pl.when(jnp.logical_not(is_up))
    def _():
        down.wait()
        fill(dot(pick, half[...]))

    copies = [
        pltpu.make_async_copy(piece, out_ref.at[g, :, t], sems.at[1 + 8 * g + t])
        for g in range(4)
        for t in range(8)
    ]
    for copy in copies:
        copy.start()
    for copy in copies:
        copy.wait()


def prep(place, w_up, w_down, b_up):
    out = pl.pallas_call(
        prep_kernel,
        out_shape=pltpu.HBM((4, CLASSES, 8, UNITS, 8, 128), bf16),
        in_specs=[SMEM, HBM, HBM, HBM],
        out_specs=HBM,
        scratch_shapes=[
            pltpu.VMEM((384, 384), bf16),
            pltpu.VMEM((CLASSES, UNITS, 8, 128), bf16),
            pltpu.VMEM((384,), bf16),
            pltpu.SemaphoreType.DMA((34,)),
        ],
        compiler_params=params(16),
        name="prep",
    )(
        place,
        pltpu.with_memory_space_constraint(w_up, pltpu.HBM),
        pltpu.with_memory_space_constraint(w_down, pltpu.HBM),
        pltpu.with_memory_space_constraint(b_up, pltpu.HBM),
    )
    return out.reshape(128, UNITS, 8, 128)


def segment_ends(len_ref):
    e0 = len_ref[0, 0]
    e1 = e0 + len_ref[0, 1]
    return e0, e1, e1 + len_ref[0, 2]


def segment_of(p, ends):
    return sum((p >= e).astype(i32) for e in ends)


def turn(product):
    r = product.astype(f32) * (1.0 / DFT_LEN)
    m = product - DFT_LEN * jnp.round(r).astype(i32)
    x = m.astype(f32) * (2.0 * math.pi / DFT_LEN)
    z = x * x
    c = 1.0
    s = 1.0
    for k in range(8, 0, -1):
        c = 1.0 - z * c * (1.0 / ((2 * k - 1) * (2 * k)))
        s = 1.0 - z * s * (1.0 / ((2 * k) * (2 * k + 1)))
    return c, x * s


def attend_kernel(
    len_ref, x_ref, wv_ref, bv_ref, taps_ref, wo_ref, bo_ref, ga_ref, sa_ref, q_ref, k_ref, live_ref,
    n_ref, inv_ref, low_ref, ctx_ref, col_ref, nrm_ref, scl_ref, wave_ref, wavet_ref, ks_ref, vs_ref,
    tapt_ref, live_out, qw, kb, jn, tapbuf, mix, mskd,
):
    ends = segment_ends(len_ref)
    square = (ROWS, ROWS)
    rows_i = lax.broadcasted_iota(i32, square, 0)
    lanes_i = lax.broadcasted_iota(i32, square, 1)
    jn[...] = jnp.where(segment_of(rows_i, ends) == segment_of(lanes_i, ends), 1.0 / SETS, 0.0)
    d = lax.broadcasted_iota(i32, (384, 128), 0) - 4 * lax.broadcasted_iota(i32, (384, 128), 1)
    w_lo = jnp.where(d == 0, 1.0, jnp.where(d == 1, 256.0, 0.0)).astype(bf16)
    w_hi = jnp.where(d == 2, 1.0, jnp.where(d == 3, 256.0, 0.0)).astype(bf16)
    q_codes = q_ref[...].astype(f32).astype(bf16)
    k_codes = k_ref[...].astype(f32).astype(bf16)
    qw[...] = dot(q_codes, w_lo).astype(i32) | (dot(q_codes, w_hi).astype(i32) << 16)
    kw = dot(k_codes, w_lo).T.astype(i32) | (dot(k_codes, w_hi).T.astype(i32) << 16)
    for r in range(96):
        for j in range(2):
            kb[r, j] = jnp.broadcast_to(kw[r : r + 1, j * 128 : j * 128 + 128], (8, 128))
    low7 = jnp.int32(0x7F7F7F7F)
    ones = jnp.int32(0x01010101)
    byte2 = jnp.int32(0x00FF00FF)
    tile_rows = 16
    groups = tile_rows // 8

    def tile(rt, carry):
        rs = pl.ds(pl.multiple_of(rt * tile_rows, tile_rows), tile_rows)
        qt = qw[rs, :]
        for h in range(HEADS):
            acc = [[jnp.zeros((8, 128), i32) for _ in range(2)] for _ in range(groups)]
            for g in range(8):
                c = h * 8 + g
                qc = [
                    jnp.broadcast_to(qt[t * 8 : t * 8 + 8, c : c + 1], (8, 128))
                    for t in range(groups)
                ]
                for j in range(2):
                    kk = kb[c, j]
                    for t in range(groups):
                        x = qc[t] ^ kk
                        y = ((x & low7) + low7) | x
                        acc[t][j] = acc[t][j] + (lax.shift_right_logical(y, 7) & ones)
            for j in range(2):
                parts = []
                for t in range(groups):
                    z = acc[t][j]
                    z = (z & byte2) + (lax.shift_right_logical(z, 8) & byte2)
                    z = (z & jnp.int32(0xFFFF)) + lax.shift_right_logical(z, 16)
                    parts.append((SETS - z).astype(f32))
                m = jnp.concatenate(parts, axis=0) * jn[rs, j * 128 : j * 128 + 128]
                col_ref[h, rs, j * 128 : j * 128 + 128] = m.astype(bf16)
        return carry

    lax.fori_loop(0, ROWS // tile_rows, tile, 0)

    col_ref.leave()

    dims = (FREQ, ROWS)
    f = lax.broadcasted_iota(i32, dims, 0)
    p = lax.broadcasted_iota(i32, dims, 1)
    c, s = turn(f * (p + MARGIN * segment_of(p, ends)))
    ok = f < LIVE_FREQ
    wave_ref[0:FREQ] = jnp.where(ok, c, 0.0).astype(bf16)
    wave_ref[FREQ:] = jnp.where(ok, s, 0.0).astype(bf16)
    p = lax.broadcasted_iota(i32, dims, 0)
    f = lax.broadcasted_iota(i32, dims, 1)
    c, s = turn(f * (p + MARGIN * segment_of(p, ends)))
    ok = f < LIVE_FREQ
    wavet_ref[:, 0:FREQ] = jnp.where(ok, c, 0.0).astype(bf16)
    wavet_ref[:, FREQ:] = jnp.where(ok, s, 0.0).astype(bf16)
    dims = (FREQ, 128)
    f = lax.broadcasted_iota(i32, dims, 0)
    c, s = turn(f * (lax.broadcasted_iota(i32, dims, 1) - MARGIN))
    tap_c = c.astype(bf16)
    tap_s = s.astype(bf16)
    dims = (128, FREQ)
    f = lax.broadcasted_iota(i32, dims, 1)
    c, s = turn(f * (lax.broadcasted_iota(i32, dims, 0) - MARGIN))
    tapt_ref[:, 0:FREQ] = c.astype(bf16)
    tapt_ref[:, FREQ:] = s.astype(bf16)
    tapbuf[...] = jnp.zeros(tapbuf.shape, f32)
    tapbuf[0:TAPS] = taps_ref[...].astype(f32)
    kernel = tapbuf[...].astype(bf16)
    f = lax.broadcasted_iota(i32, (FREQ, 1), 0)
    weight = jnp.where((f == 0) | (f == DFT_LEN // 2), 1.0 / DFT_LEN, 2.0 / DFT_LEN)
    weight = jnp.where(f < LIVE_FREQ, weight, 0.0)
    k_cos = dot(tap_c, kernel) * weight
    k_sin = dot(tap_s, kernel) * weight
    ks_ref[0:FREQ] = k_cos
    ks_ref[FREQ:] = k_sin

    live = jnp.broadcast_to(live_ref[...].astype(f32), (8, ROWS)).T[:, 0:1]
    live_out[...] = jnp.broadcast_to(live, (ROWS, 128))
    values = (dot(x_ref[...], wv_ref[...]) + bv_ref[...].astype(f32)).astype(bf16).astype(f32)
    mskd[...] = (values * live).astype(bf16)
    masked = mskd[...]
    spec = dot(wave_ref[...], masked)
    vs_ref[...] = spec.astype(bf16)
    v_cos = spec[0:FREQ]
    v_sin = spec[FREQ:]
    first_head = lanes((ROWS, 128)) < HEAD_DIM
    y_cos = (k_cos * v_cos + k_sin * v_sin).astype(bf16)
    y_sin = (k_cos * v_sin - k_sin * v_cos).astype(bf16)
    conv = dot(wavet_ref[:, 0:FREQ], y_cos) + dot(wavet_ref[:, FREQ:], y_sin)
    for done in (wave_ref, wavet_ref, tapt_ref, ks_ref, live_out, vs_ref):
        done.leave()

    def heads(b, carry):
        cs = pl.ds(pl.multiple_of(b * 128, 128), 128)
        block = mskd[:, cs]
        m = jnp.where(first_head, dot(col_ref[2 * b], block), dot(col_ref[2 * b + 1], block))
        sq = m * m
        one = jnp.sum(jnp.where(first_head, sq, 0.0), axis=1, keepdims=True)
        two = jnp.sum(jnp.where(first_head, 0.0, sq), axis=1, keepdims=True)
        scale = lax.rsqrt(jnp.where(first_head, one, two) * (1.0 / HEAD_DIM) + 1e-06)
        scl_ref[:, cs] = scale
        nrm = m * scale
        nrm_ref[:, cs] = nrm.astype(bf16)
        mix[:, cs] = nrm
        return carry

    lax.fori_loop(0, COLS, heads, 0)
    context = (mix[...] + conv).astype(bf16)
    ctx_ref[...] = context
    for done in (scl_ref, nrm_ref, ctx_ref):
        done.leave()
    attended = dot(context, wo_ref[...]) + bo_ref[...].astype(f32)
    n, inv = norm_rows(x_ref[...].astype(f32) + attended)
    n_ref[...] = n
    inv_ref[...] = jnp.broadcast_to(inv, (ROWS, 128))
    low_ref[...] = (n * ga_ref[...].astype(f32) + sa_ref[...].astype(f32)).astype(bf16)


def attend(seq_lengths, x, wv, bv, taps, wo, bo, ga, sa, q, k, live):
    wide = (ROWS, WIDTH)
    h = "hbm"
    v = "vmem"
    return staged_call(
        attend_kernel, "attend", 36,
        [
            ("smem", seq_lengths), (h, x), (h, wv), (v, bv), (v, taps), (h, wo), (v, bo), (v, ga),
            (v, sa), (h, q), (h, k), (v, live),
        ],
        [
            (h, shape(wide, f32)), (h, shape((ROWS, 128), f32)), (v, shape(wide, bf16)),
            (h, shape(wide, bf16)),
            (h, shape((HEADS, ROWS, ROWS), bf16)), (h, shape(wide, bf16)), (h, shape(wide, f32)),
            (h, shape((2 * FREQ, ROWS), bf16)), (h, shape((ROWS, 2 * FREQ), bf16)),
            (h, shape((2 * FREQ, WIDTH), f32)), (h, shape((2 * FREQ, WIDTH), bf16)),
            (h, shape((128, 2 * FREQ), bf16)), (h, shape((ROWS, 128), f32)),
        ],
        [
            pltpu.VMEM((ROWS, 128), i32),
            pltpu.VMEM((96, 2, 8, 128), i32),
            pltpu.VMEM((ROWS, ROWS), f32),
            pltpu.VMEM((128, WIDTH), f32),
            pltpu.VMEM(wide, f32),
            pltpu.VMEM(wide, bf16),
        ],
    )


def unpack(ref, m, out):
    for a in range(PIECES):
        rs = slice(a * 192, a * 192 + 192)
        for ct in range(COLS):
            first = 3 * (ct % 3)
            part = ref[m, a, ct // 3, :, first : first + 3].astype(f32)
            out[rs, ct * 128 : ct * 128 + 128] = part.reshape(192, 128).astype(bf16)


def unpack_bias(ref, out):
    for a in range(PIECES):
        tile = ref[0, a, 0, :, UNITS - 1].astype(f32)
        lane = lanes(tile.shape)
        parts = [jnp.where(lane == rt, tile, 0.0)[:, None] for rt in range(3)]
        column = jnp.concatenate(parts, axis=1).reshape(192, 128)
        out[a * 192 : a * 192 + 192, WIDTH:] = column.astype(bf16)


def ffn_blocks(rows, wu, wd, act, slope, acc):
    acc[...] = jnp.zeros(acc.shape, f32)

    def block(i, carry):
        hs = pl.ds(pl.multiple_of(i * 256, 256), 256)
        upper = dot_last(rows[...], wu[hs, :])
        cdf = 0.5 * (1.0 + lax.erf(upper * math.sqrt(0.5)))
        a = (upper * cdf).astype(bf16)
        act[:, hs] = a
        density = jnp.exp(-0.5 * upper * upper) * (1.0 / math.sqrt(2.0 * math.pi))
        slope[:, hs] = (cdf + upper * density).astype(bf16)
        acc[...] += dot(a, wd[hs, :])
        return carry

    lax.fori_loop(0, HIDDEN // 256, block, 0, unroll=True)


def unpack_kernel(w, wu, wd):
    unpack(w, 0, wu)
    unpack_bias(w, wu)
    unpack(w, 1, wd)


def unpack_weights(weights):
    return staged_call(
        unpack_kernel, "unpack", 12, [("pair", weights)],
        [("vmem", shape((HIDDEN, WIDTH + 128), bf16)), ("vmem", shape((HIDDEN, WIDTH), bf16))],
    )


def ffn_kernel(own, sib, wu, wd, act, slope, part_own, part_sib, rows_out, rows, acc):
    rows[0:ROWS, 0:WIDTH] = own[...]
    rows[ROWS:, 0:WIDTH] = sib[...]
    rows[:, WIDTH:] = jnp.where(lanes((2 * ROWS, 128)) < 3, 1.0, 0.0).astype(bf16)
    rows_out[...] = rows[:, 0:WIDTH]
    ffn_blocks(rows, wu, wd, act, slope, acc)
    part_own[...] = acc[0:ROWS]
    part_sib[...] = acc[ROWS:].astype(bf16)


def ffn(*args):
    wide = (ROWS, WIDTH)
    tall = shape((2 * ROWS, WIDTH), bf16)
    outs = (tall, tall, shape(wide, f32), shape(wide, bf16), tall)
    return staged_call(
        ffn_kernel, "ffn", 20, [("vmem", a) for a in args], [("vmem", o) for o in outs],
        [pltpu.VMEM((2 * ROWS, WIDTH + 128), bf16), pltpu.VMEM((2 * ROWS, WIDTH), f32)],
    )


def combine_kernel(own, got, out):
    out[...] = (own[...] + got[...].astype(f32)).astype(bf16)


def combine(own, got):
    return pl.pallas_call(
        combine_kernel,
        out_shape=shape((ROWS, WIDTH), bf16),
        in_specs=[VMEM] * 2,
        out_specs=VMEM,
        compiler_params=params(16),
        name="combine",
    )(own, got)


def gather_rows(own, near, far):
    return own[...] + near[...].astype(f32) + far[...].astype(f32)


def second_norm(n1, own, near, far, bd, ga, sa, gf, og):
    first = n1[...] * ga[...].astype(f32) + sa[...].astype(f32)
    n, inv = norm_rows(first + gather_rows(own, near, far) + bd[...].astype(f32))
    g = og[...].astype(f32)
    return n, g, norm_back(g, n, inv, gf[...].astype(f32))


def middle_kernel(n1, own, near, far, bd, ga, sa, gf, og, low):
    low[...] = second_norm(n1, own, near, far, bd, ga, sa, gf, og)[2].astype(bf16)


def middle(*args):
    return pl.pallas_call(
        middle_kernel,
        out_shape=shape((ROWS, WIDTH), bf16),
        in_specs=[VMEM] * len(args),
        out_specs=VMEM,
        compiler_params=params(16),
        name="middle",
    )(*args)


def outputs_kernel(
    n1, own, near, far, bd, ga, sa, gf, og, sf, out, second, sums,
):
    n, g, grad = second_norm(n1, own, near, far, bd, ga, sa, gf, og)
    out[...] = (n * gf[...].astype(f32) + sf[...].astype(f32)).astype(bf16)
    second[...] = grad
    sums[0:1] = jnp.sum(grad.astype(bf16).astype(f32), axis=0, keepdims=True)
    sums[1:2] = jnp.sum(g * n, axis=0, keepdims=True)
    sums[2:3] = jnp.sum(g, axis=0, keepdims=True)
    sums[3:8] = jnp.zeros((5, WIDTH), f32)


def outputs(*args):
    wide = (ROWS, WIDTH)
    return staged_call(
        outputs_kernel, "outputs", 16, [("vmem", a) for a in args],
        [("hbm", shape(wide, bf16)), ("hbm", shape(wide, f32)), ("hbm", shape((8, WIDTH), f32))],
    )


def back_blocks(g, wu, wd, slope, u_out, bias, acc):
    acc[...] = jnp.zeros(acc.shape, f32)
    bias[...] = jnp.zeros((8, HIDDEN), f32)

    def block(i, carry):
        hs = pl.ds(pl.multiple_of(i * 256, 256), 256)
        u = (dot_last(g[...], wd[hs, :]) * slope[:, hs].astype(f32)).astype(bf16)
        u_out[:, hs] = u
        bias[0:1, hs] = jnp.sum(u.astype(f32), axis=0, keepdims=True)
        acc[...] += dot(u, wu[hs, 0:WIDTH])
        return carry

    lax.fori_loop(0, HIDDEN // 256, block, 0, unroll=True)


def back_ffn_kernel(own, sib, wu, wd, slope, first_own, first_sib, g, u, bias, acc):
    g[0:ROWS] = own[...]
    g[ROWS:] = sib[...]
    back_blocks(g, wu, wd, slope, u, bias, acc)
    first_own[...] = acc[0:ROWS]
    first_sib[...] = acc[ROWS:].astype(bf16)


def back_ffn(name, *args):
    wide = (ROWS, WIDTH)
    tall = shape((2 * ROWS, WIDTH), bf16)
    return staged_call(
        back_ffn_kernel, name, 20, [("vmem", a) for a in args],
        [
            ("hbm" if name == "back_near" else "vmem", shape(wide, f32)), ("vmem", shape(wide, bf16)),
            ("vmem", tall), ("vmem", tall), ("hbm", shape((8, HIDDEN), f32)),
        ],
        [pltpu.VMEM((2 * ROWS, WIDTH), f32)],
    )


def pack_kernel(gu, gd, grads):
    def piece(a, carry):
        rs = pl.ds(pl.multiple_of(a * 192, 192), 192)
        for m, ref in enumerate((gu, gd)):
            for ct in range(COLS):
                us = slice(3 * (ct % 3), 3 * (ct % 3) + 3)
                part = ref[rs, ct * 128 : ct * 128 + 128].astype(f32).reshape(8, 3, 8, 128)
                grads[m, a, ct // 3, :, us] = part.astype(bf16)
        return carry

    lax.fori_loop(0, PIECES, piece, 0)


def pack(*args):
    return staged_call(
        pack_kernel, "pack", 12, [("vmem", a) for a in args],
        [("hbm", shape((2, PIECES, 2, 8, GRAD_UNITS, 8, 128), bf16))],
    )[0]


def back_kernel(
    place, own, near, far, second, n1, inv1, ga, ctx, wo, nrm, scl, wave, wavet, ks, vs, tapt, col, live, x,
    wv, sums, bias_n, bias_f, in_grad, keep, give, buf_a, buf_b, mb,
):
    first_grad = second[...] + gather_rows(own, near, far)
    n = n1[...]
    buf_a[768 + 2 : 768 + 3] = jnp.sum(first_grad * n, axis=0, keepdims=True)
    buf_a[768 + 3 : 768 + 4] = jnp.sum(first_grad, axis=0, keepdims=True)
    resid = norm_back(first_grad, n, inv1[...][:, 0:1], ga[...].astype(f32))
    ag = resid.astype(bf16)
    buf_a[768 + 1 : 768 + 2] = jnp.sum(ag.astype(f32), axis=0, keepdims=True)
    buf_a[768 + 4 : 768 + 7] = sums[0:3]
    buf_a[768 + 7 :] = jnp.zeros((TALL - 775, WIDTH), f32)
    mine = lax.broadcasted_iota(i32, (8, WIDTH), 0) == place[0] % CLASSES
    bias = jnp.broadcast_to(bias_n[0:1] + bias_f[0:1], (8, WIDTH))
    buf_a[776:784] = jnp.where(mine, bias, 0.0)
    buf_b[0:768] = dot_first(ctx[...], ag)
    cg = dot_last(ag, wo[...])
    mb[...] = cg
    first_head = lanes((ROWS, 128)) < HEAD_DIM
    nrm.ready()
    scl.ready()
    col.ready()

    def heads(b, carry):
        cs = pl.ds(pl.multiple_of(b * 128, 128), 128)
        c = mb[:, cs]
        m = nrm[:, cs].astype(f32)
        prod = c * m
        one = jnp.sum(jnp.where(first_head, prod, 0.0), axis=1, keepdims=True)
        two = jnp.sum(jnp.where(first_head, 0.0, prod), axis=1, keepdims=True)
        mean = jnp.where(first_head, one, two) * (1.0 / HEAD_DIM)
        block = (scl[:, cs] * (c - m * mean)).astype(bf16)
        mb[:, cs] = jnp.where(
            first_head, dot_first(col[2 * b], block), dot_first(col[2 * b + 1], block)
        )
        return carry

    lax.fori_loop(0, COLS, heads, 0)
    spec = dot(wave[...], cg.astype(bf16))
    g_cos = spec[0:FREQ]
    g_sin = spec[FREQ:]
    k_cos = ks[0:FREQ]
    k_sin = ks[FREQ:]
    z_cos = (k_cos * g_cos - k_sin * g_sin).astype(bf16)
    z_sin = (k_cos * g_sin + k_sin * g_cos).astype(bf16)
    conv = dot(wavet[:, 0:FREQ], z_cos) + dot(wavet[:, FREQ:], z_sin)
    v_cos = vs[0:FREQ].astype(f32)
    v_sin = vs[FREQ:].astype(f32)
    f = lax.broadcasted_iota(i32, (FREQ, 1), 0)
    weight = jnp.where((f == 0) | (f == DFT_LEN // 2), 1.0 / DFT_LEN, 2.0 / DFT_LEN)
    weight = jnp.where(f < LIVE_FREQ, weight, 0.0)
    re = ((g_cos * v_cos + g_sin * v_sin) * weight).astype(bf16)
    im = ((g_cos * v_sin - g_sin * v_cos) * weight).astype(bf16)
    gk = dot(tapt[:, 0:FREQ], re) + dot(tapt[:, FREQ:], im)
    buf_b[768:] = jnp.zeros((TALL - 768, WIDTH), f32)
    buf_b[768 : 768 + TAPS] = gk[0:TAPS]
    vg = ((mb[...] + conv) * live[...][:, 0:1]).astype(bf16)
    buf_a[768:769] = jnp.sum(vg.astype(f32), axis=0, keepdims=True)
    buf_a[0:768] = dot_first(x[...], vg)
    in_grad[...] = resid + dot_last(vg, wv[...])

    def write(kept, given):
        for ct in range(COLS):
            cs = slice(ct * 128, ct * 128 + 128)
            ts = slice(ct * TALL_TILES, ct * TALL_TILES + TALL_TILES)
            keep[ts] = kept[:, cs].reshape(TALL_TILES, 8, 128).astype(bf16)
            give[ts] = given[:, cs].reshape(TALL_TILES, 8, 128).astype(bf16)

    rest = PACK - COLS * TALL_TILES
    keep[PACK - rest :] = jnp.zeros((rest, 8, 128), bf16)
    give[PACK - rest :] = jnp.zeros((rest, 8, 128), bf16)

    @pl.when(place[0] % 2 == 0)
    def _():
        write(buf_a, buf_b)

    @pl.when(place[0] % 2 == 1)
    def _():
        write(buf_b, buf_a)


def attend_back(*args):
    wide = (ROWS, WIDTH)
    packed = shape((PACK, 8, 128), bf16)
    kinds = ["smem"] + ["hbm"] * (len(args) - 1)
    for i in (2, 3, 7):
        kinds[i] = "vmem"
    return staged_call(
        back_kernel, "attend_back", 40, list(zip(kinds, args, strict=True)),
        [("hbm", shape(wide, f32)), ("vmem", packed), ("vmem", packed)],
        [
            pltpu.VMEM((TALL, WIDTH), f32),
            pltpu.VMEM((TALL, WIDTH), f32),
            pltpu.VMEM(wide, f32),
        ],
    )


def sum_ffn_kernel(got, out, acc):
    step = pl.program_id(0)

    @pl.when(step == 0)
    def _():
        acc[...] = jnp.zeros(acc.shape, f32)

    for q in range(CLASSES):
        total = acc[q]
        for t in range(8):
            total = total + got[q * 8 + t].astype(f32)
        acc[q] = total

    @pl.when(step == 3)
    def _():
        out[...] = acc[...].astype(bf16)


def sum_ffn(got):
    return pl.pallas_call(
        sum_ffn_kernel,
        grid=(4,),
        out_shape=shape((CLASSES, GRAD_UNITS, 8, 128), bf16),
        in_specs=[pl.BlockSpec((32, GRAD_UNITS, 8, 128), lambda i: (i, 0, 0, 0))],
        out_specs=pl.BlockSpec((CLASSES, GRAD_UNITS, 8, 128), lambda i: (0, 0, 0, 0)),
        scratch_shapes=[pltpu.VMEM((CLASSES, GRAD_UNITS, 8, 128), f32)],
        compiler_params=params(32),
        name="sum_ffn",
    )(got)


def sum_rest_kernel(got, out):
    per = PACK // 128
    total = [jnp.zeros((per, 8, 128), f32) for _ in range(2)]
    for i in range(8):
        for c in range(2):
            for t in range(8):
                total[c] = total[c] + got[i * 16 + c * 8 + t].astype(f32)
    low = [t.astype(bf16) for t in total]
    for i in range(8):
        for c in range(2):
            for t in range(8):
                out[i * 16 + c * 8 + t] = low[c]


def sum_rest(got):
    return pl.pallas_call(
        sum_rest_kernel,
        out_shape=shape(got.shape, bf16),
        in_specs=[VMEM],
        out_specs=VMEM,
        compiler_params=params(32),
        name="sum_rest",
    )(got)


def final_ffn_kernel(place, ffn_own, ffn_oth, g_up, g_down, tall):
    ct = pl.program_id(0)
    core = place[0] % 2
    x_lo = place[0] // 8
    half = ct // 3

    def spread(up_ref, down_ref):
        for a in range(PIECES):
            at = (place[0] // 2 % 4 + 4 - a) % 4 * 2
            up = up_ref[at + (half + x_lo) % 2].astype(f32)
            down = down_ref[at + (half + x_lo + 1) % 2].astype(f32)
            for q in range(CLASSES):
                rs = slice(SUB * q + PIECE * a, SUB * q + PIECE * a + PIECE)
                tall[rs, :] = up[q].reshape(PIECE, 128)
                g_down[rs, :] = down[q].reshape(PIECE, 128)

    @pl.when(x_lo == core)
    def _():
        spread(ffn_own, ffn_oth)

    @pl.when(x_lo != core)
    def _():
        spread(ffn_oth, ffn_own)

    g_up[...] = tall[...].T


def final_ffn(place, ffn_own, ffn_oth):
    units = pl.BlockSpec((8, CLASSES, 3, 8, 128), lambda i: (0, 0, i % 3, 0, 0))
    return pl.pallas_call(
        final_ffn_kernel,
        grid=(COLS,),
        out_shape=(shape((768, 384), f32), shape((384, 768), f32)),
        in_specs=[SMEM, units, units],
        out_specs=(
            pl.BlockSpec((128, 384), lambda i: (i, 0)),
            pl.BlockSpec((384, 128), lambda i: (0, i)),
        ),
        scratch_shapes=[pltpu.VMEM((384, 128), f32)],
        compiler_params=params(16),
        name="final_ffn",
    )(place, ffn_own, ffn_oth)


def final_kernel(
    place, own, other, g_wv, g_bv, g_conv, g_wo, g_bo, g_ga, g_sa, g_bup, g_bd, g_gf, g_sf, vecs,
    bias, line,
):
    step = pl.program_id(0)

    def write(a, b):
        for j in range(3):
            cs = slice(j * 128, j * 128 + 128)
            at = j * TALL_TILES
            g_wv[:, cs] = a[at : at + 96].astype(f32).reshape(768, 128)
            vecs[step * 3 + j] = a[at + 96].astype(f32)
            bias[step * 3 + j] = a[at + 97].astype(f32)
            g_wo[:, cs] = b[at : at + 96].astype(f32).reshape(768, 128)
            g_conv[:, cs] = b[at + 96 : at + 105].astype(f32).reshape(72, 128)[0:TAPS]

    @pl.when(place[0] % 2 == 0)
    def _():
        write(own, other)

    @pl.when(place[0] % 2 == 1)
    def _():
        write(other, own)

    @pl.when(step == COLS // 3 - 1)
    def _():
        for j, ref in enumerate((g_bv, g_bo, g_ga, g_sa, g_bd, g_gf, g_sf)):
            for i in range(COLS):
                ref[i * 128 : i * 128 + 128] = vecs[i, j]
        n = lanes((128, 128))
        a = (n >= PIECE).astype(i32) + (n >= 2 * PIECE).astype(i32) + (n >= 3 * PIECE).astype(i32)
        at = (8 * a + place[1]) * PIECE + n - PIECE * a
        total = jnp.zeros((8, 128), f32)
        for i in range(COLS):
            pick = lax.broadcasted_iota(i32, (128, 128), 0) + 128 * i == at
            total = total + dot(bias[i].astype(bf16), jnp.where(pick, 1.0, 0.0).astype(bf16))
        for q in range(CLASSES):
            line[0:1, SUB * q : SUB * q + SUB] = total[q : q + 1, 0:SUB]
        g_bup[...] = line[...][0]


def final(place, own, other):
    tile = pl.BlockSpec((3 * TALL_TILES, 8, 128), lambda i: (i, 0, 0))
    tall = pl.BlockSpec((768, 384), lambda i: (0, i))
    vec = pl.BlockSpec((WIDTH,), lambda i: (0,))
    v = shape((WIDTH,), f32)
    return pl.pallas_call(
        final_kernel,
        grid=(COLS // 3,),
        out_shape=(
            shape((768, 768), f32), v, shape((TAPS, 768), f32), shape((768, 768), f32), v, v, v,
            shape((384,), f32), v, v, v,
        ),
        in_specs=[SMEM, tile, tile],
        out_specs=(
            tall, vec, pl.BlockSpec((TAPS, 384), lambda i: (0, i)), tall, vec, vec, vec,
            pl.BlockSpec((384,), lambda i: (0,)), vec, vec, vec,
        ),
        scratch_shapes=[
            pltpu.VMEM((COLS, 8, 128), f32),
            pltpu.VMEM((COLS, 8, 128), f32),
            pltpu.VMEM((1, 384), f32),
        ],
        compiler_params=params(16),
        name="final",
    )(place, own, other)


def body(
    block_input,
    w_value,
    b_value,
    conv_kernel,
    w_out,
    b_out,
    gain_attn,
    shift_attn,
    w_up,
    b_up,
    w_down,
    b_down,
    gain_ffn,
    shift_ffn,
    query_codes,
    key_codes,
    key_live,
    seq_lengths,
    out_grad,
):
    dp = lax.axis_index("dp")
    place = jnp.stack([dp, lax.axis_index("tensor")]).astype(i32)
    n_dp = lax.axis_size("dp")

    def shift(i, by):
        return i // 8 * 8 + (i // 2 + by) % 4 * 2 + i % 2

    def swap(x):
        return lax.ppermute(x, "dp", [(i, i ^ 1) for i in range(n_dp)])

    def away(x):
        pairs = [(i, shift(i, 1 - i % 2 * 2)) for i in range(n_dp)]
        return lax.ppermute(x, "dp", pairs)

    def home(x):
        pairs = [(shift(i, 1 - i % 2 * 2), i) for i in range(n_dp)]
        return lax.ppermute(x, "dp", pairs)

    def exchange(x):
        return lax.all_to_all(x, ALL, 0, 0, tiled=True)

    def row(v):
        return v.reshape(1, -1)

    weights = exchange(prep(place, w_up, w_down, b_up))
    weights = weights.reshape(2, PIECES, 2, 8, UNITS, 8, 128)
    (n1, inv1, low, ctx, collide, nrm, scl, wave, wavet, ks, vs, tapt, live) = attend(
        seq_lengths, block_input, w_value, row(b_value), conv_kernel, w_out, row(b_out),
        row(gain_attn), row(shift_attn), query_codes, key_codes, row(key_live),
    )
    low_sib = swap(low)
    got = away(low)
    wu, wd = unpack_weights(weights)
    act_f, slope_f, far_own, far_sib, rows_f = ffn(got, swap(got), wu, wd)
    sent = combine(far_own, swap(far_sib))
    wu, sent = lax.optimization_barrier((wu, sent))
    act_n, slope_n, near_own, near_sib, rows_n = ffn(low, low_sib, wu, wd)
    near_sib, far = lax.optimization_barrier((near_sib, home(sent)))
    second_args = (
        n1, near_own, swap(near_sib), far, row(b_down), row(gain_attn), row(shift_attn),
        row(gain_ffn), out_grad,
    )
    grad = middle(*second_args)
    got = away(grad)
    near_own, near_sib, g_n, u_n, bias_n = back_ffn("back_near", grad, swap(grad), wu, wd, slope_n)
    block_output, second, sums = outputs(*second_args, row(shift_ffn))
    got, near_sib, second = lax.optimization_barrier((got, near_sib, second))
    far_own, far_sib, g_f, u_f, bias_f = back_ffn("back_far", got, swap(got), wu, wd, slope_f)
    sent = combine(far_own, swap(far_sib))
    u_f, sent = lax.optimization_barrier((u_f, sent))
    grad_down = (dot_first(act_n, g_n) + dot_first(act_f, g_f)).astype(bf16)
    grad_up = (dot_first(u_n, rows_n) + dot_first(u_f, rows_f)).astype(bf16)
    grads, far = lax.optimization_barrier((pack(grad_up, grad_down), home(sent)))
    owned = exchange(grads.reshape(128, GRAD_UNITS, 8, 128))
    input_grad, keep, give = attend_back(
        place, near_own, swap(near_sib), far, second, n1, inv1,
        row(gain_attn), ctx, w_out, nrm, scl, wave, wavet, ks, vs, tapt, collide, live, block_input,
        w_value, sums, bias_n, bias_f,
    )
    pair = (keep.astype(f32) + swap(give).astype(f32)).astype(bf16)
    pair = pair.reshape(128, PACK // 128, 8, 128)
    owned = sum_ffn(owned)
    pair, owned = lax.optimization_barrier((pair, owned))
    both = jnp.stack([owned, swap(owned)])
    around = []
    for by in range(4):
        pairs = [(i, (i // 8 ^ i % 2) * 8 + shift(i % 8, by)) for i in range(n_dp)]
        around.append(lax.ppermute(both, "dp", pairs))
    summed = sum_rest(exchange(pair))
    summed, *around = lax.optimization_barrier((summed, *around))
    back = exchange(summed).reshape(PACK, 8, 128)
    ffn_own = jnp.stack(around).reshape(8, CLASSES, GRAD_UNITS, 8, 128)
    g_up, g_down = final_ffn(place, ffn_own, swap(ffn_own))
    back, g_up, g_down = lax.optimization_barrier((back, g_up, g_down))
    g_wv, g_bv, g_conv, g_wo, g_bo, g_ga, g_sa, g_bup, g_bd, g_gf, g_sf = final(
        place, back, swap(back)
    )
    return (
        block_output, input_grad, g_wv, g_bv, g_conv, g_wo, g_bo, g_ga, g_sa, g_up, g_bup, g_down,
        g_bd, g_gf, g_sf,
    )


def solution(mesh):
    rows = P(ALL, None)
    return jax.shard_map(
        body,
        mesh=mesh,
        in_specs=(
            rows, P(), P(), P(), P(), P(), P(), P(),
            P(None, "tensor"), P("tensor"), P("tensor", None), P(), P(), P(),
            rows, rows, P(ALL), rows, rows,
        ),
        out_specs=(
            rows, rows, P(), P(), P(), P(), P(), P(), P(),
            P(None, "tensor"), P("tensor"), P("tensor", None), P(), P(), P(),
        ),
        check_vma=False,
    )
```
